32 devices in a mesh: dp: 8 (over z, x), fsdp: 4 (over y, core).
Axes of the slice: x: 2, y: 2, z: 4, core: 2. Of those that a mesh axis runs over, the one named last changes fastest.
Arguments:
- hidden: bfloat16 [16, 1024, 896], P('dp', 'fsdp'), may hold values from -20 to 20
- neighbours: bfloat16 [16, 16, 256, 896], P('dp', 'fsdp'), may hold values from -5 to 5
- piece_starts: int32 [16, 2], P('dp'), may hold values from 0 to 768, as said below
- out_grad: bfloat16 [16, 1024, 896], P('dp', 'fsdp'), may hold values from -5 to 5
- attn_weights: bfloat16 [7168, 896], P(('dp', 'fsdp')), may hold values from -2 to 2
- ffw_weights: bfloat16 [7168, 896], P(('dp', 'fsdp')), may hold values from -0.1875 to 0.1875
- vectors: bfloat16 [7168], P(('dp', 'fsdp')), may hold values from -2 to 2
- rel_table: float32 [32, 14], replicated, may hold values from -4 to 4
Outputs:
- out: bfloat16 [16, 1024, 896], P('dp', 'fsdp')
- hidden_grad: float32 [16, 1024, 896], P('dp', 'fsdp')
- neighbour_grad: float32 [16, 16, 256, 896], P('dp', 'fsdp')
- attn_grad: float32 [7168, 896], P(('dp', 'fsdp'))
- ffw_grad: float32 [7168, 896], P(('dp', 'fsdp'))
- vectors_grad: float32 [7168], P(('dp', 'fsdp'))
- table_grad: float32 [32, 14], replicated
The draws below stay inside these ranges and needn't reach their ends.
Inputs may be any that keep to these rules, and one draw needn't show every extreme that they name: `piece_starts`: piece j of a sequence starts between j * 512 and (j + 1) * 512 - 256, so pieces do not intersect.
All inputs are finite; a program needn't handle non-finite values.
Results may differ from the reference program's by a relative error of at most 0.02.
Values may be sent and summed in bfloat16 or wider, within the bound.
A program may use at most 512 MiB of HBM per device.

```python
import jax
import jax.numpy as jnp
from jax import lax

D = 896
HEADS = 14
DH = 64
FF = 3584
SPAN = 64
PIECE = 256
PIECES = 2
BUCKETS = 32
LEN = 1024
SEQS = 16
SPANS = 16
KEYS = 256


def draw_hidden(key, part):
    base_key = jax.random.fold_in(key, 11)
    row_key = jax.random.fold_in(key, 12)
    core = jax.random.truncated_normal(base_key, -4.0, 4.0, (SEQS, LEN, D), jnp.float32)
    rising = 1.0 + 2.0 * jnp.arange(SEQS, dtype=jnp.float32) / (SEQS - 1)
    spread = jnp.exp(jax.random.uniform(row_key, (SEQS, LEN, 1), jnp.float32, -0.5, 0.5))
    return (core * rising[:, None, None] * spread).astype(jnp.bfloat16)


def draw_attn_weights(key, part):
    matrix_index = jnp.arange(8 * D, dtype=jnp.int32) // D
    factor = jnp.where(matrix_index % 4 == 3, 3.0, 1.0) * D ** (-0.5)
    core = jax.random.truncated_normal(key, -3.0, 3.0, (8 * D, D), jnp.float32)
    return (core * factor[:, None]).astype(jnp.bfloat16)


def draw_vectors(key, part):
    gain_key = jax.random.fold_in(key, 21)
    relative_bias_key = jax.random.fold_in(key, 22)
    index = jnp.arange(FF + 4 * D, dtype=jnp.int32)
    is_gain = (index >= FF) & (index < FF + 3 * D)
    gains = 1.0 + jax.random.uniform(gain_key, (FF + 4 * D,), jnp.float32, -0.4, 0.4)
    biases = 0.5 * jax.random.truncated_normal(relative_bias_key, -4.0, 4.0, (FF + 4 * D,), jnp.float32)
    return jnp.where(is_gain, gains, biases).astype(jnp.bfloat16)


def draw_piece_starts(key, part):
    region = LEN // PIECES
    offsets = jax.random.randint(key, (SEQS, PIECES), 0, region - PIECE + 1, dtype=jnp.int32)
    offsets = offsets.at[0, 0].set(0).at[1, PIECES - 1].set(region - PIECE)
    return offsets + jnp.arange(PIECES, dtype=jnp.int32)[None, :] * region


def steps_of(stream_key, dims, cuts, least, largest):
    loudness = 1.0
    for axis_at, shards_of in cuts:
        steps = jax.random.uniform(jax.random.fold_in(jax.random.fold_in(stream_key, 6), axis_at), (shards_of,), jnp.float32, least / len(cuts), largest / len(cuts))
        loudness = loudness * jnp.repeat(jnp.exp(steps), dims[axis_at] // shards_of).reshape((-1,) + (1,) * (len(dims) - 1 - axis_at))
    return loudness


def bell_draw(rng, shape, width, limit, shards=(), held_as=jnp.bfloat16):
    array = width * jax.random.normal(rng, shape, jnp.float32)
    if shards:
        array = array * steps_of(rng, shape, shards, -0.22, 0.18)
    return jnp.clip(array, -limit, limit).astype(held_as)


def setup_inputs(seed: int = 0) -> dict:
    arg_keys = jax.random.split(jax.random.key(seed), 9)
    return {
        "hidden": draw_hidden(jax.random.fold_in(arg_keys[8], 71), 0),
        "neighbours": bell_draw(arg_keys[1], (SEQS, SPANS, KEYS, D), 1.0, 5.0, ((0, 8), (1, 4))),
        "piece_starts": draw_piece_starts(jax.random.fold_in(arg_keys[8], 71), 0),
        "out_grad": bell_draw(arg_keys[3], (SEQS, LEN, D), 1.0, 5.0, ((0, 8), (1, 4))),
        "attn_weights": draw_attn_weights(jax.random.fold_in(arg_keys[8], 71), 0),
        "ffw_weights": bell_draw(arg_keys[5], (2 * FF, D), D ** -0.5, 0.1875, ((0, 32),)),
        "vectors": draw_vectors(jax.random.fold_in(arg_keys[8], 71), 0),
        "rel_table": bell_draw(arg_keys[7], (BUCKETS, HEADS), 1.0, 4.0, (), jnp.float32),
    }


@jax.custom_vjp
def low(v):
    return lax.optimization_barrier(v.astype(jnp.bfloat16)).astype(jnp.float32)

@jax.custom_vjp
def low_back(v):
    return v

def low_keep(v):
    return (low(v), None)

def low_pass(kept, grad):
    return (grad,)

def back_keep(v):
    return (v, None)

def back_low(kept, grad):
    return (low(grad),)
low.defvjp(low_keep, low_pass)
low_back.defvjp(back_keep, back_low)
relative_bucket_limits = (1, 2, 3, 4, 5, 6, 7, 8, 12, 16, 24, 32, 64, 128, 256)
norm_eps = 1e-06
gelu_scale = 0.7978845608028654
gelu_cubic = 0.044715
masked_score = -1e+30
highest = lax.Precision.HIGHEST

def rounded(values):
    return low(low_back(values))

def matmul(left_side, right_side):
    return jnp.dot(left_side, right_side, precision=highest, preferred_element_type=jnp.float32)

def rms_normed(residual, gain):
    return residual * lax.rsqrt(lax.optimization_barrier(jnp.mean(residual * residual, axis=-1, keepdims=True)) + norm_eps) * gain

def gelu_tanh(values):
    return 0.5 * values * (1.0 + jnp.tanh(gelu_scale * (values + gelu_cubic * values * values * values)))

def softmax_rows(scores):
    exp_scores = jnp.exp(scores - lax.optimization_barrier(jnp.max(scores, axis=-1, keepdims=True)))
    return exp_scores / lax.optimization_barrier(jnp.sum(exp_scores, axis=-1, keepdims=True))

def rel_buckets(query_pos, key_pos):
    offset = key_pos[None, :] - query_pos[:, None]
    magnitude = jnp.abs(offset)
    counted = jnp.zeros(offset.shape, jnp.int32)
    for threshold in relative_bucket_limits:
        counted = counted + (magnitude >= threshold).astype(jnp.int32)
    return counted + (offset > 0).astype(jnp.int32) * (len(relative_bucket_limits) + 1)

def piece_labels(positions, starts_row):
    inside = (positions[:, None] >= starts_row[None, :]) & (positions[:, None] < starts_row[None, :] + PIECE)
    labels = jnp.arange(1, starts_row.shape[0] + 1, dtype=jnp.int32)
    return lax.optimization_barrier(jnp.sum(jnp.where(inside, labels[None, :], 0), axis=1)).astype(jnp.int32)

def visible(query_pos, key_pos, query_piece, key_piece):
    causal = key_pos[None, :] <= query_pos[:, None]
    shared = (query_piece[:, None] == key_piece[None, :]) & (query_piece[:, None] > 0)
    return causal | shared

def decoder_layer(params, residual, near_tokens, starts_row):
    attn_all, ffw_all, vector_all, table = params
    matrices = attn_all.reshape(8, D, D)
    w_input = ffw_all[:FF]
    w_output = ffw_all[FF:]
    bias_input = vector_all[:FF]
    gain_rows = vector_all[FF:FF + 3 * D].reshape(3, D)
    bias_output = vector_all[FF + 3 * D:]
    positions = jnp.arange(LEN, dtype=jnp.int32)
    pieces = piece_labels(positions, starts_row)
    allowed = visible(positions, positions, pieces, pieces)
    rel_bias = jnp.transpose(table[rel_buckets(positions, positions)], (2, 0, 1))
    normed_one = low(rms_normed(residual, gain_rows[0]))
    queries = rounded(matmul(normed_one, matrices[0])).reshape(LEN, HEADS, DH)
    keys_all = rounded(matmul(normed_one, matrices[1])).reshape(LEN, HEADS, DH)
    values_all = rounded(matmul(normed_one, matrices[2])).reshape(LEN, HEADS, DH)
    raw_scores = jnp.einsum('qhd,khd->hqk', queries, keys_all, precision=highest)
    scores = jnp.where(allowed[None], low_back(raw_scores) * 0.125 + rel_bias, masked_score)
    self_weights = low(softmax_rows(scores))
    context = rounded(jnp.einsum('hqk,khd->qhd', self_weights, values_all, precision=highest).reshape(LEN, D))
    first_sum = residual + low_back(matmul(context, matrices[3]))
    normed_two = low(rms_normed(first_sum, gain_rows[1]))
    cross_queries = rounded(matmul(normed_two, matrices[4])).reshape(LEN, HEADS, DH)
    near_flat = near_tokens.reshape(SPANS * KEYS, D)
    cross_keys = rounded(matmul(near_flat, matrices[5])).reshape(SPANS, KEYS, HEADS, DH)
    cross_values = rounded(matmul(near_flat, matrices[6])).reshape(SPANS, KEYS, HEADS, DH)
    carried_rows = SPAN - 1
    block_queries = jnp.concatenate([cross_queries[carried_rows:], jnp.zeros((carried_rows, HEADS, DH), jnp.float32)], axis=0).reshape(SPANS, SPAN, HEADS, DH)
    cross_raw = jnp.einsum('cqhd,ckhd->chqk', block_queries, cross_keys, precision=highest)
    cross_weights = low(softmax_rows(low_back(cross_raw) * 0.125))
    cross_context = rounded(jnp.einsum('chqk,ckhd->cqhd', cross_weights, cross_values, precision=highest).reshape(LEN, D))
    placed = jnp.concatenate([jnp.zeros((carried_rows, D), jnp.float32), cross_context[:LEN - carried_rows]], axis=0)
    second_sum = first_sum + low_back(matmul(placed, matrices[7]))
    third_normalized = low(rms_normed(second_sum, gain_rows[2]))
    pre_act = low_back(matmul(third_normalized, jnp.transpose(w_input))) + bias_input
    activated = low(gelu_tanh(pre_act))
    return second_sum + low_back(matmul(activated, w_output)) + bias_output

def add_pair(left_sum, right_sum):
    return left_sum + right_sum

def reference(hidden, neighbours, piece_starts, out_grad, attn_weights, ffw_weights, vectors, rel_table):
    params = (attn_weights.astype(jnp.float32), ffw_weights.astype(jnp.float32), vectors.astype(jnp.float32), rel_table.astype(jnp.float32))
    zero_totals = jax.tree.map(jnp.zeros_like, params)

    def one_sequence(totals, batch_item):
        residual, near_tokens, starts_row, cotangent = batch_item

        def forward_fn(param_set, residual_in, near_in):
            return decoder_layer(param_set, residual_in, near_in, starts_row)
        result, pullback = jax.vjp(forward_fn, params, residual.astype(jnp.float32), near_tokens.astype(jnp.float32))
        param_grads, residual_grad, near_grad = pullback(cotangent.astype(jnp.float32))
        totals = jax.tree.map(add_pair, totals, param_grads)
        return (totals, (result.astype(jnp.bfloat16), residual_grad, near_grad))
    totals, stacked = lax.scan(one_sequence, zero_totals, (hidden, neighbours, piece_starts, out_grad))
    return (stacked[0], stacked[1], stacked[2], totals[0], totals[1], totals[2], totals[3])
```

```python
import jax
import jax.numpy as jnp
from jax import lax
from jax.experimental import pallas as pl
from jax.experimental.pallas import tpu as pltpu
from jax.sharding import PartitionSpec as P

FF = 3584
SPAN = 64
PIECE = 256

relative_bucket_limits = (1, 2, 3, 4, 5, 6, 7, 8, 12, 16, 24, 32, 64, 128, 256)
norm_eps = 1e-06
gelu_scale = 0.7978845608028654
gelu_cubic = 0.044715
masked_score = -1e30
F32 = jnp.float32
BF16 = jnp.bfloat16
AXES = ("dp", "fsdp")


def from_behind(array, axis, by):
    length = lax.axis_size(axis)
    pairs = [(i, i + by) for i in range(length) if 0 <= i + by < length]
    return lax.ppermute(array, axis, pairs)


def product(left_side, right_side):
    return jnp.dot(left_side, right_side, preferred_element_type=F32)


def times_transposed(left_side, right_side):
    return lax.dot_general(left_side, right_side, (((1,), (1,)), ((), ())), preferred_element_type=F32)


def transposed_times(left_side, right_side):
    return lax.dot_general(left_side, right_side, (((0,), (0,)), ((), ())), preferred_element_type=F32)


def inverse_rms(residual):
    return lax.rsqrt(jnp.mean(residual * residual, axis=-1, keepdims=True) + norm_eps)


def norm_back(residual, scale, gain, incoming):
    weighted = gain * incoming
    return scale * weighted - residual * scale * scale * scale * jnp.mean(
        residual * weighted, axis=-1, keepdims=True
    )


def gelu_parts(values):
    tangent = jnp.tanh(gelu_scale * (values + gelu_cubic * values * values * values))
    result = 0.5 * values * (1.0 + tangent)
    slope = 0.5 * (1.0 + tangent) + 0.5 * values * (1.0 - tangent * tangent) * gelu_scale * (
        1.0 + 3.0 * gelu_cubic * values * values
    )
    return (result, slope)


def bucket_of(offset):
    magnitude = jnp.abs(offset)
    counted = jnp.zeros(offset.shape, jnp.int32)
    for threshold in relative_bucket_limits:
        counted = counted + (magnitude >= threshold).astype(jnp.int32)
    return counted + (offset > 0).astype(jnp.int32) * (len(relative_bucket_limits) + 1)


def piece_labels(positions, starts):
    inside = (positions[None, :, None] >= starts[:, None, :]) & (
        positions[None, :, None] < starts[:, None, :] + PIECE
    )
    labels = jnp.arange(1, starts.shape[1] + 1, dtype=jnp.int32)
    return jnp.sum(jnp.where(inside, labels[None, None, :], 0), axis=2)


def dot_t(left_side, right_side):
    return lax.dot_general(left_side, right_side, (((1,), (1,)), ((), ())), preferred_element_type=F32)


def own_lanes(values, which, width):
    lane = lax.broadcasted_iota(jnp.int32, values.shape, 1)
    return jnp.where((lane >= which * width) & (lane < (which + 1) * width), values, jnp.zeros_like(values))


def flipped(values):
    return values.astype(F32).T.astype(BF16)


def bias_tiles(rel_table, rows, reach):
    heads = rel_table.shape[1]
    width = 2 * rows
    count = 2 * reach + 1
    shift = jnp.arange(width, dtype=jnp.int32)
    behind = jnp.where(shift < rows, shift, shift - width)
    far = (jnp.arange(count, dtype=jnp.int32) - reach) * rows
    ids = bucket_of(far[:, None] - behind[None, :])
    hot = (ids[:, :, None] == jnp.arange(rel_table.shape[0], dtype=jnp.int32)).astype(F32)
    lines = jnp.einsum("dwb,bh->hdw", hot, rel_table, precision=lax.Precision.HIGHEST)
    lines = lines.reshape(heads, count, 1, width)

    def spread(line_ref, tile_ref):
        for d in range(count):
            wide = jnp.broadcast_to(line_ref[0, d], (rows, width))
            tile_ref[0, d] = pltpu.roll(wide, 0, 1, stride=1, stride_axis=0)[:, :rows]

    return pl.pallas_call(
        spread,
        out_shape=jax.ShapeDtypeStruct((heads, count, rows, rows), F32),
        grid=(heads,),
        in_specs=[pl.BlockSpec((1, count, 1, width), lambda i: (i, 0, 0, 0))],
        out_specs=pl.BlockSpec((1, count, rows, rows), lambda i: (i, 0, 0, 0)),
        name="bias_tiles",
    )(lines)


def tile_at(block, place, reach):
    return jnp.clip(block - place, -reach, reach) + reach


def self_attention(place, query, keys, values, tiles, hidden_mask, head_size, reach):
    count, rows, width = query.shape
    blocks = keys.shape[0]
    pair = 128
    per = pair // head_size

    def body(place_ref, q_ref, k_ref, v_ref, tile_ref, mask_ref, o_ref, ot_ref, lse_ref, s_ref, p_ref):
        for b in range(count):
            scaled = q_ref[b] * jnp.asarray(0.125, BF16)
            value_t = jnp.concatenate([flipped(v_ref[j, b]) for j in range(blocks)], axis=1)
            for h in range(per):
                mine = own_lanes(scaled, h, head_size)
                top = jnp.full((1, rows), -jnp.inf, F32)
                for j in range(blocks):
                    s = dot_t(k_ref[j, b], mine)
                    s = s + tile_ref[h, tile_at(j, place_ref[0], reach)] + mask_ref[b, j]
                    s_ref[j] = s
                    top = jnp.maximum(top, jnp.max(s, axis=0, keepdims=True))
                total = jnp.zeros((1, rows), F32)
                for j in range(blocks):
                    p = jnp.exp(s_ref[j] - top)
                    total = total + jnp.sum(p, axis=0, keepdims=True)
                    p_ref[j * rows : (j + 1) * rows, :] = p.astype(BF16)
                part = product(value_t[h * head_size : (h + 1) * head_size], p_ref[...]) / total
                ot_ref[0, b, h * head_size : (h + 1) * head_size, :] = part
                lse_ref[0, b * per + h : b * per + h + 1, :] = top + jnp.log(total)
            o_ref[b] = ot_ref[0, b].T.astype(BF16)

    steps = width // pair
    grid_spec = pltpu.PrefetchScalarGridSpec(
        num_scalar_prefetch=1,
        grid=(steps,),
        in_specs=[
            pl.BlockSpec((count, rows, pair), lambda i, _: (0, 0, i)),
            pl.BlockSpec((blocks, count, rows, pair), lambda i, _: (0, 0, 0, i)),
            pl.BlockSpec((blocks, count, rows, pair), lambda i, _: (0, 0, 0, i)),
            pl.BlockSpec((per,) + tiles.shape[1:], lambda i, _: (i, 0, 0, 0)),
            pl.BlockSpec(hidden_mask.shape, lambda i, _: (0, 0, 0, 0)),
        ],
        out_specs=[
            pl.BlockSpec((count, rows, pair), lambda i, _: (0, 0, i)),
            pl.BlockSpec((1, count, pair, rows), lambda i, _: (i, 0, 0, 0)),
            pl.BlockSpec((1, count * per, rows), lambda i, _: (i, 0, 0)),
        ],
        scratch_shapes=[
            pltpu.VMEM((blocks, rows, rows), F32),
            pltpu.VMEM((blocks * rows, rows), BF16),
        ],
    )
    cost = 4 * count * blocks * rows * rows * width
    return pl.pallas_call(
        body,
        grid_spec=grid_spec,
        out_shape=[
            jax.ShapeDtypeStruct((count, rows, width), BF16),
            jax.ShapeDtypeStruct((steps, count, pair, rows), F32),
            jax.ShapeDtypeStruct((steps, count * per, rows), F32),
        ],
        cost_estimate=pl.CostEstimate(flops=4 * cost, transcendentals=0, bytes_accessed=30_000_000),
        name="self_attention",
    )(place, query, keys, values, tiles, hidden_mask)


def self_attention_back(place, query, keys, values, tiles, hidden_mask, outer_t, lse, grad, head_size, reach):
    count, rows, width = query.shape
    blocks = keys.shape[0]
    pair = 128
    per = pair // head_size
    half = rows // 2

    def body(
        place_ref, q_ref, k_ref, v_ref, tile_ref, mask_ref, ot_ref, lse_ref, do_ref,
        dq_ref, dk_ref, dv_ref, sum_ref, acc_ref, dk_acc, dv_acc,
    ):
        for b in range(count):
            scaled = q_ref[b] * jnp.asarray(0.125, BF16)
            incoming = do_ref[b]
            key_t = jnp.concatenate([flipped(k_ref[j, b]) for j in range(blocks)], axis=1)
            weighed = incoming.astype(F32).T * ot_ref[0, b]
            query_parts = []
            for h in range(per):
                lanes = slice(h * head_size, (h + 1) * head_size)
                mine = own_lanes(scaled, h, head_size)
                theirs = own_lanes(incoming, h, head_size)
                delta = jnp.sum(weighed[lanes], axis=0, keepdims=True)
                level = lse_ref[0, b * per + h : b * per + h + 1, :]
                part = jnp.zeros((head_size, rows), F32)
                for j in range(blocks):
                    s = dot_t(k_ref[j, b], mine)
                    s = s + tile_ref[h, tile_at(j, place_ref[0], reach)] + mask_ref[b, j]
                    p = jnp.exp(s - level)
                    ds = p * (dot_t(v_ref[j, b], theirs) - delta)
                    p_low = p.astype(BF16)
                    ds_low = ds.astype(BF16)
                    dv = product(p_low, theirs)
                    dk = product(ds_low, mine)
                    if h == 0:
                        dv_acc[j] = dv
                        dk_acc[j] = dk
                    else:
                        dv_ref[j, b] = (dv_acc[j] + dv).astype(BF16)
                        dk_ref[j, b] = (dk_acc[j] + dk).astype(BF16)
                    part = part + product(key_t[lanes, j * rows : (j + 1) * rows], ds_low)
                    if b == 0:
                        acc_ref[h, j] = ds
                    else:
                        acc_ref[h, j] = acc_ref[h, j] + ds
                query_parts.append(part)
            dq_ref[b] = (jnp.concatenate(query_parts, axis=0) * 0.125).T.astype(BF16)
        for h in range(per):
            for j in range(blocks):
                upper, lower = acc_ref[h, j, :half, :], acc_ref[h, j, half:, :]
                folded = jnp.concatenate(
                    [lower[:, :half], lower[:, half:] + upper[:, :half], upper[:, half:], jnp.zeros((half, half), F32)],
                    axis=1,
                )
                left = half // 2
                while left >= 8:
                    folded = folded[left:] + pltpu.roll(folded[:left], left, 1)
                    left //= 2
                sum_ref[h, j] = folded

    steps = width // pair
    grid_spec = pltpu.PrefetchScalarGridSpec(
        num_scalar_prefetch=1,
        grid=(steps,),
        in_specs=[
            pl.BlockSpec((count, rows, pair), lambda i, _: (0, 0, i)),
            pl.BlockSpec((blocks, count, rows, pair), lambda i, _: (0, 0, 0, i)),
            pl.BlockSpec((blocks, count, rows, pair), lambda i, _: (0, 0, 0, i)),
            pl.BlockSpec((per,) + tiles.shape[1:], lambda i, _: (i, 0, 0, 0)),
            pl.BlockSpec(hidden_mask.shape, lambda i, _: (0, 0, 0, 0)),
            pl.BlockSpec((1, count, pair, rows), lambda i, _: (i, 0, 0, 0)),
            pl.BlockSpec((1, count * per, rows), lambda i, _: (i, 0, 0)),
            pl.BlockSpec((count, rows, pair), lambda i, _: (0, 0, i)),
        ],
        out_specs=[
            pl.BlockSpec((count, rows, pair), lambda i, _: (0, 0, i)),
            pl.BlockSpec((blocks, count, rows, pair), lambda i, _: (0, 0, 0, i)),
            pl.BlockSpec((blocks, count, rows, pair), lambda i, _: (0, 0, 0, i)),
            pl.BlockSpec((per, blocks, 8, 2 * rows), lambda i, _: (i, 0, 0, 0)),
        ],
        scratch_shapes=[
            pltpu.VMEM((per, blocks, rows, rows), F32),
            pltpu.VMEM((blocks, rows, pair), F32),
            pltpu.VMEM((blocks, rows, pair), F32),
        ],
    )
    cost = 4 * count * blocks * rows * rows * width
    return pl.pallas_call(
        body,
        grid_spec=grid_spec,
        out_shape=[
            jax.ShapeDtypeStruct((count, rows, width), BF16),
            jax.ShapeDtypeStruct((blocks, count, rows, width), BF16),
            jax.ShapeDtypeStruct((blocks, count, rows, width), BF16),
            jax.ShapeDtypeStruct((width // head_size, blocks, 8, 2 * rows), F32),
        ],
        cost_estimate=pl.CostEstimate(flops=10 * cost, transcendentals=0, bytes_accessed=40_000_000),
        name="self_attention_back",
    )(place, query, keys, values, tiles, hidden_mask, outer_t, lse, grad)


def both_heads(values, head_size):
    return jnp.concatenate([own_lanes(values, h, head_size) for h in range(128 // head_size)], axis=0)


def picked(wide, rows, head_size):
    total = own_lanes(wide[:rows], 0, head_size)
    for h in range(1, 128 // head_size):
        total = total + own_lanes(wide[h * rows : (h + 1) * rows], h, head_size)
    return total


def softmax_down(scores):
    raised = jnp.exp(scores - jnp.max(scores, axis=0, keepdims=True))
    return raised / jnp.sum(raised, axis=0, keepdims=True)


def span_attention(query, keys, values, head_size):
    blocks, rows, width = query.shape
    span_keys = keys.shape[1]

    def body(q_ref, k_ref, v_ref, o_ref):
        for i in range(width // 128):
            lanes = slice(i * 128, (i + 1) * 128)
            stacked = both_heads(q_ref[0, :, lanes] * jnp.asarray(0.125, BF16), head_size)
            p = softmax_down(dot_t(k_ref[0, :, lanes], stacked)).astype(BF16)
            wide = product(flipped(v_ref[0, :, lanes]), p).T
            o_ref[0, :, lanes] = picked(wide, rows, head_size).astype(BF16)

    q_spec = pl.BlockSpec((1, rows, width), lambda i: (i, 0, 0))
    k_spec = pl.BlockSpec((1, span_keys, width), lambda i: (i, 0, 0))
    return pl.pallas_call(
        body,
        grid=(blocks,),
        in_specs=[q_spec, k_spec, k_spec],
        out_specs=q_spec,
        out_shape=jax.ShapeDtypeStruct(query.shape, BF16),
        cost_estimate=pl.CostEstimate(flops=16 * blocks * rows * span_keys * width, transcendentals=0, bytes_accessed=12_000_000),
        name="span_attention",
    )(query, keys, values)


def span_attention_back(query, keys, values, grad, head_size):
    blocks, rows, width = query.shape
    span_keys = keys.shape[1]

    def body(q_ref, k_ref, v_ref, do_ref, dq_ref, dk_ref, dv_ref):
        for i in range(width // 128):
            lanes = slice(i * 128, (i + 1) * 128)
            stacked = both_heads(q_ref[0, :, lanes] * jnp.asarray(0.125, BF16), head_size)
            theirs = both_heads(do_ref[0, :, lanes], head_size)
            k, v = k_ref[0, :, lanes], v_ref[0, :, lanes]
            p = softmax_down(dot_t(k, stacked))
            dp = dot_t(v, theirs)
            ds = p * (dp - jnp.sum(p * dp, axis=0, keepdims=True))
            ds_low = ds.astype(BF16)
            dv_ref[0, :, lanes] = product(p.astype(BF16), theirs).astype(BF16)
            dk_ref[0, :, lanes] = product(ds_low, stacked).astype(BF16)
            wide = (product(flipped(k), ds_low) * 0.125).T
            dq_ref[0, :, lanes] = picked(wide, rows, head_size).astype(BF16)

    q_spec = pl.BlockSpec((1, rows, width), lambda i: (i, 0, 0))
    k_spec = pl.BlockSpec((1, span_keys, width), lambda i: (i, 0, 0))
    return pl.pallas_call(
        body,
        grid=(blocks,),
        in_specs=[q_spec, k_spec, k_spec, q_spec],
        out_specs=[q_spec, k_spec, k_spec],
        out_shape=[
            jax.ShapeDtypeStruct(query.shape, BF16),
            jax.ShapeDtypeStruct(keys.shape, BF16),
            jax.ShapeDtypeStruct(keys.shape, BF16),
        ],
        cost_estimate=pl.CostEstimate(flops=40 * blocks * rows * span_keys * width, transcendentals=0, bytes_accessed=24_000_000),
        name="span_attention_back",
    )(query, keys, values, grad)


def per_device(hidden, neighbours, piece_starts, out_grad, attn_weights, ffw_weights, vectors, rel_table):
    count, rows, width = hidden.shape
    group = lax.axis_size("fsdp")
    length = rows * group
    heads = rel_table.shape[1]
    head_size = width // heads
    buckets = rel_table.shape[0]
    spans = neighbours.shape[1]
    span_keys = neighbours.shape[2]
    carried = SPAN - 1
    kept = rows - carried
    tokens = count * rows
    reach = -(-relative_bucket_limits[-1] // rows) + 1
    place = lax.axis_index("fsdp").astype(jnp.int32)
    share = attn_weights.shape[0]

    gather = lambda array, axes: lax.all_gather(array, axes, axis=0, tiled=True)
    vector_row = jnp.pad(vectors.reshape(1, -1), ((0, 15), (0, width - vectors.shape[0])))
    hidden_all = gather(hidden[None], "fsdp")
    first_full = gather(jnp.concatenate([attn_weights, vector_row], axis=0)[None], AXES)
    ffw_full = gather(ffw_weights, AXES)
    matrices = first_full[:, :share].reshape(8, width, width)
    vector_full = first_full[:, share, : vectors.shape[0]].reshape(-1).astype(F32)
    w_input, w_output = ffw_full[:FF], ffw_full[FF:]
    bias_input = vector_full[:FF]
    gains = vector_full[FF : FF + 3 * width].reshape(3, width)
    bias_output = vector_full[FF + 3 * width :]

    tiles = bias_tiles(rel_table, rows, reach)
    key_pos = jnp.arange(length, dtype=jnp.int32)
    query_pos = place * rows + jnp.arange(rows, dtype=jnp.int32)
    key_piece = piece_labels(key_pos, piece_starts)
    query_piece = piece_labels(query_pos, piece_starts)
    allowed = (key_pos[:, None] <= query_pos[None, :])[None] | (
        (key_piece[:, :, None] == query_piece[:, None, :]) & (query_piece[:, None, :] > 0)
    )
    mask = jnp.where(allowed, 0.0, masked_score).reshape(count, group, rows, rows)
    place_arg = place.reshape(1)

    residual = hidden.reshape(tokens, width).astype(F32)
    every = hidden_all.reshape(group * tokens, width).astype(F32)
    normed_every = (every * inverse_rms(every) * gains[0]).astype(BF16)
    scale_one = inverse_rms(residual)
    normed_one = (residual * scale_one * gains[0]).astype(BF16)
    queries = product(normed_one, matrices[0]).astype(BF16).reshape(count, rows, width)
    keys = product(normed_every, matrices[1]).astype(BF16).reshape(group, count, rows, width)
    values = product(normed_every, matrices[2]).astype(BF16).reshape(group, count, rows, width)
    near_flat = neighbours.reshape(count * spans * span_keys, width)
    cross_keys = product(near_flat, matrices[5]).astype(BF16).reshape(count * spans, span_keys, width)
    cross_values = product(near_flat, matrices[6]).astype(BF16).reshape(count * spans, span_keys, width)
    context, context_t, lse = self_attention(
        place_arg, queries, keys, values, tiles, mask, head_size, reach
    )
    context = context.reshape(tokens, width)
    first_sum = residual + product(context, matrices[3])
    scale_two = inverse_rms(first_sum)
    normed_two = (first_sum * scale_two * gains[1]).astype(BF16)
    cross_queries = product(normed_two, matrices[4]).astype(BF16).reshape(count, rows, width)

    def ahead(array):
        incoming = from_behind(array[:, :carried], "fsdp", -1)
        return jnp.concatenate([array[:, carried:], incoming], axis=1).reshape(count * spans, SPAN, width)

    def behind(array):
        array = array.reshape(count, rows, width)
        arriving = from_behind(array[:, kept:], "fsdp", 1)
        return jnp.concatenate([arriving, array[:, :kept]], axis=1).reshape(tokens, width)

    block_queries = ahead(cross_queries)
    placed = behind(span_attention(block_queries, cross_keys, cross_values, head_size))
    second_sum = first_sum + product(placed, matrices[7])
    scale_three = inverse_rms(second_sum)
    normed_three = (second_sum * scale_three * gains[2]).astype(BF16)
    pre_act = times_transposed(normed_three, w_input) + bias_input
    act_value, act_slope = gelu_parts(pre_act)
    activated = act_value.astype(BF16)
    output = (second_sum + product(activated, w_output) + bias_output).astype(BF16)

    grad_out_low = out_grad.reshape(tokens, width)
    grad_out = grad_out_low.astype(F32)
    grad_bias_output = jnp.sum(grad_out, axis=0)
    grad_w_output = transposed_times(activated, grad_out_low).astype(BF16)
    grad_pre = times_transposed(grad_out_low, w_output) * act_slope
    grad_bias_input = jnp.sum(grad_pre, axis=0)
    grad_pre_low = grad_pre.astype(BF16)
    grad_w_input = transposed_times(grad_pre_low, normed_three).astype(BF16)
    scatter = lambda array: lax.psum_scatter(array, AXES, scatter_dimension=0, tiled=True)
    ffw_sum = scatter(jnp.concatenate([grad_w_input, grad_w_output], axis=0))
    grad_norm_three = product(grad_pre_low, w_input)
    grad_gain_three = jnp.sum(grad_norm_three * second_sum * scale_three, axis=0)
    grad_second = grad_out + norm_back(second_sum, scale_three, gains[2], grad_norm_three)
    grad_second_low = grad_second.astype(BF16)
    grad_cross_out = transposed_times(placed, grad_second_low)
    grad_placed = times_transposed(grad_second_low, matrices[7]).astype(BF16).reshape(count, rows, width)
    grad_block_queries, grad_cross_keys, grad_cross_values = span_attention_back(
        block_queries, cross_keys, cross_values, ahead(grad_placed), head_size
    )
    grad_cross_keys = grad_cross_keys.reshape(count * spans * span_keys, width)
    grad_cross_values = grad_cross_values.reshape(count * spans * span_keys, width)
    grad_cross_queries = behind(grad_block_queries)
    grad_cross_query_mat = transposed_times(normed_two, grad_cross_queries)
    grad_norm_two = times_transposed(grad_cross_queries, matrices[4])
    grad_gain_two = jnp.sum(grad_norm_two * first_sum * scale_two, axis=0)
    grad_first = grad_second + norm_back(first_sum, scale_two, gains[1], grad_norm_two)
    grad_first_low = grad_first.astype(BF16)
    grad_self_out = transposed_times(context, grad_first_low)
    grad_context = times_transposed(grad_first_low, matrices[3]).astype(BF16).reshape(count, rows, width)
    grad_queries, grad_keys, grad_values, diagonal = self_attention_back(
        place_arg, queries, keys, values, tiles, mask, context_t, lse, grad_context, head_size, reach
    )
    grad_queries = grad_queries.reshape(tokens, width)
    grad_keys = grad_keys.reshape(group * tokens, width)
    grad_values = grad_values.reshape(group * tokens, width)
    partial_one = (
        times_transposed(grad_keys, matrices[1]) + times_transposed(grad_values, matrices[2])
    ).astype(BF16)
    joined = lax.psum_scatter(
        partial_one.reshape(group, tokens, width), "fsdp", scatter_dimension=0, tiled=True
    ).reshape(tokens, width)
    grad_cross_key_mat = transposed_times(near_flat, grad_cross_keys)
    grad_cross_value_mat = transposed_times(near_flat, grad_cross_values)
    near_grad = times_transposed(grad_cross_keys, matrices[5]) + times_transposed(
        grad_cross_values, matrices[6]
    )
    grad_query_mat = transposed_times(normed_one, grad_queries)
    grad_key_mat = transposed_times(normed_every, grad_keys)
    grad_value_mat = transposed_times(normed_every, grad_values)
    grad_norm_one = times_transposed(grad_queries, matrices[0]) + joined.astype(F32)
    grad_gain_one = jnp.sum(grad_norm_one * residual * scale_one, axis=0)
    hidden_grad = grad_first + norm_back(residual, scale_one, gains[0], grad_norm_one)

    lane = jnp.arange(2 * rows, dtype=jnp.int32)
    line = jnp.arange(8, dtype=jnp.int32)
    block = jnp.arange(group, dtype=jnp.int32)
    between = (block[:, None, None] - place) * rows - (lane[None, None, :] - (rows - 8) - line[None, :, None])
    hot = (bucket_of(between)[..., None] == jnp.arange(buckets, dtype=jnp.int32)).astype(F32)
    table_step = jnp.einsum("hjsl,jslb->bh", diagonal, hot, precision=lax.Precision.HIGHEST)

    attn_sum = scatter(
        jnp.concatenate(
            [
                part.astype(BF16)
                for part in (
                    grad_query_mat,
                    grad_key_mat,
                    grad_value_mat,
                    grad_self_out,
                    grad_cross_query_mat,
                    grad_cross_key_mat,
                    grad_cross_value_mat,
                    grad_cross_out,
                )
            ],
            axis=0,
        )
    )
    vector_step = jnp.concatenate(
        [grad_bias_input, grad_gain_one, grad_gain_two, grad_gain_three, grad_bias_output]
    )
    vector_sum = lax.psum_scatter(vector_step, AXES, scatter_dimension=0, tiled=True)
    table_sum = lax.psum(table_step, AXES)
    return (
        output.reshape(count, rows, width),
        hidden_grad.reshape(count, rows, width),
        near_grad.reshape(count, spans, span_keys, width),
        attn_sum.astype(F32),
        ffw_sum.astype(F32),
        vector_sum,
        table_sum,
    )


def solution(mesh):
    placed = (
        P("dp", "fsdp", None),
        P("dp", "fsdp", None, None),
        P("dp", None),
        P("dp", "fsdp", None),
        P(("dp", "fsdp"), None),
        P(("dp", "fsdp"), None),
        P(("dp", "fsdp")),
        P(),
    )
    return jax.shard_map(
        per_device,
        mesh=mesh,
        in_specs=placed,
        out_specs=(
            P("dp", "fsdp", None),
            P("dp", "fsdp", None),
            P("dp", "fsdp", None, None),
            P(("dp", "fsdp"), None),
            P(("dp", "fsdp"), None),
            P(("dp", "fsdp")),
            P(),
        ),
        check_vma=False,
    )
```

```python
import functools

import jax
import jax.numpy as jnp
from jax import lax
from jax.experimental import pallas as pl
from jax.experimental.pallas import tpu as pltpu
from jax.sharding import PartitionSpec as P

FF = 3584
SPAN = 64
PIECE = 256

relative_bucket_limits = (1, 2, 3, 4, 5, 6, 7, 8, 12, 16, 24, 32, 64, 128, 256)
norm_eps = 1e-06
gelu_scale = 0.7978845608028654
gelu_cubic = 0.044715
masked_score = -1e30
F32 = jnp.float32
BF16 = jnp.bfloat16
AXES = ("dp", "fsdp")
MESH = pl.DeviceIdType.MESH


def layout_of(sizes):
    dp, fsdp = sizes
    known = {
        (8, 4): (("fsdp", 1, 2), ("fsdp", 2, 2), ("dp", 1, 2), ("dp", 2, 4)),
        (64, 4): (("dp", 1, 2), ("fsdp", 1, 4), ("dp", 16, 4), ("dp", 2, 8)),
    }
    if sizes in known:
        return known[sizes]
    if fsdp % 2 == 0:
        return (("fsdp", 1, 2), ("fsdp", 2, fsdp // 2), ("dp", 1, 1), ("dp", 1, dp))
    return (("dp", 1, 2), ("fsdp", 1, fsdp), ("dp", 2, 1), ("dp", 2, dp // 2))


def pick(values, index):
    total = jnp.int32(values[0])
    for i in range(1, len(values)):
        total = jnp.where(index == i, jnp.int32(values[i]), total)
    return total


def by_distance(position, places, k):
    table = [sorted(range(places), key=lambda q, p=p: (abs(q - p), q))[k] for p in range(places)]
    return pick(table, position)


class Place:
    def __init__(self, layout):
        self.layout = layout
        self.core_dim, self.y_dim, self.x_dim, self.z_dim = layout
        self.swaps = self.x_dim[2] == self.y_dim[2]
        self.index = {axis: lax.axis_index(axis).astype(jnp.int32) for axis in AXES}
        where = [(self.index[axis] // step) % places for axis, step, places in layout]
        self.core, self.y, self.x, self.z = where
        self.a, self.b = self.roles(self.core, self.x, self.y)
        self.na, self.nb, self.nz = self.x_dim[2], self.y_dim[2], self.z_dim[2]
        self.cores = self.core_dim[2]

    def roles(self, core, first, second):
        if not self.swaps:
            return first, second
        return first + core * (second - first), second + core * (first - second)

    def coords(self, core, z, a, b):
        x, y = self.roles(core, a, b)
        total = {axis: jnp.int32(0) for axis in AXES}
        for (axis, step, _), at in zip(self.layout, (core, y, x, z), strict=True):
            total[axis] = total[axis] + at * step
        return total

    def device(self, core=None, z=None, a=None, b=None, roles_of=None):
        core_at = self.core if core is None else core
        if core is not None and roles_of is None:
            x, y = self.x, self.y
            total = {axis: jnp.int32(0) for axis in AXES}
            for (axis, step, _), at in zip(self.layout, (core_at, y, x, self.z), strict=True):
                total[axis] = total[axis] + at * step
            return total
        return self.coords(
            core_at, self.z if z is None else z, self.a if a is None else a, self.b if b is None else b
        )

    def block(self, core, z, a, b):
        at = self.coords(core, z, a, b)
        return at["dp"] * lax.axis_size("fsdp") + at["fsdp"]

    def neighbours(self):
        found = []
        for name, places in (("z", self.nz), ("a", self.na), ("b", self.nb)):
            at = getattr(self, name)
            for move in (-1, 1):
                if places == 1:
                    continue
                if places == 2:
                    if move == 1:
                        found.append((None, self.device(**{name: 1 - at})))
                    continue
                found.append(((at + move >= 0) & (at + move < places), self.device(**{name: at + move})))
        if self.cores == 2:
            found.append((None, self.device(core=1 - self.core)))
        return found


def when(condition, action):
    if condition is None:
        action()
    else:
        pl.when(condition)(action)


def meet(place):
    barrier = pltpu.get_barrier_semaphore()
    count = jnp.int32(0)
    for condition, device in place.neighbours():
        when(
            condition,
            lambda device=device: pl.semaphore_signal(barrier, inc=1, device_id=device, device_id_type=MESH),
        )
        count = count + (1 if condition is None else condition.astype(jnp.int32))
    pl.semaphore_wait(barrier, count)


def part_of(ref, block, size):
    if size is None:
        return ref.at[block]
    return ref.at[pl.ds(pl.multiple_of(block * size, size), size)]


def gather_steps(layout, arrays, side_work):
    place = Place(layout)
    meet(place)
    sent = []
    a, b, z, core = place.a, place.b, place.z, place.core
    sibling = place.device(core=1 - core)

    def send(block, kind, slot, device, condition, own):
        for x_ref, out_ref, size, send_sem, recv_sem, _ in arrays:
            copy = pltpu.make_async_remote_copy(
                src_ref=x_ref if own else part_of(out_ref, block, size),
                dst_ref=part_of(out_ref, block, size),
                send_sem=send_sem.at[kind, slot],
                recv_sem=recv_sem.at[block],
                device_id=device,
                device_id_type=MESH,
            )
            when(condition, copy.start)
            sent.append((condition, copy))

    def arrived(block):
        for x_ref, out_ref, size, send_sem, recv_sem, _ in arrays:
            pltpu.make_async_remote_copy(
                src_ref=x_ref, dst_ref=part_of(out_ref, block, size), send_sem=send_sem.at[0, 0], recv_sem=recv_sem.at[block],
                device_id=sibling, device_id_type=MESH,
            ).wait_recv()

    def along(name, at, places, block, slot, origin, kinds, own=False):
        if places == 1:
            return
        if places == 2:
            if origin is None:
                send(block, kinds[0], slot, place.device(**{name: 1 - at}), None, own)
            return
        if origin is None:
            for move, kind in ((-1, kinds[0]), (1, kinds[1])):
                inside = (at + move >= 0) & (at + move < places)
                send(block, kind, slot, place.device(**{name: at + move}), inside, own)
            return
        move = jnp.where(origin < at, 1, -1)
        inside = (at + move >= 0) & (at + move < places)
        send(block, kinds[0], slot, place.device(**{name: at + move}), inside, own)

    mine = place.block(core, z, a, b)
    keeps = []
    slot = 0
    along("z", z, place.nz, mine, slot, None, (0, 1), True)
    along("a", a, place.na, mine, slot, None, (2, 3), True)
    along("b", b, place.nb, mine, slot, None, (4, 5), True)
    if place.cores == 2:
        send(mine, 6, slot, sibling, None, True)
    for x_ref, out_ref, size, _, _, own_sem in arrays:
        keep = pltpu.make_async_copy(x_ref, part_of(out_ref, mine, size), own_sem)
        keep.start()
        keeps.append(keep)
    visits = []
    for kz in range(place.nz):
        visits.append((kz, 0, 0))
        if kz:
            visits += [(kz - 1, ka, 0) for ka in range(1, place.na)]
    visits += [(place.nz - 1, ka, 0) for ka in range(1, place.na)]
    visits += [(kz, ka, kb) for kb in range(1, place.nb) for ka in range(place.na) for kz in range(place.nz)]
    side_work = list(side_work)
    for kz, ka, kb in visits[1:]:
        if side_work:
            side_work.pop(0)()
        slot += 1
        zb, ab, bb = by_distance(z, place.nz, kz), by_distance(a, place.na, ka), by_distance(b, place.nb, kb)
        block = place.block(core, zb, ab, bb)
        arrived(block)
        if kb == 0 and ka == 0:
            along("z", z, place.nz, block, slot, zb, (0, 1))
        if kb == 0:
            along("a", a, place.na, block, slot, None if ka == 0 else ab, (2, 3))
        along("b", b, place.nb, block, slot, None if kb == 0 else bb, (4, 5))
        if place.cores == 2:
            send(block, 6, slot, sibling, None, False)
    for action in side_work:
        action()
    if place.cores == 2:
        for bb in range(place.nb):
            for ab in range(place.na):
                for zb in range(place.nz):
                    arrived(place.block(1 - core, jnp.int32(zb), jnp.int32(ab), jnp.int32(bb)))
    for condition, copy in sent:
        when(condition, copy.wait_send)
    for keep in keeps:
        keep.wait()


def gather_with_tiles(layout, blocks, lines, rows):
    n = 1
    for _, _, places in layout:
        n *= places
    per_core = n // layout[0][2]
    count = len(blocks)
    heads, reach_count, _, width = lines.shape
    sizes = [block.shape[0] if block.shape[0] % 16 == 0 else None for block in blocks]

    def body(*refs):
        xs, line_ref, outs, tile_ref = refs[:count], refs[count], refs[count + 1 : 2 * count + 1], refs[2 * count + 1]
        tile_buf, tile_sem = refs[2 * count + 2 : 2 * count + 4]
        sems = refs[2 * count + 4 :]
        arrays = [(xs[i], outs[i], sizes[i], *sems[3 * i : 3 * i + 3]) for i in range(count)]

        def tile_copy(h):
            return pltpu.make_async_copy(tile_buf.at[h], tile_ref.at[h], tile_sem.at[h])

        def spread(h):
            for d in range(reach_count):
                wide = jnp.broadcast_to(line_ref[h, d], (rows, width))
                tile_buf[h, d] = pltpu.roll(wide, 0, 1, stride=1, stride_axis=0)[:, :rows]
            tile_copy(h).start()

        gather_steps(layout, arrays, [functools.partial(spread, h) for h in range(heads)])
        for h in range(heads):
            tile_copy(h).wait()

    scratch = [pltpu.VMEM((heads, reach_count, rows, rows), F32), pltpu.SemaphoreType.DMA((heads,))]
    for _ in blocks:
        scratch += [pltpu.SemaphoreType.DMA((7, per_core)), pltpu.SemaphoreType.DMA((n,)), pltpu.SemaphoreType.DMA]
    anywhere = pl.BlockSpec(memory_space=pl.ANY)
    inside = pl.BlockSpec(memory_space=pltpu.VMEM)
    *gathered, tiles = pl.pallas_call(
        body,
        out_shape=[
            jax.ShapeDtypeStruct((n,) + block.shape if size is None else (n * size,) + block.shape[1:], block.dtype)
            for block, size in zip(blocks, sizes, strict=True)
        ]
        + [jax.ShapeDtypeStruct((heads, reach_count, rows, rows), F32)],
        in_specs=[inside] * (count + 1),
        out_specs=[anywhere] * (count + 1),
        scratch_shapes=scratch,
        compiler_params=pltpu.CompilerParams(collective_id=1, has_side_effects=True, vmem_limit_bytes=40_000_000),
        name="gather_all",
    )(*blocks, lines)
    return gathered, tiles


class Payload:
    def __init__(self, source, own, sib, line_b, line_a, line_z, load_sem, send_sem, sems):
        self.source, self.own, self.sib = source, own, sib
        self.lines = {"b": line_b, "a": line_a, "z": line_z}
        self.load_sem, self.send_sem, self.sems = load_sem, send_sem, sems


def buffers_of(layout, block_shape, dtype):
    _, (_, _, nb), (_, _, na), (_, _, nz) = layout
    per_core = nz * na * nb
    deep = lambda places: 1 if places <= 2 else places + 1
    vm = lambda *lead: pltpu.VMEM(lead + block_shape, dtype)
    dma = pltpu.SemaphoreType.DMA
    counts = {"s": per_core, "b": deep(nb) * nz * na, "a": deep(na) * nz, "z": deep(nz)}
    return [
        vm(per_core), vm(per_core), vm(counts["b"]), vm(counts["a"]), vm(counts["z"]),
        dma((per_core,)), dma((2, per_core)),
        dma((per_core,)), dma((counts["b"],)), dma((counts["a"],)), dma((counts["z"],)),
    ]


def scatter_steps(layout, payloads, finish):
    place = Place(layout)
    a, b, z, core = place.a, place.b, place.z, place.core
    na, nb, nz = place.na, place.nb, place.nz
    slot_of = lambda zb, ab, bb: (zb * na + ab) * nb + bb
    meet(place)
    sent = []

    def remote(src, dst, send_sem, recv_sem, device):
        return pltpu.make_async_remote_copy(
            src_ref=src, dst_ref=dst, send_sem=send_sem, recv_sem=recv_sem, device_id=device, device_id_type=MESH
        )

    def order(a_at, b_at):
        found = []
        for kz in reversed(range(nz)):
            for kb in reversed(range(nb)):
                for ka in reversed(range(na)):
                    found.append((by_distance(z, nz, kz), by_distance(a_at, na, ka), by_distance(b_at, nb, kb)))
        return found

    sibling = place.device(core=1 - core)
    own_order = order(a, b)
    their_a, their_b = (b, a) if place.swaps else (a, b)
    for (zo, ao, bo), (zt, at, bt) in zip(own_order, order(their_a, their_b), strict=True):
        for p in payloads:
            slot = slot_of(zo, ao, bo)
            pltpu.make_async_copy(p.source.at[place.block(core, zo, ao, bo)], p.own.at[slot], p.load_sem.at[slot]).start()
            slot = slot_of(zt, at, bt)
            copy = remote(
                p.source.at[place.block(1 - core, zt, at, bt)], p.sib.at[slot], p.send_sem.at[0, slot], p.sems["s"].at[slot], sibling
            )
            copy.start()
            sent.append((None, copy))

    waiting = []

    def release():
        while waiting:
            condition, copy = waiting.pop(0)
            when(condition, copy.start)
            sent.append((condition, copy))

    def add_arrival(p, slot, buffer, sem, at):
        remote(p.own.at[slot], buffer.at[at], p.send_sem.at[1, slot], sem.at[at], sibling).wait_recv()
        p.own[slot] = (p.own[slot].astype(F32) + buffer[at].astype(F32)).astype(p.own.dtype)

    def start_sum(zb, ab, bb):
        for p in payloads:
            slot = slot_of(zb, ab, bb)
            pltpu.make_async_copy(p.source.at[place.block(core, zb, ab, bb)], p.own.at[slot], p.load_sem.at[slot]).wait()
            add_arrival(p, slot, p.sib, p.sems["s"], slot)

    def pass_on(name, at, places, target, inner, inner_count, zb, ab, bb):
        move = jnp.where(target > at, 1, -1)
        for p in payloads:
            slot = slot_of(zb, ab, bb)
            line, sem = p.lines[name], p.sems[name]
            if places == 2:
                there = inner
            else:
                outer = (at - move >= 0) & (at - move < places)
                here = target * inner_count + inner
                pl.when(outer)(lambda p=p, slot=slot, line=line, sem=sem, here=here: add_arrival(p, slot, line, sem, here))
                last = (target == at + move) & (move < 0)
                there = jnp.where(last, places, target) * inner_count + inner
            waiting.append(
                (None, remote(p.own.at[slot], line.at[there], p.send_sem.at[1, slot], sem.at[there], place.device(**{name: at + move})))
            )
        release()

    def take_in(name, at, places, inner, inner_count, zb, ab, bb):
        for p in payloads:
            slot = slot_of(zb, ab, bb)
            line, sem = p.lines[name], p.sems[name]
            if places == 1:
                continue
            if places == 2:
                add_arrival(p, slot, line, sem, inner)
                continue
            pl.when(at > 0)(lambda p=p, slot=slot, line=line, sem=sem: add_arrival(p, slot, line, sem, at * inner_count + inner))
            pl.when(at < places - 1)(
                lambda p=p, slot=slot, line=line, sem=sem: add_arrival(p, slot, line, sem, places * inner_count + inner)
            )

    def first_stage(zb):
        for kb in reversed(range(1, nb)):
            bb = by_distance(b, nb, kb)
            for ka in reversed(range(na)):
                ab = by_distance(a, na, ka)
                start_sum(zb, ab, bb)
                release()
                pass_on("b", b, nb, bb, zb * na + ab, nz * na, zb, ab, bb)
        for ka in reversed(range(na)):
            start_sum(zb, by_distance(a, na, ka), b)
            release()

    def second_stage(zb):
        for ka in reversed(range(1, na)):
            ab = by_distance(a, na, ka)
            take_in("b", b, nb, zb * na + ab, nz * na, zb, ab, b)
            release()
            pass_on("a", a, na, ab, zb, nz, zb, ab, b)
        take_in("b", b, nb, zb * na + a, nz * na, zb, a, b)
        release()

    def third_stage(zb, onward):
        take_in("a", a, na, zb, nz, zb, a, b)
        release()
        if onward:
            pass_on("z", z, nz, zb, 0, 1, zb, a, b)

    far_first = [by_distance(z, nz, kz) for kz in reversed(range(nz))]
    for i in range(nz + 2):
        if i < nz:
            first_stage(far_first[i])
        if 0 <= i - 1 < nz:
            second_stage(far_first[i - 1])
        if 0 <= i - 2 < nz:
            third_stage(far_first[i - 2], i - 2 < nz - 1)
    release()
    take_in("z", z, nz, 0, 1, z, a, b)
    mine = slot_of(z, a, b)
    for p, done in zip(payloads, finish, strict=True):
        done(p.own[mine])
    for condition, copy in sent:
        when(condition, copy.wait_send)


def scatter_all(layout, blocks, collective_id):
    count = len(blocks)

    def body(*refs):
        sources, outs, rest = refs[:count], refs[count : 2 * count], refs[2 * count :]
        payloads, finish = [], []
        for i in range(count):
            own, sib, line_b, line_a, line_z, load, send, s, sb, sa, sz = rest[11 * i : 11 * (i + 1)]
            payloads.append(
                Payload(sources[i], own, sib, line_b, line_a, line_z, load, send, {"s": s, "b": sb, "a": sa, "z": sz})
            )

            def done(value, i=i):
                outs[i][...] = value.astype(F32)

            finish.append(done)
        scatter_steps(layout, payloads, finish)

    scratch = []
    for block in blocks:
        scratch += buffers_of(layout, block.shape[1:], block.dtype)
    return pl.pallas_call(
        body,
        out_shape=[jax.ShapeDtypeStruct(block.shape[1:], F32) for block in blocks],
        in_specs=[pl.BlockSpec(memory_space=pl.ANY)] * count,
        out_specs=[pl.BlockSpec(memory_space=pltpu.VMEM)] * count,
        scratch_shapes=scratch,
        compiler_params=pltpu.CompilerParams(
            collective_id=collective_id, has_side_effects=True, vmem_limit_bytes=60_000_000
        ),
        name="scatter_all",
    )(*blocks)


def from_behind(array, axis, by):
    length = lax.axis_size(axis)
    pairs = [(i, i + by) for i in range(length) if 0 <= i + by < length]
    return lax.ppermute(array, axis, pairs)


def sum_of_group(parts, place):
    group = parts.shape[0]
    if group & (group - 1):
        return lax.psum_scatter(parts, "fsdp", scatter_dimension=0, tiled=True)[0].astype(F32)
    step = 1
    while step < group:
        halves = parts.reshape((parts.shape[0] // 2, 2) + parts.shape[1:])
        bit = (place // step) % 2
        away = lax.dynamic_index_in_dim(halves, 1 - bit, axis=1, keepdims=False)
        kept = lax.dynamic_index_in_dim(halves, bit, axis=1, keepdims=False)
        came = lax.ppermute(away, "fsdp", [(i, i ^ step) for i in range(group)])
        parts = kept.astype(F32) + came.astype(F32)
        step *= 2
        if step < group:
            parts = parts.astype(BF16)
    return parts[0]


def product(left_side, right_side):
    return jnp.dot(left_side, right_side, preferred_element_type=F32)


def times_transposed(left_side, right_side):
    return lax.dot_general(left_side, right_side, (((1,), (1,)), ((), ())), preferred_element_type=F32)


def transposed_times(left_side, right_side):
    return lax.dot_general(left_side, right_side, (((0,), (0,)), ((), ())), preferred_element_type=F32)


def inverse_rms(residual):
    return lax.rsqrt(jnp.mean(residual * residual, axis=-1, keepdims=True) + norm_eps)


def norm_back(residual, scale, gain, incoming):
    weighted = gain * incoming
    return scale * weighted - residual * scale * scale * scale * jnp.mean(
        residual * weighted, axis=-1, keepdims=True
    )


def gelu_parts(values):
    tangent = jnp.tanh(gelu_scale * (values + gelu_cubic * values * values * values))
    result = 0.5 * values * (1.0 + tangent)
    slope = 0.5 * (1.0 + tangent) + 0.5 * values * (1.0 - tangent * tangent) * gelu_scale * (
        1.0 + 3.0 * gelu_cubic * values * values
    )
    return (result, slope)


def bucket_of(offset):
    magnitude = jnp.abs(offset)
    counted = jnp.zeros(offset.shape, jnp.int32)
    for threshold in relative_bucket_limits:
        counted = counted + (magnitude >= threshold).astype(jnp.int32)
    return counted + (offset > 0).astype(jnp.int32) * (len(relative_bucket_limits) + 1)


def piece_labels(positions, starts):
    inside = (positions[None, :, None] >= starts[:, None, :]) & (
        positions[None, :, None] < starts[:, None, :] + PIECE
    )
    labels = jnp.arange(1, starts.shape[1] + 1, dtype=jnp.int32)
    return jnp.sum(jnp.where(inside, labels[None, None, :], 0), axis=2)


def dot_t(left_side, right_side):
    return lax.dot_general(left_side, right_side, (((1,), (1,)), ((), ())), preferred_element_type=F32)


def own_lanes(values, which, width):
    lane = lax.broadcasted_iota(jnp.int32, values.shape, 1)
    return jnp.where((lane >= which * width) & (lane < (which + 1) * width), values, jnp.zeros_like(values))


def flipped(values):
    return values.astype(F32).T.astype(BF16)


def bias_lines(rel_table, rows, reach):
    heads = rel_table.shape[1]
    width = 2 * rows
    count = 2 * reach + 1
    shift = jnp.arange(width, dtype=jnp.int32)
    behind = jnp.where(shift < rows, shift, shift - width)
    far = (jnp.arange(count, dtype=jnp.int32) - reach) * rows
    ids = bucket_of(far[:, None] - behind[None, :])
    hot = (ids[:, :, None] == jnp.arange(rel_table.shape[0], dtype=jnp.int32)).astype(F32)
    lines = jnp.einsum("dwb,bh->hdw", hot, rel_table, precision=lax.Precision.HIGHEST)
    return lines.reshape(heads, count, 1, width)


def tile_at(block, place, reach):
    return jnp.clip(block - place, -reach, reach) + reach


def self_attention(place, query, keys, values, tiles, hidden_mask, head_size, reach):
    count, rows, width = query.shape
    blocks = keys.shape[0]
    pair = 128
    per = pair // head_size

    def body(place_ref, q_ref, k_ref, v_ref, tile_ref, mask_ref, o_ref, ot_ref, lse_ref, s_ref, p_ref):
        for b in range(count):
            scaled = q_ref[b] * jnp.asarray(0.125, BF16)
            value_t = jnp.concatenate([flipped(v_ref[j, b]) for j in range(blocks)], axis=1)
            for h in range(per):
                mine = own_lanes(scaled, h, head_size)
                top = jnp.full((1, rows), -jnp.inf, F32)
                for j in range(blocks):
                    s = dot_t(k_ref[j, b], mine)
                    s = s + tile_ref[h, tile_at(j, place_ref[0], reach)] + mask_ref[b, j]
                    s_ref[j] = s
                    top = jnp.maximum(top, jnp.max(s, axis=0, keepdims=True))
                total = jnp.zeros((1, rows), F32)
                for j in range(blocks):
                    p = jnp.exp(s_ref[j] - top)
                    total = total + jnp.sum(p, axis=0, keepdims=True)
                    p_ref[j * rows : (j + 1) * rows, :] = p.astype(BF16)
                part = product(value_t[h * head_size : (h + 1) * head_size], p_ref[...]) / total
                ot_ref[0, b, h * head_size : (h + 1) * head_size, :] = part
                lse_ref[0, b * per + h : b * per + h + 1, :] = top + jnp.log(total)
            o_ref[b] = ot_ref[0, b].T.astype(BF16)

    steps = width // pair
    grid_spec = pltpu.PrefetchScalarGridSpec(
        num_scalar_prefetch=1,
        grid=(steps,),
        in_specs=[
            pl.BlockSpec((count, rows, pair), lambda i, _: (0, 0, i)),
            pl.BlockSpec((blocks, count, rows, pair), lambda i, _: (0, 0, 0, i)),
            pl.BlockSpec((blocks, count, rows, pair), lambda i, _: (0, 0, 0, i)),
            pl.BlockSpec((per,) + tiles.shape[1:], lambda i, _: (i, 0, 0, 0)),
            pl.BlockSpec(hidden_mask.shape, lambda i, _: (0, 0, 0, 0)),
        ],
        out_specs=[
            pl.BlockSpec((count, rows, pair), lambda i, _: (0, 0, i)),
            pl.BlockSpec((1, count, pair, rows), lambda i, _: (i, 0, 0, 0)),
            pl.BlockSpec((1, count * per, rows), lambda i, _: (i, 0, 0)),
        ],
        scratch_shapes=[
            pltpu.VMEM((blocks, rows, rows), F32),
            pltpu.VMEM((blocks * rows, rows), BF16),
        ],
    )
    cost = 4 * count * blocks * rows * rows * width
    return pl.pallas_call(
        body,
        grid_spec=grid_spec,
        out_shape=[
            jax.ShapeDtypeStruct((count, rows, width), BF16),
            jax.ShapeDtypeStruct((steps, count, pair, rows), F32),
            jax.ShapeDtypeStruct((steps, count * per, rows), F32),
        ],
        cost_estimate=pl.CostEstimate(flops=4 * cost, transcendentals=0, bytes_accessed=30_000_000),
        name="self_attention",
    )(place, query, keys, values, tiles, hidden_mask)


def self_attention_back(place, query, keys, values, tiles, hidden_mask, outer_t, lse, grad, head_size, reach):
    count, rows, width = query.shape
    blocks = keys.shape[0]
    pair = 128
    per = pair // head_size
    half = rows // 2

    def body(
        place_ref, q_ref, k_ref, v_ref, tile_ref, mask_ref, ot_ref, lse_ref, do_ref,
        dq_ref, dk_ref, dv_ref, sum_ref, acc_ref, dk_acc, dv_acc,
    ):
        for b in range(count):
            scaled = q_ref[b] * jnp.asarray(0.125, BF16)
            incoming = do_ref[b]
            key_t = jnp.concatenate([flipped(k_ref[j, b]) for j in range(blocks)], axis=1)
            weighed = incoming.astype(F32).T * ot_ref[0, b]
            query_parts = []
            for h in range(per):
                lanes = slice(h * head_size, (h + 1) * head_size)
                mine = own_lanes(scaled, h, head_size)
                theirs = own_lanes(incoming, h, head_size)
                delta = jnp.sum(weighed[lanes], axis=0, keepdims=True)
                level = lse_ref[0, b * per + h : b * per + h + 1, :]
                part = jnp.zeros((head_size, rows), F32)
                for j in range(blocks):
                    s = dot_t(k_ref[j, b], mine)
                    s = s + tile_ref[h, tile_at(j, place_ref[0], reach)] + mask_ref[b, j]
                    p = jnp.exp(s - level)
                    ds = p * (dot_t(v_ref[j, b], theirs) - delta)
                    p_low = p.astype(BF16)
                    ds_low = ds.astype(BF16)
                    dv = product(p_low, theirs)
                    dk = product(ds_low, mine)
                    if h == 0:
                        dv_acc[j] = dv
                        dk_acc[j] = dk
                    else:
                        dv_ref[j, b] = (dv_acc[j] + dv).astype(BF16)
                        dk_ref[j, b] = (dk_acc[j] + dk).astype(BF16)
                    part = part + product(key_t[lanes, j * rows : (j + 1) * rows], ds_low)
                    if b == 0:
                        acc_ref[h, j] = ds
                    else:
                        acc_ref[h, j] = acc_ref[h, j] + ds
                query_parts.append(part)
            dq_ref[b] = (jnp.concatenate(query_parts, axis=0) * 0.125).T.astype(BF16)
        for h in range(per):
            for j in range(blocks):
                upper, lower = acc_ref[h, j, :half, :], acc_ref[h, j, half:, :]
                folded = jnp.concatenate(
                    [lower[:, :half], lower[:, half:] + upper[:, :half], upper[:, half:], jnp.zeros((half, half), F32)],
                    axis=1,
                )
                left = half // 2
                while left >= 8:
                    folded = folded[left:] + pltpu.roll(folded[:left], left, 1)
                    left //= 2
                sum_ref[h, j] = folded

    steps = width // pair
    grid_spec = pltpu.PrefetchScalarGridSpec(
        num_scalar_prefetch=1,
        grid=(steps,),
        in_specs=[
            pl.BlockSpec((count, rows, pair), lambda i, _: (0, 0, i)),
            pl.BlockSpec((blocks, count, rows, pair), lambda i, _: (0, 0, 0, i)),
            pl.BlockSpec((blocks, count, rows, pair), lambda i, _: (0, 0, 0, i)),
            pl.BlockSpec((per,) + tiles.shape[1:], lambda i, _: (i, 0, 0, 0)),
            pl.BlockSpec(hidden_mask.shape, lambda i, _: (0, 0, 0, 0)),
            pl.BlockSpec((1, count, pair, rows), lambda i, _: (i, 0, 0, 0)),
            pl.BlockSpec((1, count * per, rows), lambda i, _: (i, 0, 0)),
            pl.BlockSpec((count, rows, pair), lambda i, _: (0, 0, i)),
        ],
        out_specs=[
            pl.BlockSpec((count, rows, pair), lambda i, _: (0, 0, i)),
            pl.BlockSpec((blocks, count, rows, pair), lambda i, _: (0, 0, 0, i)),
            pl.BlockSpec((blocks, count, rows, pair), lambda i, _: (0, 0, 0, i)),
            pl.BlockSpec((per, blocks, 8, 2 * rows), lambda i, _: (i, 0, 0, 0)),
        ],
        scratch_shapes=[
            pltpu.VMEM((per, blocks, rows, rows), F32),
            pltpu.VMEM((blocks, rows, pair), F32),
            pltpu.VMEM((blocks, rows, pair), F32),
        ],
    )
    cost = 4 * count * blocks * rows * rows * width
    return pl.pallas_call(
        body,
        grid_spec=grid_spec,
        out_shape=[
            jax.ShapeDtypeStruct((count, rows, width), BF16),
            jax.ShapeDtypeStruct((blocks, count, rows, width), BF16),
            jax.ShapeDtypeStruct((blocks, count, rows, width), BF16),
            jax.ShapeDtypeStruct((width // head_size, blocks, 8, 2 * rows), F32),
        ],
        cost_estimate=pl.CostEstimate(flops=10 * cost, transcendentals=0, bytes_accessed=40_000_000),
        name="self_attention_back",
    )(place, query, keys, values, tiles, hidden_mask, outer_t, lse, grad)


def both_heads(values, head_size):
    return jnp.concatenate([own_lanes(values, h, head_size) for h in range(128 // head_size)], axis=0)


def picked(wide, rows, head_size):
    total = own_lanes(wide[:rows], 0, head_size)
    for h in range(1, 128 // head_size):
        total = total + own_lanes(wide[h * rows : (h + 1) * rows], h, head_size)
    return total


def softmax_down(scores):
    raised = jnp.exp(scores - jnp.max(scores, axis=0, keepdims=True))
    return raised / jnp.sum(raised, axis=0, keepdims=True)


def span_attention(query, keys, values, head_size):
    blocks, rows, width = query.shape
    span_keys = keys.shape[1]

    def body(q_ref, k_ref, v_ref, o_ref):
        for i in range(width // 128):
            lanes = slice(i * 128, (i + 1) * 128)
            stacked = both_heads(q_ref[0, :, lanes] * jnp.asarray(0.125, BF16), head_size)
            p = softmax_down(dot_t(k_ref[0, :, lanes], stacked)).astype(BF16)
            wide = product(flipped(v_ref[0, :, lanes]), p).T
            o_ref[0, :, lanes] = picked(wide, rows, head_size).astype(BF16)

    q_spec = pl.BlockSpec((1, rows, width), lambda i: (i, 0, 0))
    k_spec = pl.BlockSpec((1, span_keys, width), lambda i: (i, 0, 0))
    return pl.pallas_call(
        body,
        grid=(blocks,),
        in_specs=[q_spec, k_spec, k_spec],
        out_specs=q_spec,
        out_shape=jax.ShapeDtypeStruct(query.shape, BF16),
        cost_estimate=pl.CostEstimate(flops=16 * blocks * rows * span_keys * width, transcendentals=0, bytes_accessed=12_000_000),
        name="span_attention",
    )(query, keys, values)


def span_attention_back(query, keys, values, grad, head_size):
    blocks, rows, width = query.shape
    span_keys = keys.shape[1]

    def body(q_ref, k_ref, v_ref, do_ref, dq_ref, dk_ref, dv_ref):
        for i in range(width // 128):
            lanes = slice(i * 128, (i + 1) * 128)
            stacked = both_heads(q_ref[0, :, lanes] * jnp.asarray(0.125, BF16), head_size)
            theirs = both_heads(do_ref[0, :, lanes], head_size)
            k, v = k_ref[0, :, lanes], v_ref[0, :, lanes]
            p = softmax_down(dot_t(k, stacked))
            dp = dot_t(v, theirs)
            ds = p * (dp - jnp.sum(p * dp, axis=0, keepdims=True))
            ds_low = ds.astype(BF16)
            dv_ref[0, :, lanes] = product(p.astype(BF16), theirs).astype(BF16)
            dk_ref[0, :, lanes] = product(ds_low, stacked).astype(BF16)
            wide = (product(flipped(k), ds_low) * 0.125).T
            dq_ref[0, :, lanes] = picked(wide, rows, head_size).astype(BF16)

    q_spec = pl.BlockSpec((1, rows, width), lambda i: (i, 0, 0))
    k_spec = pl.BlockSpec((1, span_keys, width), lambda i: (i, 0, 0))
    return pl.pallas_call(
        body,
        grid=(blocks,),
        in_specs=[q_spec, k_spec, k_spec, q_spec],
        out_specs=[q_spec, k_spec, k_spec],
        out_shape=[
            jax.ShapeDtypeStruct(query.shape, BF16),
            jax.ShapeDtypeStruct(keys.shape, BF16),
            jax.ShapeDtypeStruct(keys.shape, BF16),
        ],
        cost_estimate=pl.CostEstimate(flops=40 * blocks * rows * span_keys * width, transcendentals=0, bytes_accessed=24_000_000),
        name="span_attention_back",
    )(query, keys, values, grad)


def per_device(hidden, neighbours, piece_starts, out_grad, attn_weights, ffw_weights, vectors, rel_table):
    count, rows, width = hidden.shape
    group = lax.axis_size("fsdp")
    length = rows * group
    heads = rel_table.shape[1]
    head_size = width // heads
    buckets = rel_table.shape[0]
    spans = neighbours.shape[1]
    span_keys = neighbours.shape[2]
    carried = SPAN - 1
    kept = rows - carried
    tokens = count * rows
    reach = -(-relative_bucket_limits[-1] // rows) + 1
    place = lax.axis_index("fsdp").astype(jnp.int32)
    share = attn_weights.shape[0]

    gather = lambda array, axes: lax.all_gather(array, axes, axis=0, tiled=True)
    layout = layout_of((lax.axis_size("dp"), group))
    vector_rows = -(-vectors.shape[0] // 2048) * 16
    vector_block = jnp.pad(vectors, (0, vector_rows * 128 - vectors.shape[0])).reshape(vector_rows, 128)
    hidden_all = gather(hidden[None], "fsdp")
    (attn_full, vector_full), tiles = gather_with_tiles(
        layout, [attn_weights, vector_block], bias_lines(rel_table, rows, reach), rows
    )
    ffw_full = gather(lax.optimization_barrier((ffw_weights, vector_full))[0], AXES)
    matrices = attn_full.reshape(8, width, width)
    vector_full = vector_full.reshape(-1, vector_rows * 128)[:, : vectors.shape[0]].reshape(-1).astype(F32)
    w_input, w_output = ffw_full[:FF], ffw_full[FF:]
    bias_input = vector_full[:FF]
    gains = vector_full[FF : FF + 3 * width].reshape(3, width)
    bias_output = vector_full[FF + 3 * width :]

    key_pos = jnp.arange(length, dtype=jnp.int32)
    query_pos = place * rows + jnp.arange(rows, dtype=jnp.int32)
    key_piece = piece_labels(key_pos, piece_starts)
    query_piece = piece_labels(query_pos, piece_starts)
    allowed = (key_pos[:, None] <= query_pos[None, :])[None] | (
        (key_piece[:, :, None] == query_piece[:, None, :]) & (query_piece[:, None, :] > 0)
    )
    mask = jnp.where(allowed, 0.0, masked_score).reshape(count, group, rows, rows)
    place_arg = place.reshape(1)

    residual = hidden.reshape(tokens, width).astype(F32)
    every = hidden_all.reshape(group * tokens, width).astype(F32)
    normed_every = (every * inverse_rms(every) * gains[0]).astype(BF16)
    scale_one = inverse_rms(residual)
    normed_one = (residual * scale_one * gains[0]).astype(BF16)
    queries = product(normed_one, matrices[0]).astype(BF16).reshape(count, rows, width)
    keys = product(normed_every, matrices[1]).astype(BF16).reshape(group, count, rows, width)
    values = product(normed_every, matrices[2]).astype(BF16).reshape(group, count, rows, width)
    near_flat = neighbours.reshape(count * spans * span_keys, width)
    cross_keys = product(near_flat, matrices[5]).astype(BF16).reshape(count * spans, span_keys, width)
    cross_values = product(near_flat, matrices[6]).astype(BF16).reshape(count * spans, span_keys, width)
    context, context_t, lse = self_attention(
        place_arg, queries, keys, values, tiles, mask, head_size, reach
    )
    context = context.reshape(tokens, width)
    first_sum = residual + product(context, matrices[3])
    scale_two = inverse_rms(first_sum)
    normed_two = (first_sum * scale_two * gains[1]).astype(BF16)
    cross_queries = product(normed_two, matrices[4]).astype(BF16).reshape(count, rows, width)

    def ahead(array):
        incoming = from_behind(array[:, :carried], "fsdp", -1)
        return jnp.concatenate([array[:, carried:], incoming], axis=1).reshape(count * spans, SPAN, width)

    def behind(array):
        array = array.reshape(count, rows, width)
        arriving = from_behind(array[:, kept:], "fsdp", 1)
        return jnp.concatenate([arriving, array[:, :kept]], axis=1).reshape(tokens, width)

    block_queries = ahead(cross_queries)
    placed = behind(span_attention(block_queries, cross_keys, cross_values, head_size))
    second_sum = first_sum + product(placed, matrices[7])
    scale_three = inverse_rms(second_sum)
    normed_three = (second_sum * scale_three * gains[2]).astype(BF16)
    pre_act = times_transposed(normed_three, w_input) + bias_input
    act_value, act_slope = gelu_parts(pre_act)
    activated = act_value.astype(BF16)
    output = (second_sum + product(activated, w_output) + bias_output).astype(BF16)

    grad_out_low = out_grad.reshape(tokens, width)
    grad_out = grad_out_low.astype(F32)
    grad_bias_output = jnp.sum(grad_out, axis=0)
    grad_w_output = transposed_times(activated, grad_out_low).astype(BF16)
    grad_pre = times_transposed(grad_out_low, w_output) * act_slope
    grad_bias_input = jnp.sum(grad_pre, axis=0)
    grad_pre_low = grad_pre.astype(BF16)
    grad_w_input = transposed_times(grad_pre_low, normed_three).astype(BF16)
    scatter = lambda array: lax.psum_scatter(array, AXES, scatter_dimension=0, tiled=True)
    ffw_step = jnp.stack([grad_w_input, grad_w_output]).reshape(2 * FF, width)
    ffw_step, grad_pre_low = lax.optimization_barrier((ffw_step, grad_pre_low))
    ffw_sum = scatter(ffw_step)
    grad_norm_three = product(grad_pre_low, w_input)
    grad_gain_three = jnp.sum(grad_norm_three * second_sum * scale_three, axis=0)
    grad_second = grad_out + norm_back(second_sum, scale_three, gains[2], grad_norm_three)
    grad_second_low = grad_second.astype(BF16)
    grad_cross_out = transposed_times(placed, grad_second_low)
    grad_placed = times_transposed(grad_second_low, matrices[7]).astype(BF16).reshape(count, rows, width)
    grad_block_queries, grad_cross_keys, grad_cross_values = span_attention_back(
        block_queries, cross_keys, cross_values, ahead(grad_placed), head_size
    )
    grad_cross_keys = grad_cross_keys.reshape(count * spans * span_keys, width)
    grad_cross_values = grad_cross_values.reshape(count * spans * span_keys, width)
    grad_cross_queries = behind(grad_block_queries)
    grad_cross_query_mat = transposed_times(normed_two, grad_cross_queries)
    grad_norm_two = times_transposed(grad_cross_queries, matrices[4])
    grad_gain_two = jnp.sum(grad_norm_two * first_sum * scale_two, axis=0)
    grad_first = grad_second + norm_back(first_sum, scale_two, gains[1], grad_norm_two)
    grad_first_low = grad_first.astype(BF16)
    grad_self_out = transposed_times(context, grad_first_low)
    grad_context = times_transposed(grad_first_low, matrices[3]).astype(BF16).reshape(count, rows, width)
    grad_queries, grad_keys, grad_values, diagonal = self_attention_back(
        place_arg, queries, keys, values, tiles, mask, context_t, lse, grad_context, head_size, reach
    )
    grad_queries = grad_queries.reshape(tokens, width)
    grad_keys = grad_keys.reshape(group * tokens, width)
    grad_values = grad_values.reshape(group * tokens, width)
    partial_one = (
        times_transposed(grad_keys, matrices[1]) + times_transposed(grad_values, matrices[2])
    ).astype(BF16)
    joined = sum_of_group(partial_one.reshape(group, tokens, width), place)
    grad_cross_key_mat = transposed_times(near_flat, grad_cross_keys)
    grad_cross_value_mat = transposed_times(near_flat, grad_cross_values)
    near_grad = times_transposed(grad_cross_keys, matrices[5]) + times_transposed(
        grad_cross_values, matrices[6]
    )
    grad_query_mat = transposed_times(normed_one, grad_queries)
    grad_key_mat = transposed_times(normed_every, grad_keys)
    grad_value_mat = transposed_times(normed_every, grad_values)
    grad_norm_one = times_transposed(grad_queries, matrices[0]) + joined.astype(F32)
    grad_gain_one = jnp.sum(grad_norm_one * residual * scale_one, axis=0)
    hidden_grad = grad_first + norm_back(residual, scale_one, gains[0], grad_norm_one)

    lane = jnp.arange(2 * rows, dtype=jnp.int32)
    line = jnp.arange(8, dtype=jnp.int32)
    block = jnp.arange(group, dtype=jnp.int32)
    between = (block[:, None, None] - place) * rows - (lane[None, None, :] - (rows - 8) - line[None, :, None])
    hot = (bucket_of(between)[..., None] == jnp.arange(buckets, dtype=jnp.int32)).astype(F32)
    table_step = jnp.einsum("hjsl,jslb->bh", diagonal, hot, precision=lax.Precision.HIGHEST)

    attn_step = jnp.stack(
        [
            part.astype(BF16)
            for part in (
                grad_query_mat,
                grad_key_mat,
                grad_value_mat,
                grad_self_out,
                grad_cross_query_mat,
                grad_cross_key_mat,
                grad_cross_value_mat,
                grad_cross_out,
            )
        ]
    )
    vector_step = jnp.concatenate(
        [grad_bias_input, grad_gain_one, grad_gain_two, grad_gain_three, grad_bias_output]
    ).reshape(-1, vectors.shape[0])
    devices = vector_step.shape[0]
    small = jnp.concatenate(
        [vector_step, jnp.broadcast_to(table_step.reshape(1, -1), (devices, buckets * heads))], axis=1
    )
    small_rows = -(-small.shape[1] // 1024) * 8
    small = jnp.pad(small, ((0, 0), (0, small_rows * 128 - small.shape[1]))).reshape(devices, small_rows, 128)
    attn_sum, small_sum = scatter_all(layout, [attn_step.reshape(devices, share, width), small], 2)
    small_sum = small_sum.reshape(-1)
    vector_sum = small_sum[: vectors.shape[0]]
    table_sum = small_sum[vectors.shape[0] : vectors.shape[0] + buckets * heads].reshape(buckets, heads)
    return (
        output.reshape(count, rows, width),
        hidden_grad.reshape(count, rows, width),
        near_grad.reshape(count, spans, span_keys, width),
        attn_sum,
        ffw_sum.astype(F32),
        vector_sum,
        table_sum,
    )


def solution(mesh):
    placed = (
        P("dp", "fsdp", None),
        P("dp", "fsdp", None, None),
        P("dp", None),
        P("dp", "fsdp", None),
        P(("dp", "fsdp"), None),
        P(("dp", "fsdp"), None),
        P(("dp", "fsdp")),
        P(),
    )
    return jax.shard_map(
        per_device,
        mesh=mesh,
        in_specs=placed,
        out_specs=(
            P("dp", "fsdp", None),
            P("dp", "fsdp", None),
            P("dp", "fsdp", None, None),
            P(("dp", "fsdp"), None),
            P(("dp", "fsdp"), None),
            P(("dp", "fsdp")),
            P(),
        ),
        check_vma=False,
    )
```

```python
import functools

import jax
import jax.numpy as jnp
from jax import lax
from jax.experimental import pallas as pl
from jax.experimental.pallas import tpu as pltpu
from jax.sharding import PartitionSpec as P

FF = 3584
SPAN = 64
PIECE = 256

relative_bucket_limits = (1, 2, 3, 4, 5, 6, 7, 8, 12, 16, 24, 32, 64, 128, 256)
norm_eps = 1e-06
gelu_scale = 0.7978845608028654
gelu_cubic = 0.044715
masked_score = -1e30
F32 = jnp.float32
BF16 = jnp.bfloat16
AXES = ("dp", "fsdp")
MESH = pl.DeviceIdType.MESH


def layout_of(sizes):
    dp, fsdp = sizes
    known = {
        (8, 4): (("fsdp", 1, 2), ("fsdp", 2, 2), ("dp", 1, 2), ("dp", 2, 4)),
        (64, 4): (("dp", 1, 2), ("fsdp", 1, 4), ("dp", 2, 8), ("dp", 16, 4)),
    }
    if sizes in known:
        return known[sizes]
    if fsdp % 2 == 0:
        return (("fsdp", 1, 2), ("fsdp", 2, fsdp // 2), ("dp", 1, 1), ("dp", 1, dp))
    return (("dp", 1, 2), ("fsdp", 1, fsdp), ("dp", 2, 1), ("dp", 2, dp // 2))


def pick(values, index):
    total = jnp.int32(values[0])
    for i in range(1, len(values)):
        total = jnp.where(index == i, jnp.int32(values[i]), total)
    return total


def by_distance(position, places, k):
    table = [sorted(range(places), key=lambda q, p=p: (abs(q - p), q))[k] for p in range(places)]
    return pick(table, position)


class Place:
    def __init__(self, layout):
        self.layout = layout
        self.core_dim, self.y_dim, self.x_dim, self.z_dim = layout
        self.swaps = self.x_dim[2] == self.y_dim[2]
        self.index = {axis: lax.axis_index(axis).astype(jnp.int32) for axis in AXES}
        where = [(self.index[axis] // step) % places for axis, step, places in layout]
        self.core, self.y, self.x, self.z = where
        self.a, self.b = self.roles(self.core, self.x, self.y)
        self.na, self.nb, self.nz = self.x_dim[2], self.y_dim[2], self.z_dim[2]
        self.cores = self.core_dim[2]

    def roles(self, core, first, second):
        if not self.swaps:
            return first, second
        return first + core * (second - first), second + core * (first - second)

    def coords(self, core, z, a, b):
        x, y = self.roles(core, a, b)
        total = {axis: jnp.int32(0) for axis in AXES}
        for (axis, step, _), at in zip(self.layout, (core, y, x, z), strict=True):
            total[axis] = total[axis] + at * step
        return total

    def device(self, core=None, z=None, a=None, b=None, roles_of=None):
        core_at = self.core if core is None else core
        if core is not None and roles_of is None:
            x, y = self.x, self.y
            total = {axis: jnp.int32(0) for axis in AXES}
            for (axis, step, _), at in zip(self.layout, (core_at, y, x, self.z), strict=True):
                total[axis] = total[axis] + at * step
            return total
        return self.coords(
            core_at, self.z if z is None else z, self.a if a is None else a, self.b if b is None else b
        )

    def block(self, core, z, a, b):
        at = self.coords(core, z, a, b)
        return at["dp"] * lax.axis_size("fsdp") + at["fsdp"]

    def neighbours(self):
        found = []
        for name, places in (("z", self.nz), ("a", self.na), ("b", self.nb)):
            at = getattr(self, name)
            for move in (-1, 1):
                if places == 1:
                    continue
                if places == 2:
                    if move == 1:
                        found.append((None, self.device(**{name: 1 - at})))
                    continue
                found.append(((at + move >= 0) & (at + move < places), self.device(**{name: at + move})))
        if self.cores == 2:
            found.append((None, self.device(core=1 - self.core)))
        return found


def when(condition, action):
    if condition is None:
        action()
    else:
        pl.when(condition)(action)


def meet(place, others=()):
    barrier = pltpu.get_barrier_semaphore()
    count = jnp.int32(0)
    for condition, device in place.neighbours() + [(None, other) for other in others]:
        when(
            condition,
            lambda device=device: pl.semaphore_signal(barrier, inc=1, device_id=device, device_id_type=MESH),
        )
        count = count + (1 if condition is None else condition.astype(jnp.int32))
    pl.semaphore_wait(barrier, count)


def part_of(ref, block, size):
    if size is None:
        return ref.at[block]
    return ref.at[pl.ds(pl.multiple_of(block * size, size), size)]


def gather_steps(layout, arrays, side_work):
    place = Place(layout)
    meet(place)
    sent = []
    a, b, z, core = place.a, place.b, place.z, place.core
    sibling = place.device(core=1 - core)

    def send(block, kind, slot, device, condition, own):
        for x_ref, out_ref, size, send_sem, recv_sem, _ in arrays:
            copy = pltpu.make_async_remote_copy(
                src_ref=x_ref if own else part_of(out_ref, block, size),
                dst_ref=part_of(out_ref, block, size),
                send_sem=send_sem.at[kind, slot],
                recv_sem=recv_sem.at[block],
                device_id=device,
                device_id_type=MESH,
            )
            when(condition, copy.start)
            sent.append((condition, copy))

    def arrived(block):
        for x_ref, out_ref, size, send_sem, recv_sem, _ in arrays:
            pltpu.make_async_remote_copy(
                src_ref=x_ref, dst_ref=part_of(out_ref, block, size), send_sem=send_sem.at[0, 0], recv_sem=recv_sem.at[block],
                device_id=sibling, device_id_type=MESH,
            ).wait_recv()

    def along(name, at, places, block, slot, origin, kinds, own=False):
        if places == 1:
            return
        if places == 2:
            if origin is None:
                send(block, kinds[0], slot, place.device(**{name: 1 - at}), None, own)
            return
        if origin is None:
            for move, kind in ((-1, kinds[0]), (1, kinds[1])):
                inside = (at + move >= 0) & (at + move < places)
                send(block, kind, slot, place.device(**{name: at + move}), inside, own)
            return
        move = jnp.where(origin < at, 1, -1)
        inside = (at + move >= 0) & (at + move < places)
        send(block, kinds[0], slot, place.device(**{name: at + move}), inside, own)

    mine = place.block(core, z, a, b)
    keeps = []
    slot = 0
    along("z", z, place.nz, mine, slot, None, (0, 1), True)
    along("a", a, place.na, mine, slot, None, (2, 3), True)
    along("b", b, place.nb, mine, slot, None, (4, 5), True)
    if place.cores == 2:
        send(mine, 6, slot, sibling, None, True)
    for x_ref, out_ref, size, _, _, own_sem in arrays:
        keep = pltpu.make_async_copy(x_ref, part_of(out_ref, mine, size), own_sem)
        keep.start()
        keeps.append(keep)
    visits = []
    for kz in range(place.nz):
        visits.append((kz, 0, 0))
        if kz:
            visits += [(kz - 1, ka, 0) for ka in range(1, place.na)]
    visits += [(place.nz - 1, ka, 0) for ka in range(1, place.na)]
    visits += [(kz, ka, kb) for kb in range(1, place.nb) for ka in range(place.na) for kz in range(place.nz)]
    side_work = list(side_work)
    for kz, ka, kb in visits[1:]:
        if side_work:
            side_work.pop(0)()
        slot += 1
        zb, ab, bb = by_distance(z, place.nz, kz), by_distance(a, place.na, ka), by_distance(b, place.nb, kb)
        block = place.block(core, zb, ab, bb)
        arrived(block)
        if kb == 0 and ka == 0:
            along("z", z, place.nz, block, slot, zb, (0, 1))
        if kb == 0:
            along("a", a, place.na, block, slot, None if ka == 0 else ab, (2, 3))
        along("b", b, place.nb, block, slot, None if kb == 0 else bb, (4, 5))
        if place.cores == 2:
            send(block, 6, slot, sibling, None, False)
    for action in side_work:
        action()
    if place.cores == 2:
        for bb in range(place.nb):
            for ab in range(place.na):
                for zb in range(place.nz):
                    arrived(place.block(1 - core, jnp.int32(zb), jnp.int32(ab), jnp.int32(bb)))
    for condition, copy in sent:
        when(condition, copy.wait_send)
    for keep in keeps:
        keep.wait()


def gather_with_tiles(layout, blocks, lines, rows):
    n = 1
    for _, _, places in layout:
        n *= places
    per_core = n // layout[0][2]
    count = len(blocks)
    heads, reach_count, _, width = lines.shape
    sizes = [block.shape[0] if block.shape[0] % 16 == 0 else None for block in blocks]

    def body(*refs):
        xs, line_ref, outs, tile_ref = refs[:count], refs[count], refs[count + 1 : 2 * count + 1], refs[2 * count + 1]
        tile_buf, tile_sem = refs[2 * count + 2 : 2 * count + 4]
        sems = refs[2 * count + 4 :]
        arrays = [(xs[i], outs[i], sizes[i], *sems[3 * i : 3 * i + 3]) for i in range(count)]

        def tile_copy(h):
            return pltpu.make_async_copy(tile_buf.at[h], tile_ref.at[h], tile_sem.at[h])

        def spread(h):
            for d in range(reach_count):
                wide = jnp.broadcast_to(line_ref[h, d], (rows, width))
                tile_buf[h, d] = pltpu.roll(wide, 0, 1, stride=1, stride_axis=0)[:, :rows]
            tile_copy(h).start()

        gather_steps(layout, arrays, [functools.partial(spread, h) for h in range(heads)])
        for h in range(heads):
            tile_copy(h).wait()

    scratch = [pltpu.VMEM((heads, reach_count, rows, rows), F32), pltpu.SemaphoreType.DMA((heads,))]
    for _ in blocks:
        scratch += [pltpu.SemaphoreType.DMA((7, per_core)), pltpu.SemaphoreType.DMA((n,)), pltpu.SemaphoreType.DMA]
    anywhere = pl.BlockSpec(memory_space=pl.ANY)
    inside = pl.BlockSpec(memory_space=pltpu.VMEM)
    *gathered, tiles = pl.pallas_call(
        body,
        out_shape=[
            jax.ShapeDtypeStruct((n,) + block.shape if size is None else (n * size,) + block.shape[1:], block.dtype)
            for block, size in zip(blocks, sizes, strict=True)
        ]
        + [jax.ShapeDtypeStruct((heads, reach_count, rows, rows), F32)],
        in_specs=[inside] * (count + 1),
        out_specs=[anywhere] * (count + 1),
        scratch_shapes=scratch,
        compiler_params=pltpu.CompilerParams(collective_id=1, has_side_effects=True, vmem_limit_bytes=40_000_000),
        name="gather_all",
    )(*blocks, lines)
    return gathered, tiles


class Reduction:
    def __init__(self, place, source, size, lanes, buffers):
        self.place, self.source, self.size, self.lanes = place, source, size, lanes
        self.own, self.sib, line_b, line_a, line_z, self.load_sem, self.send_sem, self.sib_sem, sem_b, sem_a, sem_z = buffers
        self.lines = {"b": (line_b, sem_b), "a": (line_a, sem_a), "z": (line_z, sem_z)}
        self.order = [by_distance(place.z, place.nz, k) for k in reversed(range(place.nz))]
        self.sibling = place.device(core=1 - place.core)

    def slot(self, zb, ab, bb):
        return (zb * self.place.na + ab) * self.place.nb + bb

    def piece(self, core, zb, ab, bb):
        block = self.place.block(core, zb, ab, bb)
        if self.size is None:
            return self.source.at[block, :, pl.ds(*self.lanes)]
        return self.source.at[pl.ds(pl.multiple_of(block * self.size, self.size), self.size), pl.ds(*self.lanes)]

    def remote(self, src, dst, send_sem, recv_sem, device):
        return pltpu.make_async_remote_copy(
            src_ref=src, dst_ref=dst, send_sem=send_sem, recv_sem=recv_sem, device_id=device, device_id_type=MESH
        )

    def inner(self, a_at, b_at):
        place = self.place
        return [
            (by_distance(a_at, place.na, ka), by_distance(b_at, place.nb, kb))
            for kb in reversed(range(place.nb))
            for ka in reversed(range(place.na))
        ]

    def open(self, i):
        place, zb = self.place, self.order[i]
        their_a, their_b = (place.b, place.a) if place.swaps else (place.a, place.b)
        for (ao, bo), (at, bt) in zip(self.inner(place.a, place.b), self.inner(their_a, their_b), strict=True):
            slot = self.slot(zb, ao, bo)
            pltpu.make_async_copy(self.piece(place.core, zb, ao, bo), self.own.at[slot], self.load_sem.at[slot]).start()
            slot = self.slot(zb, at, bt)
            copy = self.remote(
                self.piece(1 - place.core, zb, at, bt), self.sib.at[slot], self.send_sem.at[0, slot], self.sib_sem.at[slot], self.sibling
            )
            copy.start()

    def add(self, slot, buffer, sem, at):
        self.remote(self.own.at[slot], buffer.at[at], self.send_sem.at[1, slot], sem.at[at], self.sibling).wait_recv()
        self.own[slot] = (self.own[slot].astype(F32) + buffer[at].astype(F32)).astype(self.own.dtype)

    def both_cores(self, zb, ab, bb):
        slot = self.slot(zb, ab, bb)
        pltpu.make_async_copy(self.piece(self.place.core, zb, ab, bb), self.own.at[slot], self.load_sem.at[slot]).wait()
        self.add(slot, self.sib, self.sib_sem, slot)

    def pass_on(self, name, at, places, target, inner, inner_count, slot, condition=None):
        line, sem = self.lines[name]
        move = jnp.where(target > at, 1, -1)
        if places == 2:
            there = inner
        else:
            outer = (at - move >= 0) & (at - move < places)
            if condition is not None:
                outer = outer & condition
            pl.when(outer)(lambda: self.add(slot, line, sem, target * inner_count + inner))
            there = jnp.where((target == at + move) & (move < 0), places, target) * inner_count + inner
        device = self.place.device(**{name: at + move})
        copy = self.remote(self.own.at[slot], line.at[there], self.send_sem.at[1, slot], sem.at[there], device)
        when(condition, copy.start)

    def take_in(self, name, at, places, inner, inner_count, slot, condition=None):
        line, sem = self.lines[name]
        if places == 1:
            return
        if places == 2:
            when(condition, lambda: self.add(slot, line, sem, inner))
            return
        lower, upper = at > 0, at < places - 1
        if condition is not None:
            lower, upper = lower & condition, upper & condition
        pl.when(lower)(lambda: self.add(slot, line, sem, at * inner_count + inner))
        pl.when(upper)(lambda: self.add(slot, line, sem, places * inner_count + inner))

    def first(self, i):
        place, zb = self.place, self.order[i]
        for kb in reversed(range(1, place.nb)):
            bb = by_distance(place.b, place.nb, kb)
            for ka in reversed(range(place.na)):
                ab = by_distance(place.a, place.na, ka)
                self.both_cores(zb, ab, bb)
                inner, count = zb * place.na + ab, place.nz * place.na
                self.pass_on("b", place.b, place.nb, bb, inner, count, self.slot(zb, ab, bb))
        for ka in reversed(range(place.na)):
            self.both_cores(zb, by_distance(place.a, place.na, ka), place.b)

    def second(self, i):
        place, zb = self.place, self.order[i]
        for ka in reversed(range(place.na)):
            ab = by_distance(place.a, place.na, ka)
            slot = self.slot(zb, ab, place.b)
            self.take_in("b", place.b, place.nb, zb * place.na + ab, place.nz * place.na, slot)
            if ka:
                self.pass_on("a", place.a, place.na, ab, zb, place.nz, slot)

    def third(self, i):
        place, zb = self.place, self.order[i]
        slot = self.slot(zb, place.a, place.b)
        self.take_in("a", place.a, place.na, zb, place.nz, slot)
        if i < place.nz - 1:
            self.pass_on("z", place.z, place.nz, zb, 0, 1, slot)

    def last(self, out_ref):
        place = self.place
        slot = self.slot(place.z, place.a, place.b)
        self.take_in("z", place.z, place.nz, 0, 1, slot)
        out_ref[...] = self.own[slot].astype(F32)

    def actions(self):
        n = self.place.nz
        found = []
        for i in range(n + 2):
            for step, back in ((self.first, 0), (self.second, 1), (self.third, 2)):
                if 0 <= i - back < n:
                    found.append(functools.partial(step, i - back))
        return found

    def drain(self):
        place = self.place
        mine = self.slot(place.z, place.a, place.b)
        for slot in range(place.nz * place.na * place.nb):
            for kind in range(2):
                copy = self.remote(self.sib.at[slot], self.sib.at[slot], self.send_sem.at[kind, slot], self.sib_sem.at[slot], self.sibling)
                when(None if kind == 0 else mine != slot, copy.wait_send)


def reduction_scratch(layout, block_shape, dtype):
    _, (_, _, nb), (_, _, na), (_, _, nz) = layout
    deep = lambda places: 1 if places <= 2 else places + 1
    vm = lambda *lead: pltpu.VMEM(lead + block_shape, dtype)
    dma = pltpu.SemaphoreType.DMA
    per_core = nz * na * nb
    counts = {"b": deep(nb) * nz * na, "a": deep(na) * nz, "z": deep(nz)}
    return [
        vm(per_core), vm(per_core), vm(counts["b"]), vm(counts["a"]), vm(counts["z"]),
        dma((per_core,)), dma((2, per_core)),
        dma((per_core,)), dma((counts["b"],)), dma((counts["a"],)), dma((counts["z"],)),
    ]


BUFFERS = 11


def row_tiles(rows):
    return rows if rows % 16 == 0 else None


def projection_grads(every, grad_keys, grad_values, pairs, near_grads, share):
    width = every.shape[1]
    rows = pairs[0][0].shape[0]
    tall = 2 * rows if every.shape[0] % (2 * rows) == 0 else rows
    many = every.shape[0] // tall
    order = [(7, 1), (4, 1), (3, 1), (5, 1), (6, 1), (0, 1), (1, many), (2, many)]
    matrix_of, start_of = [], {}
    for matrix, count in order:
        start_of[matrix] = len(matrix_of)
        matrix_of += [matrix] * count
    steps = len(matrix_of)

    def body(table_ref, every_ref, gk_ref, gv_ref, l0, r0, l1, r1, l2, r2, l3, r3, n5, n6, out_ref, acc_ref):
        step = pl.program_id(0)
        sources = {0: (l0, r0), 3: (l1, r1), 4: (l2, r2), 7: (l3, r3), 1: (every_ref, gk_ref), 2: (every_ref, gv_ref)}
        for matrix, count in order:
            start = start_of[matrix]
            if matrix in (5, 6):

                @pl.when(step == start)
                def _(near_ref=n5 if matrix == 5 else n6):
                    out_ref[0] = near_ref[...]

                continue
            left, right = sources[matrix]

            @pl.when((step >= start) & (step < start + count))
            def _(left=left, right=right, start=start, count=count):
                if count == 1:
                    out_ref[0] = transposed_times(left[...], right[...]).astype(BF16)
                    return
                term = transposed_times(left[...], right[...])

                @pl.when(step == start)
                def _():
                    acc_ref[...] = term

                @pl.when(step > start)
                def _():
                    acc_ref[...] += term

                @pl.when(step == start + count - 1)
                def _():
                    out_ref[0] = acc_ref[...].astype(BF16)

    def chunk(start):
        return pl.BlockSpec((tall, width), lambda i, _: (jnp.clip(i - start, 0, many - 1), 0))

    both = pl.BlockSpec(
        (tall, width), lambda i, _: (jnp.clip(jnp.where(i < start_of[2], i - start_of[1], i - start_of[2]), 0, many - 1), 0)
    )
    square = pl.BlockSpec((width, width), lambda i, _: (0, 0))
    in_specs = [both, chunk(start_of[1]), chunk(start_of[2])] + [pl.BlockSpec((rows, width), lambda i, _: (0, 0))] * 8
    return pl.pallas_call(
        body,
        grid_spec=pltpu.PrefetchScalarGridSpec(
            num_scalar_prefetch=1,
            grid=(steps,),
            in_specs=in_specs + [square, square],
            out_specs=pl.BlockSpec((1, width, width), lambda i, table: (table[i], 0, 0)),
            scratch_shapes=[pltpu.VMEM((width, width), F32)],
        ),
        out_shape=jax.ShapeDtypeStruct((8, width, width), BF16),
        cost_estimate=pl.CostEstimate(
            flops=2 * width * width * (2 * every.shape[0] + 4 * pairs[0][0].shape[0]), transcendentals=0, bytes_accessed=40_000_000
        ),
        compiler_params=pltpu.CompilerParams(vmem_limit_bytes=50_000_000),
        name="projection_grads",
    )(jnp.asarray(matrix_of, jnp.int32), every, grad_keys, grad_values, *[side for pair in pairs for side in pair], *near_grads)


def last_steps(layout, sizes, matrix_grads, share, lines, grad_queries, query_matrix, joined, hidden, gain, grad_first):
    tokens, width = grad_queries.shape
    bits = lambda count: [1 << i for i in range(count.bit_length() - 1)]
    rounds = [("fsdp", step) for step in bits(sizes[1])] + [("dp", step) for step in bits(sizes[0])]
    given = [line for line in lines if line is not None]
    per_gain = width // 128
    total_rows = sum(per_gain if line is None else line.shape[0] for line in lines)
    held_rows = -(-total_rows // 8) * 8

    def body(*refs):
        (mats_ref, dq_ref, m0_ref, in_ref, hid_ref, gf_ref, gain_ref), refs = refs[:7], refs[7:]
        line_refs, refs = list(refs[: len(given)]), refs[len(given) :]
        (attn_ref, sum_ref, hg_ref), refs = refs[:3], refs[3:]
        (q_buf, m0, in_buf, hid_buf, first_buf, load_sem), refs = refs[:6], refs[6:]
        (line_out, line_in, line_send, line_recv), buffers = refs[:4], refs[4:]
        place = Place(layout)
        index = {axis: lax.axis_index(axis).astype(jnp.int32) for axis in AXES}
        across = lambda axis, step: {axis: index[axis] + step * (1 - 2 * ((index[axis] // step) % 2))}
        meet(place, [across(axis, step) for axis, step in rounds])
        loads = [
            pltpu.make_async_copy(src, dst, load_sem.at[i])
            for i, (src, dst) in enumerate(
                ((dq_ref, q_buf), (m0_ref, m0), (in_ref, in_buf), (hid_ref, hid_buf), (gf_ref, first_buf))
            )
        ]
        big = Reduction(place, mats_ref, row_tiles(share), (0, width), buffers)
        for i in range(place.nz):
            big.open(i)
            if i == 0:
                for load in loads:
                    load.start()
        actions = big.actions()
        actions.pop(0)()
        for load in loads:
            load.wait()
        piece = tokens // 4

        def finish(i, total):
            rows = pl.ds(pl.multiple_of(i * piece, piece), piece)
            held = hid_buf[rows, :].astype(F32)
            scale = inverse_rms(held)
            grad = dot_t(q_buf[rows, :], m0[...]) + in_buf[rows, :]
            hg_ref[rows, :] = first_buf[rows, :] + norm_back(held, scale, gain_ref[...], grad)
            return total + jnp.sum(grad * held * scale, axis=0, keepdims=True)

        gain_grad = lax.fori_loop(0, 4, finish, jnp.zeros((1, width), F32))
        at = 0
        for line in lines:
            if line is None:
                for i in range(per_gain):
                    sum_ref[at + i : at + i + 1, :] = gain_grad[:, i * 128 : (i + 1) * 128]
                at += per_gain
            else:
                ref = line_refs.pop(0)
                sum_ref[at : at + ref.shape[0], :] = ref[...]
                at += ref.shape[0]
        if at < held_rows:
            sum_ref[at:, :] = jnp.zeros((held_rows - at, 128), F32)

        def round_copy(i):
            axis, step = rounds[i]
            return pltpu.make_async_remote_copy(
                src_ref=line_out.at[i], dst_ref=line_in.at[i], send_sem=line_send.at[i], recv_sem=line_recv.at[i],
                device_id=across(axis, step), device_id_type=MESH,
            )

        for i in range(len(rounds)):
            line_out[i] = sum_ref[...]
            round_copy(i).start()
            for _ in range(2):
                if actions:
                    actions.pop(0)()
            round_copy(i).wait_recv()
            sum_ref[...] += line_in[i]
        for action in actions:
            action()
        big.last(attn_ref)
        for i in range(len(rounds)):
            round_copy(i).wait_send()
        big.drain()

    anywhere = pl.BlockSpec(memory_space=pl.ANY)
    inside = pl.BlockSpec(memory_space=pltpu.VMEM)
    block = (share, width)
    dma = pltpu.SemaphoreType.DMA
    scratch = [
        pltpu.VMEM(grad_queries.shape, BF16), pltpu.VMEM((width, width), BF16), pltpu.VMEM(joined.shape, joined.dtype),
        pltpu.VMEM(hidden.shape, hidden.dtype), pltpu.VMEM(grad_first.shape, F32), dma((5,)),
        pltpu.VMEM((len(rounds), held_rows, 128), F32), pltpu.VMEM((len(rounds), held_rows, 128), F32),
        dma((len(rounds),)), dma((len(rounds),)),
    ]
    scratch += reduction_scratch(layout, block, BF16)
    return pl.pallas_call(
        body,
        out_shape=[
            jax.ShapeDtypeStruct(block, F32),
            jax.ShapeDtypeStruct((held_rows, 128), F32),
            jax.ShapeDtypeStruct((tokens, width), F32),
        ],
        in_specs=[anywhere] * 6 + [inside] * (1 + len(given)),
        out_specs=[inside] * 3,
        scratch_shapes=scratch,
        compiler_params=pltpu.CompilerParams(collective_id=2, has_side_effects=True, vmem_limit_bytes=50_000_000),
        name="last_steps",
    )(matrix_grads, grad_queries, query_matrix, joined, hidden, grad_first, gain.reshape(1, width), *given)


def from_behind(array, axis, by):
    length = lax.axis_size(axis)
    pairs = [(i, i + by) for i in range(length) if 0 <= i + by < length]
    return lax.ppermute(array, axis, pairs)


def sum_of_group(parts, place):
    group = parts.shape[0]
    if group & (group - 1):
        return lax.psum_scatter(parts, "fsdp", scatter_dimension=0, tiled=True)[0].astype(F32)
    step = 1
    while step < group:
        halves = parts.reshape((parts.shape[0] // 2, 2) + parts.shape[1:])
        bit = (place // step) % 2
        away = lax.dynamic_index_in_dim(halves, 1 - bit, axis=1, keepdims=False)
        kept = lax.dynamic_index_in_dim(halves, bit, axis=1, keepdims=False)
        came = lax.ppermute(away, "fsdp", [(i, i ^ step) for i in range(group)])
        parts = kept.astype(F32) + came.astype(F32)
        step *= 2
        if step < group:
            parts = parts.astype(BF16)
    return parts[0]


def product(left_side, right_side):
    return jnp.dot(left_side, right_side, preferred_element_type=F32)


def times_transposed(left_side, right_side):
    return lax.dot_general(left_side, right_side, (((1,), (1,)), ((), ())), preferred_element_type=F32)


def transposed_times(left_side, right_side):
    return lax.dot_general(left_side, right_side, (((0,), (0,)), ((), ())), preferred_element_type=F32)


def inverse_rms(residual):
    return lax.rsqrt(jnp.mean(residual * residual, axis=-1, keepdims=True) + norm_eps)


def norm_back(residual, scale, gain, incoming):
    weighted = gain * incoming
    return scale * weighted - residual * scale * scale * scale * jnp.mean(
        residual * weighted, axis=-1, keepdims=True
    )


def gelu_parts(values):
    tangent = jnp.tanh(gelu_scale * (values + gelu_cubic * values * values * values))
    result = 0.5 * values * (1.0 + tangent)
    slope = 0.5 * (1.0 + tangent) + 0.5 * values * (1.0 - tangent * tangent) * gelu_scale * (
        1.0 + 3.0 * gelu_cubic * values * values
    )
    return (result, slope)


def bucket_of(offset):
    magnitude = jnp.abs(offset)
    counted = jnp.zeros(offset.shape, jnp.int32)
    for threshold in relative_bucket_limits:
        counted = counted + (magnitude >= threshold).astype(jnp.int32)
    return counted + (offset > 0).astype(jnp.int32) * (len(relative_bucket_limits) + 1)


def piece_labels(positions, starts):
    inside = (positions[None, :, None] >= starts[:, None, :]) & (
        positions[None, :, None] < starts[:, None, :] + PIECE
    )
    labels = jnp.arange(1, starts.shape[1] + 1, dtype=jnp.int32)
    return jnp.sum(jnp.where(inside, labels[None, None, :], 0), axis=2)


def dot_t(left_side, right_side):
    return lax.dot_general(left_side, right_side, (((1,), (1,)), ((), ())), preferred_element_type=F32)


def own_lanes(values, which, width):
    lane = lax.broadcasted_iota(jnp.int32, values.shape, 1)
    return jnp.where((lane >= which * width) & (lane < (which + 1) * width), values, jnp.zeros_like(values))


def flipped(values):
    return values.astype(F32).T.astype(BF16)


def bias_lines(rel_table, rows, reach):
    heads = rel_table.shape[1]
    width = 2 * rows
    count = 2 * reach + 1
    shift = jnp.arange(width, dtype=jnp.int32)
    behind = jnp.where(shift < rows, shift, shift - width)
    far = (jnp.arange(count, dtype=jnp.int32) - reach) * rows
    ids = bucket_of(far[:, None] - behind[None, :])
    hot = (ids[:, :, None] == jnp.arange(rel_table.shape[0], dtype=jnp.int32)).astype(F32)
    lines = jnp.einsum("dwb,bh->hdw", hot, rel_table, precision=lax.Precision.HIGHEST)
    return lines.reshape(heads, count, 1, width)


def tile_at(block, place, reach):
    return jnp.clip(block - place, -reach, reach) + reach


def self_attention(place, query, keys, values, tiles, hidden_mask, head_size, reach):
    count, rows, width = query.shape
    blocks = keys.shape[0]
    pair = 128
    per = pair // head_size

    def body(place_ref, q_ref, k_ref, v_ref, tile_ref, mask_ref, o_ref, ot_ref, lse_ref, s_ref, p_ref):
        for b in range(count):
            scaled = q_ref[b] * jnp.asarray(0.125, BF16)
            value_t = jnp.concatenate([flipped(v_ref[j, b]) for j in range(blocks)], axis=1)
            for h in range(per):
                mine = own_lanes(scaled, h, head_size)
                top = jnp.full((1, rows), -jnp.inf, F32)
                for j in range(blocks):
                    s = dot_t(k_ref[j, b], mine)
                    s = s + tile_ref[h, tile_at(j, place_ref[0], reach)] + mask_ref[b, j]
                    s_ref[j] = s
                    top = jnp.maximum(top, jnp.max(s, axis=0, keepdims=True))
                total = jnp.zeros((1, rows), F32)
                for j in range(blocks):
                    p = jnp.exp(s_ref[j] - top)
                    total = total + jnp.sum(p, axis=0, keepdims=True)
                    p_ref[j * rows : (j + 1) * rows, :] = p.astype(BF16)
                part = product(value_t[h * head_size : (h + 1) * head_size], p_ref[...]) / total
                ot_ref[0, b, h * head_size : (h + 1) * head_size, :] = part
                lse_ref[0, b * per + h : b * per + h + 1, :] = top + jnp.log(total)
            o_ref[b] = ot_ref[0, b].T.astype(BF16)

    steps = width // pair
    grid_spec = pltpu.PrefetchScalarGridSpec(
        num_scalar_prefetch=1,
        grid=(steps,),
        in_specs=[
            pl.BlockSpec((count, rows, pair), lambda i, _: (0, 0, i)),
            pl.BlockSpec((blocks, count, rows, pair), lambda i, _: (0, 0, 0, i)),
            pl.BlockSpec((blocks, count, rows, pair), lambda i, _: (0, 0, 0, i)),
            pl.BlockSpec((per,) + tiles.shape[1:], lambda i, _: (i, 0, 0, 0)),
            pl.BlockSpec(hidden_mask.shape, lambda i, _: (0, 0, 0, 0)),
        ],
        out_specs=[
            pl.BlockSpec((count, rows, pair), lambda i, _: (0, 0, i)),
            pl.BlockSpec((1, count, pair, rows), lambda i, _: (i, 0, 0, 0)),
            pl.BlockSpec((1, count * per, rows), lambda i, _: (i, 0, 0)),
        ],
        scratch_shapes=[
            pltpu.VMEM((blocks, rows, rows), F32),
            pltpu.VMEM((blocks * rows, rows), BF16),
        ],
    )
    cost = 4 * count * blocks * rows * rows * width
    return pl.pallas_call(
        body,
        grid_spec=grid_spec,
        out_shape=[
            jax.ShapeDtypeStruct((count, rows, width), BF16),
            jax.ShapeDtypeStruct((steps, count, pair, rows), F32),
            jax.ShapeDtypeStruct((steps, count * per, rows), F32),
        ],
        cost_estimate=pl.CostEstimate(flops=4 * cost, transcendentals=0, bytes_accessed=30_000_000),
        name="self_attention",
    )(place, query, keys, values, tiles, hidden_mask)


def self_attention_back(place, query, keys, values, tiles, hidden_mask, outer_t, lse, grad, head_size, reach):
    count, rows, width = query.shape
    blocks = keys.shape[0]
    pair = 128
    per = pair // head_size
    half = rows // 2

    def body(
        place_ref, q_ref, k_ref, v_ref, tile_ref, mask_ref, ot_ref, lse_ref, do_ref,
        dq_ref, dk_ref, dv_ref, sum_ref, acc_ref, dk_acc, dv_acc,
    ):
        for b in range(count):
            scaled = q_ref[b] * jnp.asarray(0.125, BF16)
            incoming = do_ref[b]
            key_t = jnp.concatenate([flipped(k_ref[j, b]) for j in range(blocks)], axis=1)
            weighed = incoming.astype(F32).T * ot_ref[0, b]
            query_parts = []
            for h in range(per):
                lanes = slice(h * head_size, (h + 1) * head_size)
                mine = own_lanes(scaled, h, head_size)
                theirs = own_lanes(incoming, h, head_size)
                delta = jnp.sum(weighed[lanes], axis=0, keepdims=True)
                level = lse_ref[0, b * per + h : b * per + h + 1, :]
                part = jnp.zeros((head_size, rows), F32)
                for j in range(blocks):
                    s = dot_t(k_ref[j, b], mine)
                    s = s + tile_ref[h, tile_at(j, place_ref[0], reach)] + mask_ref[b, j]
                    p = jnp.exp(s - level)
                    ds = p * (dot_t(v_ref[j, b], theirs) - delta)
                    p_low = p.astype(BF16)
                    ds_low = ds.astype(BF16)
                    dv = product(p_low, theirs)
                    dk = product(ds_low, mine)
                    if h == 0:
                        dv_acc[j] = dv
                        dk_acc[j] = dk
                    else:
                        dv_ref[j, b] = (dv_acc[j] + dv).astype(BF16)
                        dk_ref[j, b] = (dk_acc[j] + dk).astype(BF16)
                    part = part + product(key_t[lanes, j * rows : (j + 1) * rows], ds_low)
                    if b == 0:
                        acc_ref[h, j] = ds
                    else:
                        acc_ref[h, j] = acc_ref[h, j] + ds
                query_parts.append(part)
            dq_ref[b] = (jnp.concatenate(query_parts, axis=0) * 0.125).T.astype(BF16)
        for h in range(per):
            for j in range(blocks):
                upper, lower = acc_ref[h, j, :half, :], acc_ref[h, j, half:, :]
                folded = jnp.concatenate(
                    [lower[:, :half], lower[:, half:] + upper[:, :half], upper[:, half:], jnp.zeros((half, half), F32)],
                    axis=1,
                )
                left = half // 2
                while left >= 8:
                    folded = folded[left:] + pltpu.roll(folded[:left], left, 1)
                    left //= 2
                sum_ref[h, j] = folded

    steps = width // pair
    grid_spec = pltpu.PrefetchScalarGridSpec(
        num_scalar_prefetch=1,
        grid=(steps,),
        in_specs=[
            pl.BlockSpec((count, rows, pair), lambda i, _: (0, 0, i)),
            pl.BlockSpec((blocks, count, rows, pair), lambda i, _: (0, 0, 0, i)),
            pl.BlockSpec((blocks, count, rows, pair), lambda i, _: (0, 0, 0, i)),
            pl.BlockSpec((per,) + tiles.shape[1:], lambda i, _: (i, 0, 0, 0)),
            pl.BlockSpec(hidden_mask.shape, lambda i, _: (0, 0, 0, 0)),
            pl.BlockSpec((1, count, pair, rows), lambda i, _: (i, 0, 0, 0)),
            pl.BlockSpec((1, count * per, rows), lambda i, _: (i, 0, 0)),
            pl.BlockSpec((count, rows, pair), lambda i, _: (0, 0, i)),
        ],
        out_specs=[
            pl.BlockSpec((count, rows, pair), lambda i, _: (0, 0, i)),
            pl.BlockSpec((blocks, count, rows, pair), lambda i, _: (0, 0, 0, i)),
            pl.BlockSpec((blocks, count, rows, pair), lambda i, _: (0, 0, 0, i)),
            pl.BlockSpec((per, blocks, 8, 2 * rows), lambda i, _: (i, 0, 0, 0)),
        ],
        scratch_shapes=[
            pltpu.VMEM((per, blocks, rows, rows), F32),
            pltpu.VMEM((blocks, rows, pair), F32),
            pltpu.VMEM((blocks, rows, pair), F32),
        ],
    )
    cost = 4 * count * blocks * rows * rows * width
    return pl.pallas_call(
        body,
        grid_spec=grid_spec,
        out_shape=[
            jax.ShapeDtypeStruct((count, rows, width), BF16),
            jax.ShapeDtypeStruct((blocks, count, rows, width), BF16),
            jax.ShapeDtypeStruct((blocks, count, rows, width), BF16),
            jax.ShapeDtypeStruct((width // head_size, blocks, 8, 2 * rows), F32),
        ],
        cost_estimate=pl.CostEstimate(flops=10 * cost, transcendentals=0, bytes_accessed=40_000_000),
        name="self_attention_back",
    )(place, query, keys, values, tiles, hidden_mask, outer_t, lse, grad)


def whole(shape):
    return pl.BlockSpec(shape, lambda *_: (0,) * len(shape))


def feed_forward(second_sum, gain, grad_out_low, weights, bias_input, bias_output):
    tokens, width = second_sum.shape
    units = bias_input.shape[0]
    tile = 512
    steps = units // tile
    part = 256

    def body(sum_ref, gain_ref, go_ref, wi_ref, wo_ref, bi_ref, bo_ref, out_ref, gs_ref, gg_ref, gbi_ref, gbo_ref, gw_ref, n_ref, acc_ref, gn_ref):
        step = pl.program_id(0)

        @pl.when(step == 0)
        def _():
            held = sum_ref[...]
            n_ref[...] = (held * inverse_rms(held) * gain_ref[...]).astype(BF16)
            acc_ref[...] = jnp.zeros_like(acc_ref)
            gn_ref[...] = jnp.zeros_like(gn_ref)

        normed = n_ref[...]
        incoming = go_ref[...]
        for at in range(0, tile, part):
            rows = slice(at, at + part)
            w_in, w_out = wi_ref[rows, :], wo_ref[rows, :]
            value, slope = gelu_parts(dot_t(normed, w_in) + bi_ref[0, :, rows])
            value_low = value.astype(BF16)
            grad_pre = dot_t(incoming, w_out) * slope
            bias_grad = jnp.sum(grad_pre, axis=0, keepdims=True)
            for i in range(part // 128):
                gbi_ref[0, at // 128 + i : at // 128 + i + 1, :] = bias_grad[:, i * 128 : (i + 1) * 128]
            grad_pre_low = grad_pre.astype(BF16)
            acc_ref[...] += product(value_low, w_out)
            gn_ref[...] += product(grad_pre_low, w_in)
            gw_ref[0, 0, rows, :] = transposed_times(grad_pre_low, normed).astype(BF16)
            gw_ref[1, 0, rows, :] = transposed_times(value_low, incoming).astype(BF16)

        @pl.when(step == steps - 1)
        def _():
            held = sum_ref[...]
            scale = inverse_rms(held)
            out_ref[...] = (held + acc_ref[...] + bo_ref[...]).astype(BF16)
            grad_norm = gn_ref[...]
            grad_out = incoming.astype(F32)
            for ref, line in (
                (gbo_ref, jnp.sum(grad_out, axis=0, keepdims=True)),
                (gg_ref, jnp.sum(grad_norm * held * scale, axis=0, keepdims=True)),
            ):
                for i in range(width // 128):
                    ref[i : i + 1, :] = line[:, i * 128 : (i + 1) * 128]
            gs_ref[...] = grad_out + norm_back(held, scale, gain_ref[...], grad_norm)

    tall, line = whole((tokens, width)), whole((1, width))
    rows_of_128 = whole((width // 128, 128))
    return pl.pallas_call(
        body,
        grid=(steps,),
        in_specs=[
            tall, line, tall,
            pl.BlockSpec((tile, width), lambda i: (i, 0)),
            pl.BlockSpec((tile, width), lambda i: (i + steps, 0)),
            pl.BlockSpec((1, 1, tile), lambda i: (i, 0, 0)),
            line,
        ],
        out_specs=[
            tall, tall, rows_of_128,
            pl.BlockSpec((1, tile // 128, 128), lambda i: (i, 0, 0)),
            rows_of_128,
            pl.BlockSpec((2, 1, tile, width), lambda i: (0, i, 0, 0)),
        ],
        out_shape=[
            jax.ShapeDtypeStruct((tokens, width), BF16),
            jax.ShapeDtypeStruct((tokens, width), F32),
            jax.ShapeDtypeStruct((width // 128, 128), F32),
            jax.ShapeDtypeStruct((steps, tile // 128, 128), F32),
            jax.ShapeDtypeStruct((width // 128, 128), F32),
            jax.ShapeDtypeStruct((2, steps, tile, width), BF16),
        ],
        scratch_shapes=[
            pltpu.VMEM((tokens, width), BF16),
            pltpu.VMEM((tokens, width), F32),
            pltpu.VMEM((tokens, width), F32),
        ],
        cost_estimate=pl.CostEstimate(flops=12 * tokens * width * units, transcendentals=0, bytes_accessed=40_000_000),
        compiler_params=pltpu.CompilerParams(vmem_limit_bytes=50_000_000),
        name="feed_forward",
    )(
        second_sum, gain.reshape(1, width), grad_out_low, weights, weights,
        bias_input.reshape(steps, 1, tile), bias_output.reshape(1, width),
    )


def span_projection(near, key_matrix, value_matrix):
    blocks, rows, width = near.shape

    def body(near_ref, mk_ref, mv_ref, k_ref, v_ref):
        k_ref[0] = product(near_ref[0], mk_ref[...]).astype(BF16)
        v_ref[0] = product(near_ref[0], mv_ref[...]).astype(BF16)

    block = pl.BlockSpec((1, rows, width), lambda i: (i, 0, 0))
    return pl.pallas_call(
        body,
        grid=(blocks,),
        in_specs=[block, whole((width, width)), whole((width, width))],
        out_specs=[block, block],
        out_shape=[jax.ShapeDtypeStruct(near.shape, BF16)] * 2,
        cost_estimate=pl.CostEstimate(flops=4 * blocks * rows * width * width, transcendentals=0, bytes_accessed=15_000_000),
        name="span_projection",
    )(near, key_matrix, value_matrix)


def both_heads(values, head_size):
    return jnp.concatenate([own_lanes(values, h, head_size) for h in range(128 // head_size)], axis=0)


def picked(wide, rows, head_size):
    total = own_lanes(wide[:rows], 0, head_size)
    for h in range(1, 128 // head_size):
        total = total + own_lanes(wide[h * rows : (h + 1) * rows], h, head_size)
    return total


def softmax_down(scores):
    raised = jnp.exp(scores - jnp.max(scores, axis=0, keepdims=True))
    return raised / jnp.sum(raised, axis=0, keepdims=True)


def lane_groups(width):
    return [slice(i, i + 128) for i in range(0, width, 128)]


def side_by_side(parts):
    return jnp.concatenate(parts, axis=1)


def span_attention(query, keys, values, head_size):
    blocks, rows, width = query.shape
    span_keys = keys.shape[1]

    def body(q_ref, k_ref, v_ref, o_ref):
        groups = lane_groups(width)
        scaled = q_ref[0] * jnp.asarray(0.125, BF16)
        scores = side_by_side([dot_t(k_ref[0, :, g], both_heads(scaled[:, g], head_size)) for g in groups])
        weights = softmax_down(scores).astype(BF16)
        turned = flipped(v_ref[0])
        wide = [product(turned[g], weights[:, g]).T for g in groups]
        o_ref[0] = side_by_side([picked(w, rows, head_size) for w in wide]).astype(BF16)

    q_spec = pl.BlockSpec((1, rows, width), lambda i: (i, 0, 0))
    k_spec = pl.BlockSpec((1, span_keys, width), lambda i: (i, 0, 0))
    return pl.pallas_call(
        body,
        grid=(blocks,),
        in_specs=[q_spec, k_spec, k_spec],
        out_specs=q_spec,
        out_shape=jax.ShapeDtypeStruct(query.shape, BF16),
        cost_estimate=pl.CostEstimate(flops=16 * blocks * rows * span_keys * width, transcendentals=0, bytes_accessed=12_000_000),
        name="span_attention",
    )(query, keys, values)


def span_attention_back(query, keys, values, grad, near, key_matrix, value_matrix, head_size):
    blocks, rows, width = query.shape
    span_keys = keys.shape[1]

    def body(q_ref, k_ref, v_ref, do_ref, near_ref, mk_ref, mv_ref, dq_ref, dn_ref, gk_ref, gv_ref, gk_acc, gv_acc):
        step = pl.program_id(0)
        groups = lane_groups(width)
        scaled = q_ref[0] * jnp.asarray(0.125, BF16)
        incoming = do_ref[0]
        stacked = [both_heads(scaled[:, g], head_size) for g in groups]
        theirs = [both_heads(incoming[:, g], head_size) for g in groups]
        k, v = k_ref[0], v_ref[0]
        p = softmax_down(side_by_side([dot_t(k[:, g], s) for g, s in zip(groups, stacked)]))
        dp = side_by_side([dot_t(v[:, g], t) for g, t in zip(groups, theirs)])
        ds = p * (dp - jnp.sum(p * dp, axis=0, keepdims=True))
        ds_low, p_low = ds.astype(BF16), p.astype(BF16)
        dv = side_by_side([product(p_low[:, g], t) for g, t in zip(groups, theirs)]).astype(BF16)
        dk = side_by_side([product(ds_low[:, g], s) for g, s in zip(groups, stacked)]).astype(BF16)
        turned = flipped(k)
        wide = [(product(turned[g], ds_low[:, g]) * 0.125).T for g in groups]
        dq_ref[0] = side_by_side([picked(w, rows, head_size) for w in wide]).astype(BF16)
        dn_ref[0] = dot_t(dk, mk_ref[...]) + dot_t(dv, mv_ref[...])
        near_t = flipped(near_ref[0])

        @pl.when(step == 0)
        def _():
            gk_acc[...] = product(near_t, dk)
            gv_acc[...] = product(near_t, dv)

        @pl.when(step > 0)
        def _():
            gk_acc[...] += product(near_t, dk)
            gv_acc[...] += product(near_t, dv)

        @pl.when(step == blocks - 1)
        def _():
            gk_ref[...] = gk_acc[...].astype(BF16)
            gv_ref[...] = gv_acc[...].astype(BF16)

    q_spec = pl.BlockSpec((1, rows, width), lambda i: (i, 0, 0))
    k_spec = pl.BlockSpec((1, span_keys, width), lambda i: (i, 0, 0))
    square = whole((width, width))
    return pl.pallas_call(
        body,
        grid=(blocks,),
        in_specs=[q_spec, k_spec, k_spec, q_spec, k_spec, square, square],
        out_specs=[q_spec, k_spec, square, square],
        out_shape=[
            jax.ShapeDtypeStruct(query.shape, BF16),
            jax.ShapeDtypeStruct(keys.shape, F32),
            jax.ShapeDtypeStruct((width, width), BF16),
            jax.ShapeDtypeStruct((width, width), BF16),
        ],
        scratch_shapes=[pltpu.VMEM((width, width), F32), pltpu.VMEM((width, width), F32)],
        cost_estimate=pl.CostEstimate(flops=20 * blocks * span_keys * width * width, transcendentals=0, bytes_accessed=40_000_000),
        compiler_params=pltpu.CompilerParams(vmem_limit_bytes=50_000_000),
        name="span_attention_back",
    )(query, keys, values, grad, near, key_matrix, value_matrix)


def per_device(hidden, neighbours, piece_starts, out_grad, attn_weights, ffw_weights, vectors, rel_table):
    count, rows, width = hidden.shape
    group = lax.axis_size("fsdp")
    length = rows * group
    heads = rel_table.shape[1]
    head_size = width // heads
    buckets = rel_table.shape[0]
    spans = neighbours.shape[1]
    span_keys = neighbours.shape[2]
    carried = SPAN - 1
    kept = rows - carried
    tokens = count * rows
    reach = -(-relative_bucket_limits[-1] // rows) + 1
    place = lax.axis_index("fsdp").astype(jnp.int32)
    share = attn_weights.shape[0]

    gather = lambda array, axes: lax.all_gather(array, axes, axis=0, tiled=True)
    layout = layout_of((lax.axis_size("dp"), group))
    vector_rows = -(-vectors.shape[0] // 2048) * 16
    vector_block = jnp.pad(vectors, (0, vector_rows * 128 - vectors.shape[0])).reshape(vector_rows, 128)
    hidden_all = gather(hidden[None], "fsdp")
    (attn_full, vector_full), tiles = gather_with_tiles(
        layout, [attn_weights, vector_block], bias_lines(rel_table, rows, reach), rows
    )
    ffw_full = gather(lax.optimization_barrier((ffw_weights, vector_full))[0], AXES)
    matrices = attn_full.reshape(8, width, width)
    vector_full = vector_full.reshape(-1, vector_rows * 128)[:, : vectors.shape[0]].reshape(-1).astype(F32)
    bias_input = vector_full[:FF]
    gains = vector_full[FF : FF + 3 * width].reshape(3, width)
    bias_output = vector_full[FF + 3 * width :]

    key_pos = jnp.arange(length, dtype=jnp.int32)
    query_pos = place * rows + jnp.arange(rows, dtype=jnp.int32)
    key_piece = piece_labels(key_pos, piece_starts)
    query_piece = piece_labels(query_pos, piece_starts)
    allowed = (key_pos[:, None] <= query_pos[None, :])[None] | (
        (key_piece[:, :, None] == query_piece[:, None, :]) & (query_piece[:, None, :] > 0)
    )
    mask = jnp.where(allowed, 0.0, masked_score).reshape(count, group, rows, rows)
    place_arg = place.reshape(1)

    residual = hidden.reshape(tokens, width).astype(F32)
    every = hidden_all.reshape(group * tokens, width).astype(F32)
    normed_every = (every * inverse_rms(every) * gains[0]).astype(BF16)
    scale_one = inverse_rms(residual)
    normed_one = (residual * scale_one * gains[0]).astype(BF16)
    queries = product(normed_one, matrices[0]).astype(BF16).reshape(count, rows, width)
    keys = product(normed_every, matrices[1]).astype(BF16).reshape(group, count, rows, width)
    values = product(normed_every, matrices[2]).astype(BF16).reshape(group, count, rows, width)
    near = neighbours.reshape(count * spans, span_keys, width)
    cross_keys, cross_values = span_projection(near, matrices[5], matrices[6])
    context, context_t, lse = self_attention(
        place_arg, queries, keys, values, tiles, mask, head_size, reach
    )
    context = context.reshape(tokens, width)
    first_sum = residual + product(context, matrices[3])
    scale_two = inverse_rms(first_sum)
    normed_two = (first_sum * scale_two * gains[1]).astype(BF16)
    cross_queries = product(normed_two, matrices[4]).astype(BF16).reshape(count, rows, width)

    def ahead(array):
        incoming = from_behind(array[:, :carried], "fsdp", -1)
        return jnp.concatenate([array[:, carried:], incoming], axis=1).reshape(count * spans, SPAN, width)

    def behind(array):
        array = array.reshape(count, rows, width)
        arriving = from_behind(array[:, kept:], "fsdp", 1)
        return jnp.concatenate([arriving, array[:, :kept]], axis=1).reshape(tokens, width)

    block_queries = ahead(cross_queries)
    placed = behind(span_attention(block_queries, cross_keys, cross_values, head_size))
    second_sum = first_sum + product(placed, matrices[7])
    output, grad_second, grad_gain_three, grad_bias_input, grad_bias_output, ffw_step = feed_forward(
        second_sum, gains[2], out_grad.reshape(tokens, width), ffw_full, bias_input, bias_output
    )
    blocks_of = lambda array: array.reshape((-1, width) if row_tiles(share) else (-1, share, width))
    ffw_sum = lax.psum_scatter(ffw_step.reshape(2 * FF, width), AXES, scatter_dimension=0, tiled=True)
    grad_second_low = grad_second.astype(BF16)
    grad_placed = times_transposed(grad_second_low, matrices[7]).astype(BF16).reshape(count, rows, width)
    grad_block_queries, near_grad, grad_cross_key_mat, grad_cross_value_mat = span_attention_back(
        block_queries, cross_keys, cross_values, ahead(grad_placed), near, matrices[5], matrices[6], head_size
    )
    grad_cross_queries = behind(grad_block_queries)
    grad_norm_two = times_transposed(grad_cross_queries, matrices[4])
    grad_gain_two = jnp.sum(grad_norm_two * first_sum * scale_two, axis=0)
    grad_first = grad_second + norm_back(first_sum, scale_two, gains[1], grad_norm_two)
    grad_first_low = grad_first.astype(BF16)
    grad_context = times_transposed(grad_first_low, matrices[3]).astype(BF16).reshape(count, rows, width)
    grad_queries, grad_keys, grad_values, diagonal = self_attention_back(
        place_arg, queries, keys, values, tiles, mask, context_t, lse, grad_context, head_size, reach
    )
    grad_queries = grad_queries.reshape(tokens, width)
    partial_one = (
        times_transposed(grad_keys.reshape(group * tokens, width), matrices[1])
        + times_transposed(grad_values.reshape(group * tokens, width), matrices[2])
    ).astype(BF16)
    joined = sum_of_group(partial_one.reshape(group, tokens, width), place)
    matrix_step = projection_grads(
        normed_every,
        grad_keys.reshape(group * tokens, width),
        grad_values.reshape(group * tokens, width),
        [
            (normed_one, grad_queries),
            (context, grad_first_low),
            (normed_two, grad_cross_queries),
            (placed, grad_second_low),
        ],
        (grad_cross_key_mat, grad_cross_value_mat),
        share,
    )
    lane = jnp.arange(2 * rows, dtype=jnp.int32)
    line = jnp.arange(8, dtype=jnp.int32)
    block = jnp.arange(group, dtype=jnp.int32)
    between = (block[:, None, None] - place) * rows - (lane[None, None, :] - (rows - 8) - line[None, :, None])
    hot = (bucket_of(between)[..., None] == jnp.arange(buckets, dtype=jnp.int32)).astype(F32)
    table_step = jnp.einsum("hjsl,jslb->bh", diagonal, hot, precision=lax.Precision.HIGHEST)

    lines_of = lambda array: array.reshape(-1, 128)
    table_rows = -(-buckets * heads // 128)
    table_line = jnp.pad(table_step.reshape(-1), (0, table_rows * 128 - buckets * heads)).reshape(table_rows, 128)
    attn_sum, line_sum, hidden_grad = last_steps(
        layout, (lax.axis_size("dp"), group), blocks_of(matrix_step), share,
        [lines_of(grad_bias_input), None, lines_of(grad_gain_two), grad_gain_three, grad_bias_output, table_line],
        grad_queries, matrices[0], joined, hidden.reshape(tokens, width), gains[0], grad_first,
    )
    line_sum = line_sum.reshape(-1)
    own = vectors.shape[0]
    vector_sum = lax.dynamic_slice(line_sum, (lax.axis_index(AXES) * own,), (own,))
    table_sum = line_sum[FF + 4 * width : FF + 4 * width + buckets * heads].reshape(buckets, heads)
    return (
        output.reshape(count, rows, width),
        hidden_grad.reshape(count, rows, width),
        near_grad.reshape(count, spans, span_keys, width),
        attn_sum,
        ffw_sum.astype(F32),
        vector_sum,
        table_sum,
    )


def solution(mesh):
    placed = (
        P("dp", "fsdp", None),
        P("dp", "fsdp", None, None),
        P("dp", None),
        P("dp", "fsdp", None),
        P(("dp", "fsdp"), None),
        P(("dp", "fsdp"), None),
        P(("dp", "fsdp")),
        P(),
    )
    return jax.shard_map(
        per_device,
        mesh=mesh,
        in_specs=placed,
        out_specs=(
            P("dp", "fsdp", None),
            P("dp", "fsdp", None),
            P("dp", "fsdp", None, None),
            P(("dp", "fsdp"), None),
            P(("dp", "fsdp"), None),
            P(("dp", "fsdp")),
            P(),
        ),
        check_vma=False,
    )
```

```python
import functools

import jax
import jax.numpy as jnp
from jax import lax
from jax.experimental import pallas as pl
from jax.experimental.pallas import tpu as pltpu
from jax.sharding import PartitionSpec as P

FF = 3584
SPAN = 64
PIECE = 256

relative_bucket_limits = (1, 2, 3, 4, 5, 6, 7, 8, 12, 16, 24, 32, 64, 128, 256)
norm_eps = 1e-06
gelu_scale = 0.7978845608028654
gelu_cubic = 0.044715
masked_score = -1e30
F32 = jnp.float32
BF16 = jnp.bfloat16
AXES = ("dp", "fsdp")
MESH = pl.DeviceIdType.MESH


def layout_of(sizes):
    dp, fsdp = sizes
    known = {
        (8, 4): (("fsdp", 1, 2), ("fsdp", 2, 2), ("dp", 1, 2), ("dp", 2, 4)),
        (64, 4): (("dp", 1, 2), ("fsdp", 1, 4), ("dp", 2, 8), ("dp", 16, 4)),
    }
    if sizes in known:
        return known[sizes]
    if fsdp % 2 == 0:
        return (("fsdp", 1, 2), ("fsdp", 2, fsdp // 2), ("dp", 1, 1), ("dp", 1, dp))
    return (("dp", 1, 2), ("fsdp", 1, fsdp), ("dp", 2, 1), ("dp", 2, dp // 2))


def pick(values, index):
    total = jnp.int32(values[0])
    for i in range(1, len(values)):
        total = jnp.where(index == i, jnp.int32(values[i]), total)
    return total


def by_distance(position, places, k):
    table = [sorted(range(places), key=lambda q, p=p: (abs(q - p), q))[k] for p in range(places)]
    return pick(table, position)


class Place:
    def __init__(self, layout):
        self.layout = layout
        self.core_dim, self.y_dim, self.x_dim, self.z_dim = layout
        self.swaps = self.x_dim[2] == self.y_dim[2]
        self.index = {axis: lax.axis_index(axis).astype(jnp.int32) for axis in AXES}
        where = [(self.index[axis] // step) % places for axis, step, places in layout]
        self.core, self.y, self.x, self.z = where
        self.a, self.b = self.roles(self.core, self.x, self.y)
        self.na, self.nb, self.nz = self.x_dim[2], self.y_dim[2], self.z_dim[2]
        self.cores = self.core_dim[2]

    def roles(self, core, first, second):
        if not self.swaps:
            return first, second
        return first + core * (second - first), second + core * (first - second)

    def coords(self, core, z, a, b):
        x, y = self.roles(core, a, b)
        total = {axis: jnp.int32(0) for axis in AXES}
        for (axis, step, _), at in zip(self.layout, (core, y, x, z), strict=True):
            total[axis] = total[axis] + at * step
        return total

    def device(self, core=None, z=None, a=None, b=None, roles_of=None):
        core_at = self.core if core is None else core
        if core is not None and roles_of is None:
            x, y = self.x, self.y
            total = {axis: jnp.int32(0) for axis in AXES}
            for (axis, step, _), at in zip(self.layout, (core_at, y, x, self.z), strict=True):
                total[axis] = total[axis] + at * step
            return total
        return self.coords(
            core_at, self.z if z is None else z, self.a if a is None else a, self.b if b is None else b
        )

    def block(self, core, z, a, b):
        at = self.coords(core, z, a, b)
        return at["dp"] * lax.axis_size("fsdp") + at["fsdp"]

    def neighbours(self):
        found = []
        for name, places in (("z", self.nz), ("a", self.na), ("b", self.nb)):
            at = getattr(self, name)
            for move in (-1, 1):
                if places == 1:
                    continue
                if places == 2:
                    if move == 1:
                        found.append((None, self.device(**{name: 1 - at})))
                    continue
                found.append(((at + move >= 0) & (at + move < places), self.device(**{name: at + move})))
        if self.cores == 2:
            found.append((None, self.device(core=1 - self.core)))
        return found


def when(condition, action):
    if condition is None:
        action()
    else:
        pl.when(condition)(action)


def meet(place, others=()):
    barrier = pltpu.get_barrier_semaphore()
    count = jnp.int32(0)
    for condition, device in place.neighbours() + [(None, other) for other in others]:
        when(
            condition,
            lambda device=device: pl.semaphore_signal(barrier, inc=1, device_id=device, device_id_type=MESH),
        )
        count = count + (1 if condition is None else condition.astype(jnp.int32))
    pl.semaphore_wait(barrier, count)


def part_of(ref, block, size):
    if size is None:
        return ref.at[block]
    return ref.at[pl.ds(pl.multiple_of(block * size, size), size)]


def gather_steps(layout, arrays, side_work):
    place = Place(layout)
    meet(place)
    sent = []
    a, b, z, core = place.a, place.b, place.z, place.core
    sibling = place.device(core=1 - core)

    def send(block, kind, slot, device, condition, own):
        for x_ref, out_ref, size, send_sem, recv_sem, _ in arrays:
            copy = pltpu.make_async_remote_copy(
                src_ref=x_ref if own else part_of(out_ref, block, size),
                dst_ref=part_of(out_ref, block, size),
                send_sem=send_sem.at[kind, slot],
                recv_sem=recv_sem.at[block],
                device_id=device,
                device_id_type=MESH,
            )
            when(condition, copy.start)
            sent.append((condition, copy))

    def arrived(block):
        for x_ref, out_ref, size, send_sem, recv_sem, _ in arrays:
            pltpu.make_async_remote_copy(
                src_ref=x_ref, dst_ref=part_of(out_ref, block, size), send_sem=send_sem.at[0, 0], recv_sem=recv_sem.at[block],
                device_id=sibling, device_id_type=MESH,
            ).wait_recv()

    def along(name, at, places, block, slot, origin, kinds, own=False):
        if places == 1:
            return
        if places == 2:
            if origin is None:
                send(block, kinds[0], slot, place.device(**{name: 1 - at}), None, own)
            return
        if origin is None:
            for move, kind in ((-1, kinds[0]), (1, kinds[1])):
                inside = (at + move >= 0) & (at + move < places)
                send(block, kind, slot, place.device(**{name: at + move}), inside, own)
            return
        move = jnp.where(origin < at, 1, -1)
        inside = (at + move >= 0) & (at + move < places)
        send(block, kinds[0], slot, place.device(**{name: at + move}), inside, own)

    mine = place.block(core, z, a, b)
    keeps = []
    slot = 0
    along("z", z, place.nz, mine, slot, None, (0, 1), True)
    along("a", a, place.na, mine, slot, None, (2, 3), True)
    along("b", b, place.nb, mine, slot, None, (4, 5), True)
    if place.cores == 2:
        send(mine, 6, slot, sibling, None, True)
    for x_ref, out_ref, size, _, _, own_sem in arrays:
        keep = pltpu.make_async_copy(x_ref, part_of(out_ref, mine, size), own_sem)
        keep.start()
        keeps.append(keep)
    visits = []
    for kz in range(place.nz):
        visits.append((kz, 0, 0))
        if kz:
            visits += [(kz - 1, ka, 0) for ka in range(1, place.na)]
    visits += [(place.nz - 1, ka, 0) for ka in range(1, place.na)]
    visits += [(kz, ka, kb) for kb in range(1, place.nb) for ka in range(place.na) for kz in range(place.nz)]
    side_work = list(side_work)
    for kz, ka, kb in visits[1:]:
        if side_work:
            side_work.pop(0)()
        slot += 1
        zb, ab, bb = by_distance(z, place.nz, kz), by_distance(a, place.na, ka), by_distance(b, place.nb, kb)
        block = place.block(core, zb, ab, bb)
        arrived(block)
        if kb == 0 and ka == 0:
            along("z", z, place.nz, block, slot, zb, (0, 1))
        if kb == 0:
            along("a", a, place.na, block, slot, None if ka == 0 else ab, (2, 3))
        along("b", b, place.nb, block, slot, None if kb == 0 else bb, (4, 5))
        if place.cores == 2:
            send(block, 6, slot, sibling, None, False)
    for action in side_work:
        action()
    if place.cores == 2:
        for bb in range(place.nb):
            for ab in range(place.na):
                for zb in range(place.nz):
                    arrived(place.block(1 - core, jnp.int32(zb), jnp.int32(ab), jnp.int32(bb)))
    for condition, copy in sent:
        when(condition, copy.wait_send)
    for keep in keeps:
        keep.wait()


def gather_with_tiles(layout, blocks, lines, rows):
    n = 1
    for _, _, places in layout:
        n *= places
    per_core = n // layout[0][2]
    count = len(blocks)
    heads, reach_count, _, width = lines.shape
    sizes = [block.shape[0] if block.shape[0] % 16 == 0 else None for block in blocks]

    def body(*refs):
        xs, line_ref, outs, tile_ref = refs[:count], refs[count], refs[count + 1 : 2 * count + 1], refs[2 * count + 1]
        tile_buf, tile_sem = refs[2 * count + 2 : 2 * count + 4]
        sems = refs[2 * count + 4 :]
        arrays = [(xs[i], outs[i], sizes[i], *sems[3 * i : 3 * i + 3]) for i in range(count)]

        def tile_copy(h):
            return pltpu.make_async_copy(tile_buf.at[h], tile_ref.at[h], tile_sem.at[h])

        def spread(h):
            for d in range(reach_count):
                wide = jnp.broadcast_to(line_ref[h, d], (rows, width))
                tile_buf[h, d] = pltpu.roll(wide, 0, 1, stride=1, stride_axis=0)[:, :rows]
            tile_copy(h).start()

        gather_steps(layout, arrays, [functools.partial(spread, h) for h in range(heads)])
        for h in range(heads):
            tile_copy(h).wait()

    scratch = [pltpu.VMEM((heads, reach_count, rows, rows), F32), pltpu.SemaphoreType.DMA((heads,))]
    for _ in blocks:
        scratch += [pltpu.SemaphoreType.DMA((7, per_core)), pltpu.SemaphoreType.DMA((n,)), pltpu.SemaphoreType.DMA]
    anywhere = pl.BlockSpec(memory_space=pl.ANY)
    inside = pl.BlockSpec(memory_space=pltpu.VMEM)
    *gathered, tiles = pl.pallas_call(
        body,
        out_shape=[
            jax.ShapeDtypeStruct((n,) + block.shape if size is None else (n * size,) + block.shape[1:], block.dtype)
            for block, size in zip(blocks, sizes, strict=True)
        ]
        + [jax.ShapeDtypeStruct((heads, reach_count, rows, rows), F32)],
        in_specs=[inside] * (count + 1),
        out_specs=[anywhere] * (count + 1),
        scratch_shapes=scratch,
        compiler_params=pltpu.CompilerParams(collective_id=1, has_side_effects=True, vmem_limit_bytes=60_000_000),
        name="gather_all",
    )(*blocks, lines)
    return gathered, tiles


class Reduction:
    def __init__(self, place, source, size, lanes, buffers):
        self.place, self.source, self.size, self.lanes = place, source, size, lanes
        self.own, self.sib, line_b, line_a, line_z, self.load_sem, self.send_sem, self.sib_sem, sem_b, sem_a, sem_z = buffers
        self.lines = {"b": (line_b, sem_b), "a": (line_a, sem_a), "z": (line_z, sem_z)}
        self.order = [by_distance(place.z, place.nz, k) for k in reversed(range(place.nz))]
        self.sibling = place.device(core=1 - place.core)

    def slot(self, zb, ab, bb):
        return (zb * self.place.na + ab) * self.place.nb + bb

    def piece(self, core, zb, ab, bb):
        block = self.place.block(core, zb, ab, bb)
        if self.size is None:
            return self.source.at[block, :, pl.ds(*self.lanes)]
        return self.source.at[pl.ds(pl.multiple_of(block * self.size, self.size), self.size), pl.ds(*self.lanes)]

    def remote(self, src, dst, send_sem, recv_sem, device):
        return pltpu.make_async_remote_copy(
            src_ref=src, dst_ref=dst, send_sem=send_sem, recv_sem=recv_sem, device_id=device, device_id_type=MESH
        )

    def inner(self, a_at, b_at):
        place = self.place
        return [
            (by_distance(a_at, place.na, ka), by_distance(b_at, place.nb, kb))
            for kb in reversed(range(place.nb))
            for ka in reversed(range(place.na))
        ]

    def open(self, i):
        place, zb = self.place, self.order[i]
        their_a, their_b = (place.b, place.a) if place.swaps else (place.a, place.b)
        for (ao, bo), (at, bt) in zip(self.inner(place.a, place.b), self.inner(their_a, their_b), strict=True):
            slot = self.slot(zb, ao, bo)
            pltpu.make_async_copy(self.piece(place.core, zb, ao, bo), self.own.at[slot], self.load_sem.at[slot]).start()
            slot = self.slot(zb, at, bt)
            copy = self.remote(
                self.piece(1 - place.core, zb, at, bt), self.sib.at[slot], self.send_sem.at[0, slot], self.sib_sem.at[slot], self.sibling
            )
            copy.start()

    def add(self, slot, buffer, sem, at):
        self.remote(self.own.at[slot], buffer.at[at], self.send_sem.at[1, slot], sem.at[at], self.sibling).wait_recv()
        self.own[slot] = (self.own[slot].astype(F32) + buffer[at].astype(F32)).astype(self.own.dtype)

    def both_cores(self, zb, ab, bb):
        slot = self.slot(zb, ab, bb)
        pltpu.make_async_copy(self.piece(self.place.core, zb, ab, bb), self.own.at[slot], self.load_sem.at[slot]).wait()
        self.add(slot, self.sib, self.sib_sem, slot)

    def pass_on(self, name, at, places, target, inner, inner_count, slot, condition=None):
        line, sem = self.lines[name]
        move = jnp.where(target > at, 1, -1)
        if places == 2:
            there = inner
        else:
            outer = (at - move >= 0) & (at - move < places)
            if condition is not None:
                outer = outer & condition
            pl.when(outer)(lambda: self.add(slot, line, sem, target * inner_count + inner))
            there = jnp.where((target == at + move) & (move < 0), places, target) * inner_count + inner
        device = self.place.device(**{name: at + move})
        copy = self.remote(self.own.at[slot], line.at[there], self.send_sem.at[1, slot], sem.at[there], device)
        when(condition, copy.start)

    def take_in(self, name, at, places, inner, inner_count, slot, condition=None):
        line, sem = self.lines[name]
        if places == 1:
            return
        if places == 2:
            when(condition, lambda: self.add(slot, line, sem, inner))
            return
        lower, upper = at > 0, at < places - 1
        if condition is not None:
            lower, upper = lower & condition, upper & condition
        pl.when(lower)(lambda: self.add(slot, line, sem, at * inner_count + inner))
        pl.when(upper)(lambda: self.add(slot, line, sem, places * inner_count + inner))

    def first(self, i):
        place, zb = self.place, self.order[i]
        for kb in reversed(range(1, place.nb)):
            bb = by_distance(place.b, place.nb, kb)
            for ka in reversed(range(place.na)):
                ab = by_distance(place.a, place.na, ka)
                self.both_cores(zb, ab, bb)
                inner, count = zb * place.na + ab, place.nz * place.na
                self.pass_on("b", place.b, place.nb, bb, inner, count, self.slot(zb, ab, bb))
        for ka in reversed(range(place.na)):
            self.both_cores(zb, by_distance(place.a, place.na, ka), place.b)

    def second(self, i):
        place, zb = self.place, self.order[i]
        for ka in reversed(range(place.na)):
            ab = by_distance(place.a, place.na, ka)
            slot = self.slot(zb, ab, place.b)
            self.take_in("b", place.b, place.nb, zb * place.na + ab, place.nz * place.na, slot)
            if ka:
                self.pass_on("a", place.a, place.na, ab, zb, place.nz, slot)

    def third(self, i):
        place, zb = self.place, self.order[i]
        slot = self.slot(zb, place.a, place.b)
        self.take_in("a", place.a, place.na, zb, place.nz, slot)
        if i < place.nz - 1:
            self.pass_on("z", place.z, place.nz, zb, 0, 1, slot)

    def last(self, out_ref):
        place = self.place
        slot = self.slot(place.z, place.a, place.b)
        self.take_in("z", place.z, place.nz, 0, 1, slot)
        out_ref[...] = self.own[slot].astype(F32)

    def actions(self):
        n = self.place.nz
        found = []
        for i in range(n + 2):
            for step, back in ((self.first, 0), (self.second, 1), (self.third, 2)):
                if 0 <= i - back < n:
                    found.append(functools.partial(step, i - back))
        return found

    def drain(self):
        place = self.place
        mine = self.slot(place.z, place.a, place.b)
        for slot in range(place.nz * place.na * place.nb):
            for kind in range(2):
                copy = self.remote(self.sib.at[slot], self.sib.at[slot], self.send_sem.at[kind, slot], self.sib_sem.at[slot], self.sibling)
                when(None if kind == 0 else mine != slot, copy.wait_send)


def reduction_scratch(layout, block_shape, dtype):
    _, (_, _, nb), (_, _, na), (_, _, nz) = layout
    deep = lambda places: 1 if places <= 2 else places + 1
    vm = lambda *lead: pltpu.VMEM(lead + block_shape, dtype)
    dma = pltpu.SemaphoreType.DMA
    per_core = nz * na * nb
    counts = {"b": deep(nb) * nz * na, "a": deep(na) * nz, "z": deep(nz)}
    return [
        vm(per_core), vm(per_core), vm(counts["b"]), vm(counts["a"]), vm(counts["z"]),
        dma((per_core,)), dma((2, per_core)),
        dma((per_core,)), dma((counts["b"],)), dma((counts["a"],)), dma((counts["z"],)),
    ]


BUFFERS = 11


def row_tiles(rows):
    return rows if rows % 16 == 0 else None


def projection_grads(every, grad_keys, grad_values, pairs, near_grads, share):
    width = every.shape[1]
    rows = pairs[0][0].shape[0]
    tall = 2 * rows if every.shape[0] % (2 * rows) == 0 else rows
    many = every.shape[0] // tall
    order = [(7, 1), (4, 1), (3, 1), (5, 1), (6, 1), (0, 1), (1, many), (2, many)]
    matrix_of, start_of = [], {}
    for matrix, count in order:
        start_of[matrix] = len(matrix_of)
        matrix_of += [matrix] * count
    steps = len(matrix_of)

    def body(table_ref, every_ref, gk_ref, gv_ref, l0, r0, l1, r1, l2, r2, l3, r3, n5, n6, out_ref, acc_ref):
        step = pl.program_id(0)
        sources = {0: (l0, r0), 3: (l1, r1), 4: (l2, r2), 7: (l3, r3), 1: (every_ref, gk_ref), 2: (every_ref, gv_ref)}
        for matrix, count in order:
            start = start_of[matrix]
            if matrix in (5, 6):

                @pl.when(step == start)
                def _(near_ref=n5 if matrix == 5 else n6):
                    out_ref[0] = near_ref[...]

                continue
            left, right = sources[matrix]

            @pl.when((step >= start) & (step < start + count))
            def _(left=left, right=right, start=start, count=count):
                if count == 1:
                    out_ref[0] = transposed_times(left[...], right[...]).astype(BF16)
                    return
                term = transposed_times(left[...], right[...])

                @pl.when(step == start)
                def _():
                    acc_ref[...] = term

                @pl.when(step > start)
                def _():
                    acc_ref[...] += term

                @pl.when(step == start + count - 1)
                def _():
                    out_ref[0] = acc_ref[...].astype(BF16)

    def chunk(start):
        return pl.BlockSpec((tall, width), lambda i, _: (jnp.clip(i - start, 0, many - 1), 0))

    both = pl.BlockSpec(
        (tall, width), lambda i, _: (jnp.clip(jnp.where(i < start_of[2], i - start_of[1], i - start_of[2]), 0, many - 1), 0)
    )
    square = pl.BlockSpec((width, width), lambda i, _: (0, 0))
    in_specs = [both, chunk(start_of[1]), chunk(start_of[2])] + [pl.BlockSpec((rows, width), lambda i, _: (0, 0))] * 8
    return pl.pallas_call(
        body,
        grid_spec=pltpu.PrefetchScalarGridSpec(
            num_scalar_prefetch=1,
            grid=(steps,),
            in_specs=in_specs + [square, square],
            out_specs=pl.BlockSpec((1, width, width), lambda i, table: (table[i], 0, 0)),
            scratch_shapes=[pltpu.VMEM((width, width), F32)],
        ),
        out_shape=jax.ShapeDtypeStruct((8, width, width), BF16),
        cost_estimate=pl.CostEstimate(
            flops=2 * width * width * (2 * every.shape[0] + 4 * pairs[0][0].shape[0]), transcendentals=0, bytes_accessed=40_000_000
        ),
        compiler_params=pltpu.CompilerParams(vmem_limit_bytes=50_000_000),
        name="projection_grads",
    )(jnp.asarray(matrix_of, jnp.int32), every, grad_keys, grad_values, *[side for pair in pairs for side in pair], *near_grads)


def last_steps(layout, sizes, matrix_grads, share, lines, grad_queries, query_matrix, joined, hidden, gain, grad_first):
    tokens, width = grad_queries.shape
    bits = lambda count: [1 << i for i in range(count.bit_length() - 1)]
    rounds = [("fsdp", step) for step in bits(sizes[1])] + [("dp", step) for step in bits(sizes[0])]
    given = [line for line in lines if line is not None]
    per_gain = width // 128
    total_rows = sum(per_gain if line is None else line.shape[0] for line in lines)
    held_rows = -(-total_rows // 8) * 8

    def body(*refs):
        (mats_ref, dq_ref, m0_ref, in_ref, hid_ref, gf_ref, gain_ref), refs = refs[:7], refs[7:]
        line_refs, refs = list(refs[: len(given)]), refs[len(given) :]
        (attn_ref, sum_ref, hg_ref), refs = refs[:3], refs[3:]
        (q_buf, m0, in_buf, hid_buf, first_buf, load_sem), refs = refs[:6], refs[6:]
        (line_out, line_in, line_send, line_recv), buffers = refs[:4], refs[4:]
        place = Place(layout)
        index = {axis: lax.axis_index(axis).astype(jnp.int32) for axis in AXES}
        across = lambda axis, step: {axis: index[axis] + step * (1 - 2 * ((index[axis] // step) % 2))}
        meet(place, [across(axis, step) for axis, step in rounds])
        loads = [
            pltpu.make_async_copy(src, dst, load_sem.at[i])
            for i, (src, dst) in enumerate(
                ((dq_ref, q_buf), (m0_ref.at[0], m0), (in_ref, in_buf), (hid_ref, hid_buf), (gf_ref, first_buf))
            )
        ]
        big = Reduction(place, mats_ref, row_tiles(share), (0, width), buffers)
        for i in range(place.nz):
            big.open(i)
            if i == 0:
                for load in loads:
                    load.start()
        actions = big.actions()
        actions.pop(0)()
        for load in loads:
            load.wait()
        piece = tokens // 4

        def finish(i, total):
            rows = pl.ds(pl.multiple_of(i * piece, piece), piece)
            held = hid_buf[rows, :].astype(F32)
            scale = inverse_rms(held)
            grad = dot_t(q_buf[rows, :], m0[...]) + in_buf[rows, :]
            hg_ref[rows, :] = first_buf[rows, :] + norm_back(held, scale, gain_ref[...], grad)
            return total + jnp.sum(grad * held * scale, axis=0, keepdims=True)

        gain_grad = lax.fori_loop(0, 4, finish, jnp.zeros((1, width), F32))
        at = 0
        for line in lines:
            if line is None:
                for i in range(per_gain):
                    sum_ref[at + i : at + i + 1, :] = gain_grad[:, i * 128 : (i + 1) * 128]
                at += per_gain
            else:
                ref = line_refs.pop(0)
                sum_ref[at : at + ref.shape[0], :] = ref[...]
                at += ref.shape[0]
        if at < held_rows:
            sum_ref[at:, :] = jnp.zeros((held_rows - at, 128), F32)

        def round_copy(i):
            axis, step = rounds[i]
            return pltpu.make_async_remote_copy(
                src_ref=line_out.at[i], dst_ref=line_in.at[i], send_sem=line_send.at[i], recv_sem=line_recv.at[i],
                device_id=across(axis, step), device_id_type=MESH,
            )

        for i in range(len(rounds)):
            line_out[i] = sum_ref[...]
            round_copy(i).start()
            for _ in range(2):
                if actions:
                    actions.pop(0)()
            round_copy(i).wait_recv()
            sum_ref[...] += line_in[i]
        for action in actions:
            action()
        big.last(attn_ref)
        for i in range(len(rounds)):
            round_copy(i).wait_send()
        big.drain()

    anywhere = pl.BlockSpec(memory_space=pl.ANY)
    inside = pl.BlockSpec(memory_space=pltpu.VMEM)
    block = (share, width)
    dma = pltpu.SemaphoreType.DMA
    scratch = [
        pltpu.VMEM(grad_queries.shape, BF16), pltpu.VMEM((width, width), BF16), pltpu.VMEM(joined.shape, joined.dtype),
        pltpu.VMEM(hidden.shape, hidden.dtype), pltpu.VMEM(grad_first.shape, F32), dma((5,)),
        pltpu.VMEM((len(rounds), held_rows, 128), F32), pltpu.VMEM((len(rounds), held_rows, 128), F32),
        dma((len(rounds),)), dma((len(rounds),)),
    ]
    scratch += reduction_scratch(layout, block, BF16)
    return pl.pallas_call(
        body,
        out_shape=[
            jax.ShapeDtypeStruct(block, F32),
            jax.ShapeDtypeStruct((held_rows, 128), F32),
            jax.ShapeDtypeStruct((tokens, width), F32),
        ],
        in_specs=[anywhere] * 6 + [inside] * (1 + len(given)),
        out_specs=[inside] * 3,
        scratch_shapes=scratch,
        compiler_params=pltpu.CompilerParams(collective_id=2, has_side_effects=True, vmem_limit_bytes=50_000_000),
        name="last_steps",
    )(matrix_grads, grad_queries, query_matrix, joined, hidden, grad_first, gain.reshape(1, width), *given)


def from_behind(array, axis, by):
    length = lax.axis_size(axis)
    pairs = [(i, i + by) for i in range(length) if 0 <= i + by < length]
    return lax.ppermute(array, axis, pairs)


def sum_of_group(parts, place):
    group = parts.shape[0]
    if group & (group - 1):
        return lax.psum_scatter(parts, "fsdp", scatter_dimension=0, tiled=True)[0].astype(F32)
    step = 1
    while step < group:
        halves = parts.reshape((parts.shape[0] // 2, 2) + parts.shape[1:])
        bit = (place // step) % 2
        away = lax.dynamic_index_in_dim(halves, 1 - bit, axis=1, keepdims=False)
        kept = lax.dynamic_index_in_dim(halves, bit, axis=1, keepdims=False)
        came = lax.ppermute(away, "fsdp", [(i, i ^ step) for i in range(group)])
        parts = kept.astype(F32) + came.astype(F32)
        step *= 2
        if step < group:
            parts = parts.astype(BF16)
    return parts[0]


def product(left_side, right_side):
    return jnp.dot(left_side, right_side, preferred_element_type=F32)


def times_transposed(left_side, right_side):
    return lax.dot_general(left_side, right_side, (((1,), (1,)), ((), ())), preferred_element_type=F32)


def transposed_times(left_side, right_side):
    return lax.dot_general(left_side, right_side, (((0,), (0,)), ((), ())), preferred_element_type=F32)


def inverse_rms(residual):
    return lax.rsqrt(jnp.mean(residual * residual, axis=-1, keepdims=True) + norm_eps)


def norm_back(residual, scale, gain, incoming):
    weighted = gain * incoming
    return scale * weighted - residual * scale * scale * scale * jnp.mean(
        residual * weighted, axis=-1, keepdims=True
    )


def gelu_parts(values):
    tangent = jnp.tanh(gelu_scale * (values + gelu_cubic * values * values * values))
    result = 0.5 * values * (1.0 + tangent)
    slope = 0.5 * (1.0 + tangent) + 0.5 * values * (1.0 - tangent * tangent) * gelu_scale * (
        1.0 + 3.0 * gelu_cubic * values * values
    )
    return (result, slope)


def bucket_of(offset):
    magnitude = jnp.abs(offset)
    counted = jnp.zeros(offset.shape, jnp.int32)
    for threshold in relative_bucket_limits:
        counted = counted + (magnitude >= threshold).astype(jnp.int32)
    return counted + (offset > 0).astype(jnp.int32) * (len(relative_bucket_limits) + 1)


def piece_labels(positions, starts):
    inside = (positions[None, :, None] >= starts[:, None, :]) & (
        positions[None, :, None] < starts[:, None, :] + PIECE
    )
    labels = jnp.arange(1, starts.shape[1] + 1, dtype=jnp.int32)
    return jnp.sum(jnp.where(inside, labels[None, None, :], 0), axis=2)


def dot_t(left_side, right_side):
    return lax.dot_general(left_side, right_side, (((1,), (1,)), ((), ())), preferred_element_type=F32)


def own_lanes(values, which, width):
    lane = lax.broadcasted_iota(jnp.int32, values.shape, 1)
    return jnp.where((lane >= which * width) & (lane < (which + 1) * width), values, jnp.zeros_like(values))


def flipped(values):
    return values.astype(F32).T.astype(BF16)


def bias_lines(rel_table, rows, reach):
    heads = rel_table.shape[1]
    width = 2 * rows
    count = 2 * reach + 1
    shift = jnp.arange(width, dtype=jnp.int32)
    behind = jnp.where(shift < rows, shift, shift - width)
    far = (jnp.arange(count, dtype=jnp.int32) - reach) * rows
    ids = bucket_of(far[:, None] - behind[None, :])
    hot = (ids[:, :, None] == jnp.arange(rel_table.shape[0], dtype=jnp.int32)).astype(F32)
    lines = jnp.einsum("dwb,bh->hdw", hot, rel_table, precision=lax.Precision.HIGHEST)
    return lines.reshape(heads, count, 1, width)


def tile_at(block, place, reach):
    return jnp.clip(block - place, -reach, reach) + reach


def self_attention(place, query, keys, values, tiles, hidden_mask, head_size, reach):
    count, rows, width = query.shape
    blocks = keys.shape[0]
    pair = 128
    per = pair // head_size

    def body(place_ref, q_ref, k_ref, v_ref, tile_ref, mask_ref, o_ref, ot_ref, lse_ref, s_ref, p_ref):
        for b in range(count):
            scaled = q_ref[b] * jnp.asarray(0.125, BF16)
            value_t = jnp.concatenate([flipped(v_ref[j, b]) for j in range(blocks)], axis=1)
            for h in range(per):
                mine = own_lanes(scaled, h, head_size)
                top = jnp.full((1, rows), -jnp.inf, F32)
                for j in range(blocks):
                    s = dot_t(k_ref[j, b], mine)
                    s = s + tile_ref[h, tile_at(j, place_ref[0], reach)] + mask_ref[b, j]
                    s_ref[j] = s
                    top = jnp.maximum(top, jnp.max(s, axis=0, keepdims=True))
                total = jnp.zeros((1, rows), F32)
                for j in range(blocks):
                    p = jnp.exp(s_ref[j] - top)
                    total = total + jnp.sum(p, axis=0, keepdims=True)
                    p_ref[j * rows : (j + 1) * rows, :] = p.astype(BF16)
                part = product(value_t[h * head_size : (h + 1) * head_size], p_ref[...]) / total
                ot_ref[0, b, h * head_size : (h + 1) * head_size, :] = part
                lse_ref[0, b * per + h : b * per + h + 1, :] = top + jnp.log(total)
            o_ref[b] = ot_ref[0, b].T.astype(BF16)

    steps = width // pair
    grid_spec = pltpu.PrefetchScalarGridSpec(
        num_scalar_prefetch=1,
        grid=(steps,),
        in_specs=[
            pl.BlockSpec((count, rows, pair), lambda i, _: (0, 0, i)),
            pl.BlockSpec((blocks, count, rows, pair), lambda i, _: (0, 0, 0, i)),
            pl.BlockSpec((blocks, count, rows, pair), lambda i, _: (0, 0, 0, i)),
            pl.BlockSpec((per,) + tiles.shape[1:], lambda i, _: (i, 0, 0, 0)),
            pl.BlockSpec(hidden_mask.shape, lambda i, _: (0, 0, 0, 0)),
        ],
        out_specs=[
            pl.BlockSpec((count, rows, pair), lambda i, _: (0, 0, i)),
            pl.BlockSpec((1, count, pair, rows), lambda i, _: (i, 0, 0, 0)),
            pl.BlockSpec((1, count * per, rows), lambda i, _: (i, 0, 0)),
        ],
        scratch_shapes=[
            pltpu.VMEM((blocks, rows, rows), F32),
            pltpu.VMEM((blocks * rows, rows), BF16),
        ],
    )
    cost = 4 * count * blocks * rows * rows * width
    return pl.pallas_call(
        body,
        grid_spec=grid_spec,
        out_shape=[
            jax.ShapeDtypeStruct((count, rows, width), BF16),
            jax.ShapeDtypeStruct((steps, count, pair, rows), F32),
            jax.ShapeDtypeStruct((steps, count * per, rows), F32),
        ],
        cost_estimate=pl.CostEstimate(flops=4 * cost, transcendentals=0, bytes_accessed=30_000_000),
        name="self_attention",
    )(place, query, keys, values, tiles, hidden_mask)


def self_attention_back(place, query, keys, values, tiles, hidden_mask, outer_t, lse, grad, head_size, reach):
    count, rows, width = query.shape
    blocks = keys.shape[0]
    pair = 128
    per = pair // head_size
    half = rows // 2

    def body(
        place_ref, q_ref, k_ref, v_ref, tile_ref, mask_ref, ot_ref, lse_ref, do_ref,
        dq_ref, dk_ref, dv_ref, sum_ref, acc_ref, dk_acc, dv_acc,
    ):
        for b in range(count):
            scaled = q_ref[b] * jnp.asarray(0.125, BF16)
            incoming = do_ref[b]
            key_t = jnp.concatenate([flipped(k_ref[j, b]) for j in range(blocks)], axis=1)
            weighed = incoming.astype(F32).T * ot_ref[0, b]
            query_parts = []
            for h in range(per):
                lanes = slice(h * head_size, (h + 1) * head_size)
                mine = own_lanes(scaled, h, head_size)
                theirs = own_lanes(incoming, h, head_size)
                delta = jnp.sum(weighed[lanes], axis=0, keepdims=True)
                level = lse_ref[0, b * per + h : b * per + h + 1, :]
                part = jnp.zeros((head_size, rows), F32)
                for j in range(blocks):
                    s = dot_t(k_ref[j, b], mine)
                    s = s + tile_ref[h, tile_at(j, place_ref[0], reach)] + mask_ref[b, j]
                    p = jnp.exp(s - level)
                    ds = p * (dot_t(v_ref[j, b], theirs) - delta)
                    p_low = p.astype(BF16)
                    ds_low = ds.astype(BF16)
                    dv = product(p_low, theirs)
                    dk = product(ds_low, mine)
                    if h == 0:
                        dv_acc[j] = dv
                        dk_acc[j] = dk
                    else:
                        dv_ref[j, b] = (dv_acc[j] + dv).astype(BF16)
                        dk_ref[j, b] = (dk_acc[j] + dk).astype(BF16)
                    part = part + product(key_t[lanes, j * rows : (j + 1) * rows], ds_low)
                    if b == 0:
                        acc_ref[h, j] = ds
                    else:
                        acc_ref[h, j] = acc_ref[h, j] + ds
                query_parts.append(part)
            dq_ref[b] = (jnp.concatenate(query_parts, axis=0) * 0.125).T.astype(BF16)
        for h in range(per):
            for j in range(blocks):
                upper, lower = acc_ref[h, j, :half, :], acc_ref[h, j, half:, :]
                folded = jnp.concatenate(
                    [lower[:, :half], lower[:, half:] + upper[:, :half], upper[:, half:], jnp.zeros((half, half), F32)],
                    axis=1,
                )
                left = half // 2
                while left >= 8:
                    folded = folded[left:] + pltpu.roll(folded[:left], left, 1)
                    left //= 2
                sum_ref[h, j] = folded

    steps = width // pair
    grid_spec = pltpu.PrefetchScalarGridSpec(
        num_scalar_prefetch=1,
        grid=(steps,),
        in_specs=[
            pl.BlockSpec((count, rows, pair), lambda i, _: (0, 0, i)),
            pl.BlockSpec((blocks, count, rows, pair), lambda i, _: (0, 0, 0, i)),
            pl.BlockSpec((blocks, count, rows, pair), lambda i, _: (0, 0, 0, i)),
            pl.BlockSpec((per,) + tiles.shape[1:], lambda i, _: (i, 0, 0, 0)),
            pl.BlockSpec(hidden_mask.shape, lambda i, _: (0, 0, 0, 0)),
            pl.BlockSpec((1, count, pair, rows), lambda i, _: (i, 0, 0, 0)),
            pl.BlockSpec((1, count * per, rows), lambda i, _: (i, 0, 0)),
            pl.BlockSpec((count, rows, pair), lambda i, _: (0, 0, i)),
        ],
        out_specs=[
            pl.BlockSpec((count, rows, pair), lambda i, _: (0, 0, i)),
            pl.BlockSpec((blocks, count, rows, pair), lambda i, _: (0, 0, 0, i)),
            pl.BlockSpec((blocks, count, rows, pair), lambda i, _: (0, 0, 0, i)),
            pl.BlockSpec((per, blocks, 8, 2 * rows), lambda i, _: (i, 0, 0, 0)),
        ],
        scratch_shapes=[
            pltpu.VMEM((per, blocks, rows, rows), F32),
            pltpu.VMEM((blocks, rows, pair), F32),
            pltpu.VMEM((blocks, rows, pair), F32),
        ],
    )
    cost = 4 * count * blocks * rows * rows * width
    return pl.pallas_call(
        body,
        grid_spec=grid_spec,
        out_shape=[
            jax.ShapeDtypeStruct((count, rows, width), BF16),
            jax.ShapeDtypeStruct((blocks, count, rows, width), BF16),
            jax.ShapeDtypeStruct((blocks, count, rows, width), BF16),
            jax.ShapeDtypeStruct((width // head_size, blocks, 8, 2 * rows), F32),
        ],
        cost_estimate=pl.CostEstimate(flops=10 * cost, transcendentals=0, bytes_accessed=40_000_000),
        name="self_attention_back",
    )(place, query, keys, values, tiles, hidden_mask, outer_t, lse, grad)


def whole(shape):
    return pl.BlockSpec(shape, lambda *_: (0,) * len(shape))


FF_TILE = 512


def feed_forward_grads(second_sum, gain, grad_out_low, weights, bias_input):
    tokens, width = second_sum.shape
    units = bias_input.shape[0]
    tile = FF_TILE
    steps = units // tile
    part = 256

    def body(sum_ref, gain_ref, go_ref, wi_ref, wo_ref, bi_ref, act_ref, gp_ref, gbi_ref, gw_ref, n_ref):
        step = pl.program_id(0)

        @pl.when(step == 0)
        def _():
            held = sum_ref[...]
            n_ref[...] = (held * inverse_rms(held) * gain_ref[...]).astype(BF16)

        normed = n_ref[...]
        incoming = go_ref[...]
        for at in range(0, tile, part):
            rows = slice(at, at + part)
            value, slope = gelu_parts(dot_t(normed, wi_ref[rows, :]) + bi_ref[0, :, rows])
            value_low = value.astype(BF16)
            grad_pre = dot_t(incoming, wo_ref[rows, :]) * slope
            bias_grad = jnp.sum(grad_pre, axis=0, keepdims=True)
            for i in range(part // 128):
                gbi_ref[0, at // 128 + i : at // 128 + i + 1, :] = bias_grad[:, i * 128 : (i + 1) * 128]
            grad_pre_low = grad_pre.astype(BF16)
            act_ref[:, rows] = value_low
            gp_ref[:, rows] = grad_pre_low
            gw_ref[0, 0, rows, :] = transposed_times(grad_pre_low, normed).astype(BF16)
            gw_ref[1, 0, rows, :] = transposed_times(value_low, incoming).astype(BF16)

    tall, line = whole((tokens, width)), whole((1, width))
    across = pl.BlockSpec((tokens, tile), lambda i: (0, i))
    return pl.pallas_call(
        body,
        grid=(steps,),
        in_specs=[
            tall, line, tall,
            pl.BlockSpec((tile, width), lambda i: (i, 0)),
            pl.BlockSpec((tile, width), lambda i: (i + steps, 0)),
            pl.BlockSpec((1, 1, tile), lambda i: (i, 0, 0)),
        ],
        out_specs=[
            across, across,
            pl.BlockSpec((1, tile // 128, 128), lambda i: (i, 0, 0)),
            pl.BlockSpec((2, 1, tile, width), lambda i: (0, i, 0, 0)),
        ],
        out_shape=[
            jax.ShapeDtypeStruct((tokens, units), BF16),
            jax.ShapeDtypeStruct((tokens, units), BF16),
            jax.ShapeDtypeStruct((steps, tile // 128, 128), F32),
            jax.ShapeDtypeStruct((2, steps, tile, width), BF16),
        ],
        scratch_shapes=[pltpu.VMEM((tokens, width), BF16)],
        cost_estimate=pl.CostEstimate(flops=8 * tokens * width * units, transcendentals=0, bytes_accessed=40_000_000),
        compiler_params=pltpu.CompilerParams(vmem_limit_bytes=50_000_000),
        name="feed_forward_grads",
    )(second_sum, gain.reshape(1, width), grad_out_low, weights, weights, bias_input.reshape(steps, 1, tile))


def feed_forward_sums(second_sum, gain, grad_out_low, weights, activated, grad_pre_low, bias_output):
    tokens, width = second_sum.shape
    tile = FF_TILE
    steps = activated.shape[1] // tile

    def body(sum_ref, gain_ref, go_ref, wi_ref, wo_ref, act_ref, gp_ref, bo_ref, out_ref, gs_ref, gg_ref, gbo_ref, acc_ref, gn_ref):
        step = pl.program_id(0)
        out_part = product(act_ref[...], wo_ref[...])
        norm_part = product(gp_ref[...], wi_ref[...])

        @pl.when(step == 0)
        def _():
            acc_ref[...] = out_part
            gn_ref[...] = norm_part

        @pl.when(step > 0)
        def _():
            acc_ref[...] += out_part
            gn_ref[...] += norm_part

        @pl.when(step == steps - 1)
        def _():
            held = sum_ref[...]
            scale = inverse_rms(held)
            out_ref[...] = (held + acc_ref[...] + bo_ref[...]).astype(BF16)
            grad_norm = gn_ref[...]
            grad_out = go_ref[...].astype(F32)
            for ref, line in (
                (gbo_ref, jnp.sum(grad_out, axis=0, keepdims=True)),
                (gg_ref, jnp.sum(grad_norm * held * scale, axis=0, keepdims=True)),
            ):
                for i in range(width // 128):
                    ref[i : i + 1, :] = line[:, i * 128 : (i + 1) * 128]
            gs_ref[...] = grad_out + norm_back(held, scale, gain_ref[...], grad_norm)

    tall, line = whole((tokens, width)), whole((1, width))
    rows_of_128 = whole((width // 128, 128))
    across = pl.BlockSpec((tokens, tile), lambda i: (0, i))
    return pl.pallas_call(
        body,
        grid=(steps,),
        in_specs=[
            tall, line, tall,
            pl.BlockSpec((tile, width), lambda i: (i, 0)),
            pl.BlockSpec((tile, width), lambda i: (i + steps, 0)),
            across, across, line,
        ],
        out_specs=[tall, tall, rows_of_128, rows_of_128],
        out_shape=[
            jax.ShapeDtypeStruct((tokens, width), BF16),
            jax.ShapeDtypeStruct((tokens, width), F32),
            jax.ShapeDtypeStruct((width // 128, 128), F32),
            jax.ShapeDtypeStruct((width // 128, 128), F32),
        ],
        scratch_shapes=[pltpu.VMEM((tokens, width), F32), pltpu.VMEM((tokens, width), F32)],
        cost_estimate=pl.CostEstimate(flops=4 * tokens * width * steps * tile, transcendentals=0, bytes_accessed=25_000_000),
        compiler_params=pltpu.CompilerParams(vmem_limit_bytes=50_000_000),
        name="feed_forward_sums",
    )(
        second_sum, gain.reshape(1, width), grad_out_low, weights, weights, activated, grad_pre_low,
        bias_output.reshape(1, width),
    )


def self_projection(place, hidden_all, gain, matrices, tokens):
    total, width = hidden_all.shape
    rows = 256
    own = tokens // rows

    def body(place_ref, hid_ref, gain_ref, m0_ref, m1_ref, m2_ref, q_ref, k_ref, v_ref, every_ref, one_ref):
        held = hid_ref[...].astype(F32)
        normed = (held * inverse_rms(held) * gain_ref[...]).astype(BF16)
        every_ref[...] = normed
        k_ref[...] = product(normed, m1_ref[0]).astype(BF16)
        v_ref[...] = product(normed, m2_ref[0]).astype(BF16)

        @pl.when(pl.program_id(0) // own == place_ref[0])
        def _():
            one_ref[...] = normed
            q_ref[...] = product(normed, m0_ref[0]).astype(BF16)

    block = pl.BlockSpec((rows, width), lambda i, _: (i, 0))
    mine = pl.BlockSpec((rows, width), lambda i, place_ref: (jnp.clip(i - place_ref[0] * own, 0, own - 1), 0))
    matrix = lambda m: pl.BlockSpec((1, width, width), lambda i, _: (m, 0, 0))
    return pl.pallas_call(
        body,
        grid_spec=pltpu.PrefetchScalarGridSpec(
            num_scalar_prefetch=1,
            grid=(total // rows,),
            in_specs=[block, pl.BlockSpec((1, width), lambda i, _: (0, 0)), matrix(0), matrix(1), matrix(2)],
            out_specs=[mine, block, block, block, mine],
        ),
        out_shape=[
            jax.ShapeDtypeStruct((tokens, width), BF16),
            jax.ShapeDtypeStruct((total, width), BF16),
            jax.ShapeDtypeStruct((total, width), BF16),
            jax.ShapeDtypeStruct((total, width), BF16),
            jax.ShapeDtypeStruct((tokens, width), BF16),
        ],
        cost_estimate=pl.CostEstimate(flops=5 * total * width * width, transcendentals=0, bytes_accessed=25_000_000),
        name="self_projection",
    )(place, hidden_all, gain.reshape(1, width), matrices, matrices, matrices)


def span_projection(near, matrices):
    blocks, rows, width = near.shape

    def body(near_ref, mk_ref, mv_ref, k_ref, v_ref):
        k_ref[0] = product(near_ref[0], mk_ref[0]).astype(BF16)
        v_ref[0] = product(near_ref[0], mv_ref[0]).astype(BF16)

    block = pl.BlockSpec((1, rows, width), lambda i: (i, 0, 0))
    return pl.pallas_call(
        body,
        grid=(blocks,),
        in_specs=[block] + [pl.BlockSpec((1, width, width), lambda i, m=m: (m, 0, 0)) for m in (5, 6)],
        out_specs=[block, block],
        out_shape=[jax.ShapeDtypeStruct(near.shape, BF16)] * 2,
        cost_estimate=pl.CostEstimate(flops=4 * blocks * rows * width * width, transcendentals=0, bytes_accessed=15_000_000),
        name="span_projection",
    )(near, matrices, matrices)


def both_heads(values, head_size):
    return jnp.concatenate([own_lanes(values, h, head_size) for h in range(128 // head_size)], axis=0)


def picked(wide, rows, head_size):
    total = own_lanes(wide[:rows], 0, head_size)
    for h in range(1, 128 // head_size):
        total = total + own_lanes(wide[h * rows : (h + 1) * rows], h, head_size)
    return total


def softmax_down(scores):
    raised = jnp.exp(scores - jnp.max(scores, axis=0, keepdims=True))
    return raised / jnp.sum(raised, axis=0, keepdims=True)


def lane_groups(width):
    return [slice(i, i + 128) for i in range(0, width, 128)]


def side_by_side(parts):
    return jnp.concatenate(parts, axis=1)


def span_attention(query, keys, values, head_size):
    blocks, rows, width = query.shape
    span_keys = keys.shape[1]

    def body(q_ref, k_ref, v_ref, o_ref):
        groups = lane_groups(width)
        scaled = q_ref[0] * jnp.asarray(0.125, BF16)
        scores = side_by_side([dot_t(k_ref[0, :, g], both_heads(scaled[:, g], head_size)) for g in groups])
        weights = softmax_down(scores).astype(BF16)
        turned = flipped(v_ref[0])
        wide = [product(turned[g], weights[:, g]).T for g in groups]
        o_ref[0] = side_by_side([picked(w, rows, head_size) for w in wide]).astype(BF16)

    q_spec = pl.BlockSpec((1, rows, width), lambda i: (i, 0, 0))
    k_spec = pl.BlockSpec((1, span_keys, width), lambda i: (i, 0, 0))
    return pl.pallas_call(
        body,
        grid=(blocks,),
        in_specs=[q_spec, k_spec, k_spec],
        out_specs=q_spec,
        out_shape=jax.ShapeDtypeStruct(query.shape, BF16),
        cost_estimate=pl.CostEstimate(flops=16 * blocks * rows * span_keys * width, transcendentals=0, bytes_accessed=12_000_000),
        name="span_attention",
    )(query, keys, values)


def span_attention_back(query, keys, values, grad, near, matrices, head_size):
    blocks, rows, width = query.shape
    span_keys = keys.shape[1]

    def body(q_ref, k_ref, v_ref, do_ref, near_ref, mk_ref, mv_ref, dq_ref, dn_ref, gk_ref, gv_ref, gk_acc, gv_acc):
        step = pl.program_id(0)
        groups = lane_groups(width)
        scaled = q_ref[0] * jnp.asarray(0.125, BF16)
        incoming = do_ref[0]
        stacked = [both_heads(scaled[:, g], head_size) for g in groups]
        theirs = [both_heads(incoming[:, g], head_size) for g in groups]
        k, v = k_ref[0], v_ref[0]
        p = softmax_down(side_by_side([dot_t(k[:, g], s) for g, s in zip(groups, stacked)]))
        dp = side_by_side([dot_t(v[:, g], t) for g, t in zip(groups, theirs)])
        ds = p * (dp - jnp.sum(p * dp, axis=0, keepdims=True))
        ds_low, p_low = ds.astype(BF16), p.astype(BF16)
        dv = side_by_side([product(p_low[:, g], t) for g, t in zip(groups, theirs)]).astype(BF16)
        dk = side_by_side([product(ds_low[:, g], s) for g, s in zip(groups, stacked)]).astype(BF16)
        turned = flipped(k)
        wide = [(product(turned[g], ds_low[:, g]) * 0.125).T for g in groups]
        dq_ref[0] = side_by_side([picked(w, rows, head_size) for w in wide]).astype(BF16)
        dn_ref[0] = dot_t(dk, mk_ref[0]) + dot_t(dv, mv_ref[0])
        near_t = flipped(near_ref[0])

        @pl.when(step == 0)
        def _():
            gk_acc[...] = product(near_t, dk)
            gv_acc[...] = product(near_t, dv)

        @pl.when(step > 0)
        def _():
            gk_acc[...] += product(near_t, dk)
            gv_acc[...] += product(near_t, dv)

        @pl.when(step == blocks - 1)
        def _():
            gk_ref[...] = gk_acc[...].astype(BF16)
            gv_ref[...] = gv_acc[...].astype(BF16)

    q_spec = pl.BlockSpec((1, rows, width), lambda i: (i, 0, 0))
    k_spec = pl.BlockSpec((1, span_keys, width), lambda i: (i, 0, 0))
    square = whole((width, width))
    return pl.pallas_call(
        body,
        grid=(blocks,),
        in_specs=[q_spec, k_spec, k_spec, q_spec, k_spec]
        + [pl.BlockSpec((1, width, width), lambda i, m=m: (m, 0, 0)) for m in (5, 6)],
        out_specs=[q_spec, k_spec, square, square],
        out_shape=[
            jax.ShapeDtypeStruct(query.shape, BF16),
            jax.ShapeDtypeStruct(keys.shape, F32),
            jax.ShapeDtypeStruct((width, width), BF16),
            jax.ShapeDtypeStruct((width, width), BF16),
        ],
        scratch_shapes=[pltpu.VMEM((width, width), F32), pltpu.VMEM((width, width), F32)],
        cost_estimate=pl.CostEstimate(flops=20 * blocks * span_keys * width * width, transcendentals=0, bytes_accessed=40_000_000),
        compiler_params=pltpu.CompilerParams(vmem_limit_bytes=50_000_000),
        name="span_attention_back",
    )(query, keys, values, grad, near, matrices, matrices)


def per_device(hidden, neighbours, piece_starts, out_grad, attn_weights, ffw_weights, vectors, rel_table):
    count, rows, width = hidden.shape
    group = lax.axis_size("fsdp")
    length = rows * group
    heads = rel_table.shape[1]
    head_size = width // heads
    buckets = rel_table.shape[0]
    spans = neighbours.shape[1]
    span_keys = neighbours.shape[2]
    carried = SPAN - 1
    kept = rows - carried
    tokens = count * rows
    reach = -(-relative_bucket_limits[-1] // rows) + 1
    place = lax.axis_index("fsdp").astype(jnp.int32)
    share = attn_weights.shape[0]

    gather = lambda array, axes: lax.all_gather(array, axes, axis=0, tiled=True)
    layout = layout_of((lax.axis_size("dp"), group))
    vector_rows = -(-vectors.shape[0] // 2048) * 16
    vector_block = jnp.pad(vectors, (0, vector_rows * 128 - vectors.shape[0])).reshape(vector_rows, 128)
    hidden_all = gather(hidden[None], "fsdp")
    (attn_full, vector_full), tiles = gather_with_tiles(
        layout, [attn_weights, vector_block], bias_lines(rel_table, rows, reach), rows
    )
    ffw_full = gather(ffw_weights, AXES)
    matrices = attn_full.reshape(8, width, width)
    vector_full = vector_full.reshape(-1, vector_rows * 128)[:, : vectors.shape[0]].reshape(-1).astype(F32)
    bias_input = vector_full[:FF]
    gains = vector_full[FF : FF + 3 * width].reshape(3, width)
    bias_output = vector_full[FF + 3 * width :]

    key_pos = jnp.arange(length, dtype=jnp.int32)
    query_pos = place * rows + jnp.arange(rows, dtype=jnp.int32)
    key_piece = piece_labels(key_pos, piece_starts)
    query_piece = piece_labels(query_pos, piece_starts)
    allowed = (key_pos[:, None] <= query_pos[None, :])[None] | (
        (key_piece[:, :, None] == query_piece[:, None, :]) & (query_piece[:, None, :] > 0)
    )
    mask = jnp.where(allowed, 0.0, masked_score).reshape(count, group, rows, rows)
    place_arg = place.reshape(1)

    residual = hidden.reshape(tokens, width).astype(F32)
    queries, keys, values, normed_every, normed_one = self_projection(
        place_arg, hidden_all.reshape(group * tokens, width), gains[0], matrices, tokens
    )
    queries = queries.reshape(count, rows, width)
    keys = keys.reshape(group, count, rows, width)
    values = values.reshape(group, count, rows, width)
    near = neighbours.reshape(count * spans, span_keys, width)
    cross_keys, cross_values = span_projection(near, matrices)
    context, context_t, lse = self_attention(
        place_arg, queries, keys, values, tiles, mask, head_size, reach
    )
    context = context.reshape(tokens, width)
    first_sum = residual + product(context, matrices[3])
    scale_two = inverse_rms(first_sum)
    normed_two = (first_sum * scale_two * gains[1]).astype(BF16)
    cross_queries = product(normed_two, matrices[4]).astype(BF16).reshape(count, rows, width)

    def ahead(array):
        incoming = from_behind(array[:, :carried], "fsdp", -1)
        return jnp.concatenate([array[:, carried:], incoming], axis=1).reshape(count * spans, SPAN, width)

    def behind(array):
        array = array.reshape(count, rows, width)
        arriving = from_behind(array[:, kept:], "fsdp", 1)
        return jnp.concatenate([arriving, array[:, :kept]], axis=1).reshape(tokens, width)

    block_queries = ahead(cross_queries)
    placed = behind(span_attention(block_queries, cross_keys, cross_values, head_size))
    second_sum = first_sum + product(placed, matrices[7])
    out_low = out_grad.reshape(tokens, width)
    activated, grad_pre_low, grad_bias_input, ffw_step = feed_forward_grads(
        second_sum, gains[2], out_low, ffw_full, bias_input
    )
    output, grad_second, grad_gain_three, grad_bias_output = feed_forward_sums(
        second_sum, gains[2], out_low, ffw_full, activated, grad_pre_low, bias_output
    )
    blocks_of = lambda array: array.reshape((-1, width) if row_tiles(share) else (-1, share, width))
    ffw_sum = lax.psum_scatter(ffw_step.reshape(2 * FF, width), AXES, scatter_dimension=0, tiled=True)
    grad_second_low = grad_second.astype(BF16)
    grad_placed = times_transposed(grad_second_low, matrices[7]).astype(BF16).reshape(count, rows, width)
    grad_block_queries, near_grad, grad_cross_key_mat, grad_cross_value_mat = span_attention_back(
        block_queries, cross_keys, cross_values, ahead(grad_placed), near, matrices, head_size
    )
    grad_cross_queries = behind(grad_block_queries)
    grad_norm_two = times_transposed(grad_cross_queries, matrices[4])
    grad_gain_two = jnp.sum(grad_norm_two * first_sum * scale_two, axis=0)
    grad_first = grad_second + norm_back(first_sum, scale_two, gains[1], grad_norm_two)
    grad_first_low = grad_first.astype(BF16)
    grad_context = times_transposed(grad_first_low, matrices[3]).astype(BF16).reshape(count, rows, width)
    grad_queries, grad_keys, grad_values, diagonal = self_attention_back(
        place_arg, queries, keys, values, tiles, mask, context_t, lse, grad_context, head_size, reach
    )
    grad_queries = grad_queries.reshape(tokens, width)
    partial_one = (
        times_transposed(grad_keys.reshape(group * tokens, width), matrices[1])
        + times_transposed(grad_values.reshape(group * tokens, width), matrices[2])
    ).astype(BF16)
    joined = sum_of_group(partial_one.reshape(group, tokens, width), place)
    matrix_step = projection_grads(
        normed_every,
        grad_keys.reshape(group * tokens, width),
        grad_values.reshape(group * tokens, width),
        [
            (normed_one, grad_queries),
            (context, grad_first_low),
            (normed_two, grad_cross_queries),
            (placed, grad_second_low),
        ],
        (grad_cross_key_mat, grad_cross_value_mat),
        share,
    )
    lane = jnp.arange(2 * rows, dtype=jnp.int32)
    line = jnp.arange(8, dtype=jnp.int32)
    block = jnp.arange(group, dtype=jnp.int32)
    between = (block[:, None, None] - place) * rows - (lane[None, None, :] - (rows - 8) - line[None, :, None])
    hot = (bucket_of(between)[..., None] == jnp.arange(buckets, dtype=jnp.int32)).astype(F32)
    table_step = jnp.einsum("hjsl,jslb->bh", diagonal, hot, precision=lax.Precision.HIGHEST)

    lines_of = lambda array: array.reshape(-1, 128)
    table_rows = -(-buckets * heads // 128)
    table_line = jnp.pad(table_step.reshape(-1), (0, table_rows * 128 - buckets * heads)).reshape(table_rows, 128)
    attn_sum, line_sum, hidden_grad = last_steps(
        layout, (lax.axis_size("dp"), group), blocks_of(matrix_step), share,
        [lines_of(grad_bias_input), None, lines_of(grad_gain_two), grad_gain_three, grad_bias_output, table_line],
        grad_queries, matrices, joined, hidden.reshape(tokens, width), gains[0], grad_first,
    )
    line_sum = line_sum.reshape(-1)
    own = vectors.shape[0]
    vector_sum = lax.dynamic_slice(line_sum, (lax.axis_index(AXES) * own,), (own,))
    table_sum = line_sum[FF + 4 * width : FF + 4 * width + buckets * heads].reshape(buckets, heads)
    return (
        output.reshape(count, rows, width),
        hidden_grad.reshape(count, rows, width),
        near_grad.reshape(count, spans, span_keys, width),
        attn_sum,
        ffw_sum.astype(F32),
        vector_sum,
        table_sum,
    )


def solution(mesh):
    placed = (
        P("dp", "fsdp", None),
        P("dp", "fsdp", None, None),
        P("dp", None),
        P("dp", "fsdp", None),
        P(("dp", "fsdp"), None),
        P(("dp", "fsdp"), None),
        P(("dp", "fsdp")),
        P(),
    )
    return jax.shard_map(
        per_device,
        mesh=mesh,
        in_specs=placed,
        out_specs=(
            P("dp", "fsdp", None),
            P("dp", "fsdp", None),
            P("dp", "fsdp", None, None),
            P(("dp", "fsdp"), None),
            P(("dp", "fsdp"), None),
            P(("dp", "fsdp")),
            P(),
        ),
        check_vma=False,
    )
```

```python
import functools

import jax
import jax.numpy as jnp
from jax import lax
from jax.experimental import pallas as pl
from jax.experimental.pallas import tpu as pltpu
from jax.sharding import PartitionSpec as P

FF = 3584
SPAN = 64
PIECE = 256

relative_bucket_limits = (1, 2, 3, 4, 5, 6, 7, 8, 12, 16, 24, 32, 64, 128, 256)
norm_eps = 1e-06
gelu_scale = 0.7978845608028654
gelu_cubic = 0.044715
masked_score = -1e30
F32 = jnp.float32
BF16 = jnp.bfloat16
AXES = ("dp", "fsdp")
MESH = pl.DeviceIdType.MESH


def layout_of(sizes):
    dp, fsdp = sizes
    known = {
        (8, 4): (("fsdp", 1, 2), ("fsdp", 2, 2), ("dp", 1, 2), ("dp", 2, 4)),
        (64, 4): (("dp", 1, 2), ("fsdp", 1, 4), ("dp", 2, 8), ("dp", 16, 4)),
    }
    if sizes in known:
        return known[sizes]
    if fsdp % 2 == 0:
        return (("fsdp", 1, 2), ("fsdp", 2, fsdp // 2), ("dp", 1, 1), ("dp", 1, dp))
    return (("dp", 1, 2), ("fsdp", 1, fsdp), ("dp", 2, 1), ("dp", 2, dp // 2))


def pick(values, index):
    total = jnp.int32(values[0])
    for i in range(1, len(values)):
        total = jnp.where(index == i, jnp.int32(values[i]), total)
    return total


def by_distance(position, places, k):
    table = [sorted(range(places), key=lambda q, p=p: (abs(q - p), q))[k] for p in range(places)]
    return pick(table, position)


class Place:
    def __init__(self, layout):
        self.layout = layout
        self.core_dim, self.y_dim, self.x_dim, self.z_dim = layout
        self.swaps = self.x_dim[2] == self.y_dim[2]
        self.index = {axis: lax.axis_index(axis).astype(jnp.int32) for axis in AXES}
        where = [(self.index[axis] // step) % places for axis, step, places in layout]
        self.core, self.y, self.x, self.z = where
        self.a, self.b = self.roles(self.core, self.x, self.y)
        self.na, self.nb, self.nz = self.x_dim[2], self.y_dim[2], self.z_dim[2]
        self.cores = self.core_dim[2]

    def roles(self, core, first, second):
        if not self.swaps:
            return first, second
        return first + core * (second - first), second + core * (first - second)

    def coords(self, core, z, a, b):
        x, y = self.roles(core, a, b)
        total = {axis: jnp.int32(0) for axis in AXES}
        for (axis, step, _), at in zip(self.layout, (core, y, x, z), strict=True):
            total[axis] = total[axis] + at * step
        return total

    def device(self, core=None, z=None, a=None, b=None, roles_of=None):
        core_at = self.core if core is None else core
        if core is not None and roles_of is None:
            x, y = self.x, self.y
            total = {axis: jnp.int32(0) for axis in AXES}
            for (axis, step, _), at in zip(self.layout, (core_at, y, x, self.z), strict=True):
                total[axis] = total[axis] + at * step
            return total
        return self.coords(
            core_at, self.z if z is None else z, self.a if a is None else a, self.b if b is None else b
        )

    def block(self, core, z, a, b):
        at = self.coords(core, z, a, b)
        return at["dp"] * lax.axis_size("fsdp") + at["fsdp"]

    def neighbours(self):
        found = []
        for name, places in (("z", self.nz), ("a", self.na), ("b", self.nb)):
            at = getattr(self, name)
            for move in (-1, 1):
                if places == 1:
                    continue
                if places == 2:
                    if move == 1:
                        found.append((None, self.device(**{name: 1 - at})))
                    continue
                found.append(((at + move >= 0) & (at + move < places), self.device(**{name: at + move})))
        if self.cores == 2:
            found.append((None, self.device(core=1 - self.core)))
        return found


def when(condition, action):
    if condition is None:
        action()
    else:
        pl.when(condition)(action)


def meet(place, others=()):
    barrier = pltpu.get_barrier_semaphore()
    count = jnp.int32(0)
    for condition, device in place.neighbours() + [(None, other) for other in others]:
        when(
            condition,
            lambda device=device: pl.semaphore_signal(barrier, inc=1, device_id=device, device_id_type=MESH),
        )
        count = count + (1 if condition is None else condition.astype(jnp.int32))
    pl.semaphore_wait(barrier, count)


def part_of(ref, block, size):
    if size is None:
        return ref.at[block]
    return ref.at[pl.ds(pl.multiple_of(block * size, size), size)]


def gather_steps(layout, arrays, side_work):
    place = Place(layout)
    meet(place)
    sent = []
    a, b, z, core = place.a, place.b, place.z, place.core
    sibling = place.device(core=1 - core)

    def send(block, kind, slot, device, condition, own):
        for x_ref, out_ref, size, send_sem, recv_sem, _ in arrays:
            copy = pltpu.make_async_remote_copy(
                src_ref=x_ref if own else part_of(out_ref, block, size),
                dst_ref=part_of(out_ref, block, size),
                send_sem=send_sem.at[kind, slot],
                recv_sem=recv_sem.at[block],
                device_id=device,
                device_id_type=MESH,
            )
            when(condition, copy.start)
            sent.append((condition, copy))

    def arrived(block):
        for x_ref, out_ref, size, send_sem, recv_sem, _ in arrays:
            pltpu.make_async_remote_copy(
                src_ref=x_ref, dst_ref=part_of(out_ref, block, size), send_sem=send_sem.at[0, 0], recv_sem=recv_sem.at[block],
                device_id=sibling, device_id_type=MESH,
            ).wait_recv()

    def along(name, at, places, block, slot, origin, kinds, own=False):
        if places == 1:
            return
        if places == 2:
            if origin is None:
                send(block, kinds[0], slot, place.device(**{name: 1 - at}), None, own)
            return
        if origin is None:
            for move, kind in ((-1, kinds[0]), (1, kinds[1])):
                inside = (at + move >= 0) & (at + move < places)
                send(block, kind, slot, place.device(**{name: at + move}), inside, own)
            return
        move = jnp.where(origin < at, 1, -1)
        inside = (at + move >= 0) & (at + move < places)
        send(block, kinds[0], slot, place.device(**{name: at + move}), inside, own)

    mine = place.block(core, z, a, b)
    keeps = []
    slot = 0
    along("z", z, place.nz, mine, slot, None, (0, 1), True)
    along("a", a, place.na, mine, slot, None, (2, 3), True)
    along("b", b, place.nb, mine, slot, None, (4, 5), True)
    if place.cores == 2:
        send(mine, 6, slot, sibling, None, True)
    for x_ref, out_ref, size, _, _, own_sem in arrays:
        keep = pltpu.make_async_copy(x_ref, part_of(out_ref, mine, size), own_sem)
        keep.start()
        keeps.append(keep)
    visits = []
    for kz in range(place.nz):
        visits.append((kz, 0, 0))
        if kz:
            visits += [(kz - 1, ka, 0) for ka in range(1, place.na)]
    visits += [(place.nz - 1, ka, 0) for ka in range(1, place.na)]
    visits += [(kz, ka, kb) for kb in range(1, place.nb) for ka in range(place.na) for kz in range(place.nz)]
    side_work = list(side_work)
    for kz, ka, kb in visits[1:]:
        if side_work:
            side_work.pop(0)()
        slot += 1
        zb, ab, bb = by_distance(z, place.nz, kz), by_distance(a, place.na, ka), by_distance(b, place.nb, kb)
        block = place.block(core, zb, ab, bb)
        arrived(block)
        if kb == 0 and ka == 0:
            along("z", z, place.nz, block, slot, zb, (0, 1))
        if kb == 0:
            along("a", a, place.na, block, slot, None if ka == 0 else ab, (2, 3))
        along("b", b, place.nb, block, slot, None if kb == 0 else bb, (4, 5))
        if place.cores == 2:
            send(block, 6, slot, sibling, None, False)
    for action in side_work:
        action()
    if place.cores == 2:
        for bb in range(place.nb):
            for ab in range(place.na):
                for zb in range(place.nz):
                    arrived(place.block(1 - core, jnp.int32(zb), jnp.int32(ab), jnp.int32(bb)))
    for condition, copy in sent:
        when(condition, copy.wait_send)
    for keep in keeps:
        keep.wait()


def gather_with_tiles(layout, blocks, lines, rows):
    n = 1
    for _, _, places in layout:
        n *= places
    per_core = n // layout[0][2]
    count = len(blocks)
    heads, reach_count, _, width = lines.shape
    sizes = [block.shape[0] if block.shape[0] % 16 == 0 else None for block in blocks]

    def body(*refs):
        xs, line_ref, outs, tile_ref = refs[:count], refs[count], refs[count + 1 : 2 * count + 1], refs[2 * count + 1]
        tile_buf, tile_sem = refs[2 * count + 2 : 2 * count + 4]
        sems = refs[2 * count + 4 :]
        arrays = [(xs[i], outs[i], sizes[i], *sems[3 * i : 3 * i + 3]) for i in range(count)]

        def tile_copy(h):
            return pltpu.make_async_copy(tile_buf.at[h], tile_ref.at[h], tile_sem.at[h])

        def spread(h):
            for d in range(reach_count):
                wide = jnp.broadcast_to(line_ref[h, d], (rows, width))
                tile_buf[h, d] = pltpu.roll(wide, 0, 1, stride=1, stride_axis=0)[:, :rows]
            tile_copy(h).start()

        gather_steps(layout, arrays, [functools.partial(spread, h) for h in range(heads)])
        for h in range(heads):
            tile_copy(h).wait()

    scratch = [pltpu.VMEM((heads, reach_count, rows, rows), F32), pltpu.SemaphoreType.DMA((heads,))]
    for _ in blocks:
        scratch += [pltpu.SemaphoreType.DMA((7, per_core)), pltpu.SemaphoreType.DMA((n,)), pltpu.SemaphoreType.DMA]
    anywhere = pl.BlockSpec(memory_space=pl.ANY)
    inside = pl.BlockSpec(memory_space=pltpu.VMEM)
    *gathered, tiles = pl.pallas_call(
        body,
        out_shape=[
            jax.ShapeDtypeStruct((n,) + block.shape if size is None else (n * size,) + block.shape[1:], block.dtype)
            for block, size in zip(blocks, sizes, strict=True)
        ]
        + [jax.ShapeDtypeStruct((heads, reach_count, rows, rows), F32)],
        in_specs=[inside] * (count + 1),
        out_specs=[anywhere] * (count + 1),
        scratch_shapes=scratch,
        compiler_params=pltpu.CompilerParams(collective_id=1, has_side_effects=True, vmem_limit_bytes=60_000_000),
        name="gather_all",
    )(*blocks, lines)
    return gathered, tiles


class Reduction:
    def __init__(self, place, source, size, lanes, buffers):
        self.place, self.source, self.size, self.lanes = place, source, size, lanes
        self.own, self.sib, line_b, line_a, line_z, self.load_sem, self.send_sem, self.sib_sem, sem_b, sem_a, sem_z = buffers
        self.lines = {"b": (line_b, sem_b), "a": (line_a, sem_a), "z": (line_z, sem_z)}
        self.order = [by_distance(place.z, place.nz, k) for k in reversed(range(place.nz))]
        self.sibling = place.device(core=1 - place.core)

    def slot(self, zb, ab, bb):
        return (zb * self.place.na + ab) * self.place.nb + bb

    def piece(self, core, zb, ab, bb):
        block = self.place.block(core, zb, ab, bb)
        if self.size is None:
            return self.source.at[block, :, pl.ds(*self.lanes)]
        return self.source.at[pl.ds(pl.multiple_of(block * self.size, self.size), self.size), pl.ds(*self.lanes)]

    def remote(self, src, dst, send_sem, recv_sem, device):
        return pltpu.make_async_remote_copy(
            src_ref=src, dst_ref=dst, send_sem=send_sem, recv_sem=recv_sem, device_id=device, device_id_type=MESH
        )

    def inner(self, a_at, b_at):
        place = self.place
        return [
            (by_distance(a_at, place.na, ka), by_distance(b_at, place.nb, kb))
            for kb in reversed(range(place.nb))
            for ka in reversed(range(place.na))
        ]

    def open(self, i):
        place, zb = self.place, self.order[i]
        their_a, their_b = (place.b, place.a) if place.swaps else (place.a, place.b)
        for (ao, bo), (at, bt) in zip(self.inner(place.a, place.b), self.inner(their_a, their_b), strict=True):
            slot = self.slot(zb, ao, bo)
            pltpu.make_async_copy(self.piece(place.core, zb, ao, bo), self.own.at[slot], self.load_sem.at[slot]).start()
            slot = self.slot(zb, at, bt)
            copy = self.remote(
                self.piece(1 - place.core, zb, at, bt), self.sib.at[slot], self.send_sem.at[0, slot], self.sib_sem.at[slot], self.sibling
            )
            copy.start()

    def add(self, slot, buffer, sem, at):
        self.remote(self.own.at[slot], buffer.at[at], self.send_sem.at[1, slot], sem.at[at], self.sibling).wait_recv()
        self.own[slot] = (self.own[slot].astype(F32) + buffer[at].astype(F32)).astype(self.own.dtype)

    def both_cores(self, zb, ab, bb):
        slot = self.slot(zb, ab, bb)
        pltpu.make_async_copy(self.piece(self.place.core, zb, ab, bb), self.own.at[slot], self.load_sem.at[slot]).wait()
        self.add(slot, self.sib, self.sib_sem, slot)

    def pass_on(self, name, at, places, target, inner, inner_count, slot, condition=None):
        line, sem = self.lines[name]
        move = jnp.where(target > at, 1, -1)
        if places == 2:
            there = inner
        else:
            outer = (at - move >= 0) & (at - move < places)
            if condition is not None:
                outer = outer & condition
            pl.when(outer)(lambda: self.add(slot, line, sem, target * inner_count + inner))
            there = jnp.where((target == at + move) & (move < 0), places, target) * inner_count + inner
        device = self.place.device(**{name: at + move})
        copy = self.remote(self.own.at[slot], line.at[there], self.send_sem.at[1, slot], sem.at[there], device)
        when(condition, copy.start)

    def take_in(self, name, at, places, inner, inner_count, slot, condition=None):
        line, sem = self.lines[name]
        if places == 1:
            return
        if places == 2:
            when(condition, lambda: self.add(slot, line, sem, inner))
            return
        lower, upper = at > 0, at < places - 1
        if condition is not None:
            lower, upper = lower & condition, upper & condition
        pl.when(lower)(lambda: self.add(slot, line, sem, at * inner_count + inner))
        pl.when(upper)(lambda: self.add(slot, line, sem, places * inner_count + inner))

    def first(self, i):
        place, zb = self.place, self.order[i]
        for kb in reversed(range(1, place.nb)):
            bb = by_distance(place.b, place.nb, kb)
            for ka in reversed(range(place.na)):
                ab = by_distance(place.a, place.na, ka)
                self.both_cores(zb, ab, bb)
                inner, count = zb * place.na + ab, place.nz * place.na
                self.pass_on("b", place.b, place.nb, bb, inner, count, self.slot(zb, ab, bb))
        for ka in reversed(range(place.na)):
            self.both_cores(zb, by_distance(place.a, place.na, ka), place.b)

    def second(self, i):
        place, zb = self.place, self.order[i]
        for ka in reversed(range(place.na)):
            ab = by_distance(place.a, place.na, ka)
            slot = self.slot(zb, ab, place.b)
            self.take_in("b", place.b, place.nb, zb * place.na + ab, place.nz * place.na, slot)
            if ka:
                self.pass_on("a", place.a, place.na, ab, zb, place.nz, slot)

    def third(self, i):
        place, zb = self.place, self.order[i]
        slot = self.slot(zb, place.a, place.b)
        self.take_in("a", place.a, place.na, zb, place.nz, slot)
        if i < place.nz - 1:
            self.pass_on("z", place.z, place.nz, zb, 0, 1, slot)

    def last(self, out_ref):
        place = self.place
        slot = self.slot(place.z, place.a, place.b)
        self.take_in("z", place.z, place.nz, 0, 1, slot)
        out_ref[...] = self.own[slot].astype(F32)

    def actions(self):
        n = self.place.nz
        found = []
        for i in range(n + 2):
            for step, back in ((self.first, 0), (self.second, 1), (self.third, 2)):
                if 0 <= i - back < n:
                    found.append(functools.partial(step, i - back))
        return found

    def drain(self):
        place = self.place
        mine = self.slot(place.z, place.a, place.b)
        for slot in range(place.nz * place.na * place.nb):
            for kind in range(2):
                copy = self.remote(self.sib.at[slot], self.sib.at[slot], self.send_sem.at[kind, slot], self.sib_sem.at[slot], self.sibling)
                when(None if kind == 0 else mine != slot, copy.wait_send)


def reduction_scratch(layout, block_shape, dtype):
    _, (_, _, nb), (_, _, na), (_, _, nz) = layout
    deep = lambda places: 1 if places <= 2 else places + 1
    vm = lambda *lead: pltpu.VMEM(lead + block_shape, dtype)
    dma = pltpu.SemaphoreType.DMA
    per_core = nz * na * nb
    counts = {"b": deep(nb) * nz * na, "a": deep(na) * nz, "z": deep(nz)}
    return [
        vm(per_core), vm(per_core), vm(counts["b"]), vm(counts["a"]), vm(counts["z"]),
        dma((per_core,)), dma((2, per_core)),
        dma((per_core,)), dma((counts["b"],)), dma((counts["a"],)), dma((counts["z"],)),
    ]


BUFFERS = 11


def row_tiles(rows):
    return rows if rows % 16 == 0 else None


def projection_grads(every, grad_keys, grad_values, pairs, near_grads, share):
    width = every.shape[1]
    rows = pairs[0][0].shape[0]
    tall = 2 * rows if every.shape[0] % (2 * rows) == 0 else rows
    many = every.shape[0] // tall
    order = [(7, 1), (4, 1), (3, 1), (5, 1), (6, 1), (0, 1), (1, many), (2, many)]
    matrix_of, start_of = [], {}
    for matrix, count in order:
        start_of[matrix] = len(matrix_of)
        matrix_of += [matrix] * count
    steps = len(matrix_of)

    def body(table_ref, every_ref, gk_ref, gv_ref, l0, r0, l1, r1, l2, r2, l3, r3, n5, n6, out_ref, acc_ref):
        step = pl.program_id(0)
        sources = {0: (l0, r0), 3: (l1, r1), 4: (l2, r2), 7: (l3, r3), 1: (every_ref, gk_ref), 2: (every_ref, gv_ref)}
        for matrix, count in order:
            start = start_of[matrix]
            if matrix in (5, 6):

                @pl.when(step == start)
                def _(near_ref=n5 if matrix == 5 else n6):
                    out_ref[0] = near_ref[...]

                continue
            left, right = sources[matrix]

            @pl.when((step >= start) & (step < start + count))
            def _(left=left, right=right, start=start, count=count):
                if count == 1:
                    out_ref[0] = transposed_times(left[...], right[...]).astype(BF16)
                    return
                term = transposed_times(left[...], right[...])

                @pl.when(step == start)
                def _():
                    acc_ref[...] = term

                @pl.when(step > start)
                def _():
                    acc_ref[...] += term

                @pl.when(step == start + count - 1)
                def _():
                    out_ref[0] = acc_ref[...].astype(BF16)

    def chunk(start):
        return pl.BlockSpec((tall, width), lambda i, _: (jnp.clip(i - start, 0, many - 1), 0))

    both = pl.BlockSpec(
        (tall, width), lambda i, _: (jnp.clip(jnp.where(i < start_of[2], i - start_of[1], i - start_of[2]), 0, many - 1), 0)
    )
    square = pl.BlockSpec((width, width), lambda i, _: (0, 0))
    in_specs = [both, chunk(start_of[1]), chunk(start_of[2])] + [pl.BlockSpec((rows, width), lambda i, _: (0, 0))] * 8
    return pl.pallas_call(
        body,
        grid_spec=pltpu.PrefetchScalarGridSpec(
            num_scalar_prefetch=1,
            grid=(steps,),
            in_specs=in_specs + [square, square],
            out_specs=pl.BlockSpec((1, width, width), lambda i, table: (table[i], 0, 0)),
            scratch_shapes=[pltpu.VMEM((width, width), F32)],
        ),
        out_shape=jax.ShapeDtypeStruct((8, width, width), BF16),
        cost_estimate=pl.CostEstimate(
            flops=2 * width * width * (2 * every.shape[0] + 4 * pairs[0][0].shape[0]), transcendentals=0, bytes_accessed=40_000_000
        ),
        compiler_params=pltpu.CompilerParams(vmem_limit_bytes=50_000_000),
        name="projection_grads",
    )(jnp.asarray(matrix_of, jnp.int32), every, grad_keys, grad_values, *[side for pair in pairs for side in pair], *near_grads)


def last_steps(layout, sizes, matrix_grads, share, lines, grad_queries, query_matrix, joined, hidden, gain, grad_first):
    tokens, width = grad_queries.shape
    cut = width // 256 * 128
    windows = ((0, cut), (cut, width - cut))
    bits = lambda count: [1 << i for i in range(count.bit_length() - 1)]
    rounds = [("fsdp", step) for step in bits(sizes[1])] + [("dp", step) for step in bits(sizes[0])]
    given = [line for line in lines if line is not None]
    per_gain = width // 128
    total_rows = sum(per_gain if line is None else line.shape[0] for line in lines)
    held_rows = -(-total_rows // 8) * 8

    def body(*refs):
        (mats_ref, dq_ref, m0_ref, in_ref, hid_ref, gf_ref, gain_ref), refs = refs[:7], refs[7:]
        line_refs, refs = list(refs[: len(given)]), refs[len(given) :]
        (attn_ref, sum_ref, hg_ref), refs = refs[:3], refs[3:]
        (q_buf, m0, in_buf, hid_buf, first_buf, load_sem), refs = refs[:6], refs[6:]
        (line_out, line_in, line_send, line_recv), buffers = refs[:4], refs[4:]
        place = Place(layout)
        index = {axis: lax.axis_index(axis).astype(jnp.int32) for axis in AXES}
        across = lambda axis, step: {axis: index[axis] + step * (1 - 2 * ((index[axis] // step) % 2))}
        meet(place, [across(axis, step) for axis, step in rounds])
        loads = [
            pltpu.make_async_copy(src, dst, load_sem.at[i])
            for i, (src, dst) in enumerate(
                ((dq_ref, q_buf), (m0_ref.at[0], m0), (in_ref, in_buf), (hid_ref, hid_buf), (gf_ref, first_buf))
            )
        ]
        pieces = [
            Reduction(place, mats_ref, row_tiles(share), window, buffers[BUFFERS * i : BUFFERS * (i + 1)])
            for i, window in enumerate(windows)
        ]
        for i in range(place.nz):
            for piece_of in pieces:
                piece_of.open(i)
            if i == 0:
                for load in loads:
                    load.start()
        actions = [action for both in zip(*[piece_of.actions() for piece_of in pieces], strict=True) for action in both]
        actions.pop(0)()
        actions.pop(0)()
        for load in loads:
            load.wait()
        piece = tokens // 4

        def finish(i, total):
            rows = pl.ds(pl.multiple_of(i * piece, piece), piece)
            held = hid_buf[rows, :].astype(F32)
            scale = inverse_rms(held)
            grad = dot_t(q_buf[rows, :], m0[...]) + in_buf[rows, :]
            hg_ref[rows, :] = first_buf[rows, :] + norm_back(held, scale, gain_ref[...], grad)
            return total + jnp.sum(grad * held * scale, axis=0, keepdims=True)

        gain_grad = lax.fori_loop(0, 4, finish, jnp.zeros((1, width), F32))
        at = 0
        for line in lines:
            if line is None:
                for i in range(per_gain):
                    sum_ref[at + i : at + i + 1, :] = gain_grad[:, i * 128 : (i + 1) * 128]
                at += per_gain
            else:
                ref = line_refs.pop(0)
                sum_ref[at : at + ref.shape[0], :] = ref[...]
                at += ref.shape[0]
        if at < held_rows:
            sum_ref[at:, :] = jnp.zeros((held_rows - at, 128), F32)

        def round_copy(i):
            axis, step = rounds[i]
            return pltpu.make_async_remote_copy(
                src_ref=line_out.at[i], dst_ref=line_in.at[i], send_sem=line_send.at[i], recv_sem=line_recv.at[i],
                device_id=across(axis, step), device_id_type=MESH,
            )

        for i in range(len(rounds)):
            line_out[i] = sum_ref[...]
            if actions:
                actions.pop(0)()
            round_copy(i).start()
            for _ in range(3):
                if actions:
                    actions.pop(0)()
            round_copy(i).wait_recv()
            sum_ref[...] += line_in[i]
        for action in actions:
            action()
        for piece_of, window in zip(pieces, windows, strict=True):
            piece_of.last(attn_ref.at[:, pl.ds(*window)])
        for i in range(len(rounds)):
            round_copy(i).wait_send()
        for piece_of in pieces:
            piece_of.drain()

    anywhere = pl.BlockSpec(memory_space=pl.ANY)
    inside = pl.BlockSpec(memory_space=pltpu.VMEM)
    block = (share, width)
    dma = pltpu.SemaphoreType.DMA
    scratch = [
        pltpu.VMEM(grad_queries.shape, BF16), pltpu.VMEM((width, width), BF16), pltpu.VMEM(joined.shape, joined.dtype),
        pltpu.VMEM(hidden.shape, hidden.dtype), pltpu.VMEM(grad_first.shape, F32), dma((5,)),
        pltpu.VMEM((len(rounds), held_rows, 128), F32), pltpu.VMEM((len(rounds), held_rows, 128), F32),
        dma((len(rounds),)), dma((len(rounds),)),
    ]
    for window in windows:
        scratch += reduction_scratch(layout, (share, window[1]), BF16)
    return pl.pallas_call(
        body,
        out_shape=[
            jax.ShapeDtypeStruct(block, F32),
            jax.ShapeDtypeStruct((held_rows, 128), F32),
            jax.ShapeDtypeStruct((tokens, width), F32),
        ],
        in_specs=[anywhere] * 6 + [inside] * (1 + len(given)),
        out_specs=[inside] * 3,
        scratch_shapes=scratch,
        compiler_params=pltpu.CompilerParams(collective_id=2, has_side_effects=True, vmem_limit_bytes=50_000_000),
        name="last_steps",
    )(matrix_grads, grad_queries, query_matrix, joined, hidden, grad_first, gain.reshape(1, width), *given)


def from_behind(array, axis, by):
    length = lax.axis_size(axis)
    pairs = [(i, i + by) for i in range(length) if 0 <= i + by < length]
    return lax.ppermute(array, axis, pairs)


def sum_of_group(parts, place):
    group = parts.shape[0]
    if group & (group - 1):
        return lax.psum_scatter(parts, "fsdp", scatter_dimension=0, tiled=True)[0].astype(F32)
    step = 1
    while step < group:
        halves = parts.reshape((parts.shape[0] // 2, 2) + parts.shape[1:])
        bit = (place // step) % 2
        away = lax.dynamic_index_in_dim(halves, 1 - bit, axis=1, keepdims=False)
        kept = lax.dynamic_index_in_dim(halves, bit, axis=1, keepdims=False)
        came = lax.ppermute(away, "fsdp", [(i, i ^ step) for i in range(group)])
        parts = kept.astype(F32) + came.astype(F32)
        step *= 2
        if step < group:
            parts = parts.astype(BF16)
    return parts[0]


def product(left_side, right_side):
    return jnp.dot(left_side, right_side, preferred_element_type=F32)


def times_transposed(left_side, right_side):
    return lax.dot_general(left_side, right_side, (((1,), (1,)), ((), ())), preferred_element_type=F32)


def transposed_times(left_side, right_side):
    return lax.dot_general(left_side, right_side, (((0,), (0,)), ((), ())), preferred_element_type=F32)


def inverse_rms(residual):
    return lax.rsqrt(jnp.mean(residual * residual, axis=-1, keepdims=True) + norm_eps)


def norm_back(residual, scale, gain, incoming):
    weighted = gain * incoming
    return scale * weighted - residual * scale * scale * scale * jnp.mean(
        residual * weighted, axis=-1, keepdims=True
    )


def gelu_parts(values):
    tangent = jnp.tanh(gelu_scale * (values + gelu_cubic * values * values * values))
    result = 0.5 * values * (1.0 + tangent)
    slope = 0.5 * (1.0 + tangent) + 0.5 * values * (1.0 - tangent * tangent) * gelu_scale * (
        1.0 + 3.0 * gelu_cubic * values * values
    )
    return (result, slope)


def bucket_of(offset):
    magnitude = jnp.abs(offset)
    counted = jnp.zeros(offset.shape, jnp.int32)
    for threshold in relative_bucket_limits:
        counted = counted + (magnitude >= threshold).astype(jnp.int32)
    return counted + (offset > 0).astype(jnp.int32) * (len(relative_bucket_limits) + 1)


def piece_labels(positions, starts):
    inside = (positions[None, :, None] >= starts[:, None, :]) & (
        positions[None, :, None] < starts[:, None, :] + PIECE
    )
    labels = jnp.arange(1, starts.shape[1] + 1, dtype=jnp.int32)
    return jnp.sum(jnp.where(inside, labels[None, None, :], 0), axis=2)


def dot_t(left_side, right_side):
    return lax.dot_general(left_side, right_side, (((1,), (1,)), ((), ())), preferred_element_type=F32)


def own_lanes(values, which, width):
    lane = lax.broadcasted_iota(jnp.int32, values.shape, 1)
    return jnp.where((lane >= which * width) & (lane < (which + 1) * width), values, jnp.zeros_like(values))


def flipped(values):
    return values.astype(F32).T.astype(BF16)


def bias_lines(rel_table, rows, reach):
    heads = rel_table.shape[1]
    width = 2 * rows
    count = 2 * reach + 1
    shift = jnp.arange(width, dtype=jnp.int32)
    behind = jnp.where(shift < rows, shift, shift - width)
    far = (jnp.arange(count, dtype=jnp.int32) - reach) * rows
    ids = bucket_of(far[:, None] - behind[None, :])
    hot = (ids[:, :, None] == jnp.arange(rel_table.shape[0], dtype=jnp.int32)).astype(F32)
    lines = jnp.einsum("dwb,bh->hdw", hot, rel_table, precision=lax.Precision.HIGHEST)
    return lines.reshape(heads, count, 1, width)


def tile_at(block, place, reach):
    return jnp.clip(block - place, -reach, reach) + reach


def self_attention(place, query, keys, values, tiles, hidden_mask, head_size, reach):
    count, rows, width = query.shape
    blocks = keys.shape[0]
    pair = 128
    per = pair // head_size

    def body(place_ref, q_ref, k_ref, v_ref, tile_ref, mask_ref, o_ref, ot_ref, lse_ref, s_ref, p_ref):
        for b in range(count):
            scaled = q_ref[b] * jnp.asarray(0.125, BF16)
            value_t = jnp.concatenate([flipped(v_ref[j, b]) for j in range(blocks)], axis=1)
            for h in range(per):
                mine = own_lanes(scaled, h, head_size)
                top = jnp.full((1, rows), -jnp.inf, F32)
                for j in range(blocks):
                    s = dot_t(k_ref[j, b], mine)
                    s = s + tile_ref[h, tile_at(j, place_ref[0], reach)] + mask_ref[b, j]
                    s_ref[j] = s
                    top = jnp.maximum(top, jnp.max(s, axis=0, keepdims=True))
                total = jnp.zeros((1, rows), F32)
                for j in range(blocks):
                    p = jnp.exp(s_ref[j] - top)
                    total = total + jnp.sum(p, axis=0, keepdims=True)
                    p_ref[j * rows : (j + 1) * rows, :] = p.astype(BF16)
                part = product(value_t[h * head_size : (h + 1) * head_size], p_ref[...]) / total
                ot_ref[0, b, h * head_size : (h + 1) * head_size, :] = part
                lse_ref[0, b * per + h : b * per + h + 1, :] = top + jnp.log(total)
            o_ref[b] = ot_ref[0, b].T.astype(BF16)

    steps = width // pair
    grid_spec = pltpu.PrefetchScalarGridSpec(
        num_scalar_prefetch=1,
        grid=(steps,),
        in_specs=[
            pl.BlockSpec((count, rows, pair), lambda i, _: (0, 0, i)),
            pl.BlockSpec((blocks, count, rows, pair), lambda i, _: (0, 0, 0, i)),
            pl.BlockSpec((blocks, count, rows, pair), lambda i, _: (0, 0, 0, i)),
            pl.BlockSpec((per,) + tiles.shape[1:], lambda i, _: (i, 0, 0, 0)),
            pl.BlockSpec(hidden_mask.shape, lambda i, _: (0, 0, 0, 0)),
        ],
        out_specs=[
            pl.BlockSpec((count, rows, pair), lambda i, _: (0, 0, i)),
            pl.BlockSpec((1, count, pair, rows), lambda i, _: (i, 0, 0, 0)),
            pl.BlockSpec((1, count * per, rows), lambda i, _: (i, 0, 0)),
        ],
        scratch_shapes=[
            pltpu.VMEM((blocks, rows, rows), F32),
            pltpu.VMEM((blocks * rows, rows), BF16),
        ],
    )
    cost = 4 * count * blocks * rows * rows * width
    return pl.pallas_call(
        body,
        grid_spec=grid_spec,
        out_shape=[
            jax.ShapeDtypeStruct((count, rows, width), BF16),
            jax.ShapeDtypeStruct((steps, count, pair, rows), F32),
            jax.ShapeDtypeStruct((steps, count * per, rows), F32),
        ],
        cost_estimate=pl.CostEstimate(flops=4 * cost, transcendentals=0, bytes_accessed=30_000_000),
        name="self_attention",
    )(place, query, keys, values, tiles, hidden_mask)


def self_attention_back(place, query, keys, values, tiles, hidden_mask, outer_t, lse, grad, head_size, reach):
    count, rows, width = query.shape
    blocks = keys.shape[0]
    pair = 128
    per = pair // head_size
    half = rows // 2

    def body(
        place_ref, q_ref, k_ref, v_ref, tile_ref, mask_ref, ot_ref, lse_ref, do_ref,
        dq_ref, dk_ref, dv_ref, sum_ref, acc_ref, dk_acc, dv_acc,
    ):
        for b in range(count):
            scaled = q_ref[b] * jnp.asarray(0.125, BF16)
            incoming = do_ref[b]
            key_t = jnp.concatenate([flipped(k_ref[j, b]) for j in range(blocks)], axis=1)
            weighed = incoming.astype(F32).T * ot_ref[0, b]
            query_parts = []
            for h in range(per):
                lanes = slice(h * head_size, (h + 1) * head_size)
                mine = own_lanes(scaled, h, head_size)
                theirs = own_lanes(incoming, h, head_size)
                delta = jnp.sum(weighed[lanes], axis=0, keepdims=True)
                level = lse_ref[0, b * per + h : b * per + h + 1, :]
                part = jnp.zeros((head_size, rows), F32)
                for j in range(blocks):
                    s = dot_t(k_ref[j, b], mine)
                    s = s + tile_ref[h, tile_at(j, place_ref[0], reach)] + mask_ref[b, j]
                    p = jnp.exp(s - level)
                    ds = p * (dot_t(v_ref[j, b], theirs) - delta)
                    p_low = p.astype(BF16)
                    ds_low = ds.astype(BF16)
                    dv = product(p_low, theirs)
                    dk = product(ds_low, mine)
                    if h == 0:
                        dv_acc[j] = dv
                        dk_acc[j] = dk
                    else:
                        dv_ref[j, b] = (dv_acc[j] + dv).astype(BF16)
                        dk_ref[j, b] = (dk_acc[j] + dk).astype(BF16)
                    part = part + product(key_t[lanes, j * rows : (j + 1) * rows], ds_low)
                    if b == 0:
                        acc_ref[h, j] = ds
                    else:
                        acc_ref[h, j] = acc_ref[h, j] + ds
                query_parts.append(part)
            dq_ref[b] = (jnp.concatenate(query_parts, axis=0) * 0.125).T.astype(BF16)
        for h in range(per):
            for j in range(blocks):
                upper, lower = acc_ref[h, j, :half, :], acc_ref[h, j, half:, :]
                folded = jnp.concatenate(
                    [lower[:, :half], lower[:, half:] + upper[:, :half], upper[:, half:], jnp.zeros((half, half), F32)],
                    axis=1,
                )
                left = half // 2
                while left >= 8:
                    folded = folded[left:] + pltpu.roll(folded[:left], left, 1)
                    left //= 2
                sum_ref[h, j] = folded

    steps = width // pair
    grid_spec = pltpu.PrefetchScalarGridSpec(
        num_scalar_prefetch=1,
        grid=(steps,),
        in_specs=[
            pl.BlockSpec((count, rows, pair), lambda i, _: (0, 0, i)),
            pl.BlockSpec((blocks, count, rows, pair), lambda i, _: (0, 0, 0, i)),
            pl.BlockSpec((blocks, count, rows, pair), lambda i, _: (0, 0, 0, i)),
            pl.BlockSpec((per,) + tiles.shape[1:], lambda i, _: (i, 0, 0, 0)),
            pl.BlockSpec(hidden_mask.shape, lambda i, _: (0, 0, 0, 0)),
            pl.BlockSpec((1, count, pair, rows), lambda i, _: (i, 0, 0, 0)),
            pl.BlockSpec((1, count * per, rows), lambda i, _: (i, 0, 0)),
            pl.BlockSpec((count, rows, pair), lambda i, _: (0, 0, i)),
        ],
        out_specs=[
            pl.BlockSpec((count, rows, pair), lambda i, _: (0, 0, i)),
            pl.BlockSpec((blocks, count, rows, pair), lambda i, _: (0, 0, 0, i)),
            pl.BlockSpec((blocks, count, rows, pair), lambda i, _: (0, 0, 0, i)),
            pl.BlockSpec((per, blocks, 8, 2 * rows), lambda i, _: (i, 0, 0, 0)),
        ],
        scratch_shapes=[
            pltpu.VMEM((per, blocks, rows, rows), F32),
            pltpu.VMEM((blocks, rows, pair), F32),
            pltpu.VMEM((blocks, rows, pair), F32),
        ],
    )
    cost = 4 * count * blocks * rows * rows * width
    return pl.pallas_call(
        body,
        grid_spec=grid_spec,
        out_shape=[
            jax.ShapeDtypeStruct((count, rows, width), BF16),
            jax.ShapeDtypeStruct((blocks, count, rows, width), BF16),
            jax.ShapeDtypeStruct((blocks, count, rows, width), BF16),
            jax.ShapeDtypeStruct((width // head_size, blocks, 8, 2 * rows), F32),
        ],
        cost_estimate=pl.CostEstimate(flops=10 * cost, transcendentals=0, bytes_accessed=40_000_000),
        name="self_attention_back",
    )(place, query, keys, values, tiles, hidden_mask, outer_t, lse, grad)


def whole(shape):
    return pl.BlockSpec(shape, lambda *_: (0,) * len(shape))


FF_TILE = 512


def feed_forward_grads(second_sum, gain, grad_out_low, weights, bias_input):
    tokens, width = second_sum.shape
    units = bias_input.shape[0]
    tile = FF_TILE
    steps = units // tile
    part = 256

    def body(sum_ref, gain_ref, go_ref, wi_ref, wo_ref, bi_ref, act_ref, gp_ref, gbi_ref, gw_ref, n_ref):
        step = pl.program_id(0)

        @pl.when(step == 0)
        def _():
            held = sum_ref[...]
            n_ref[...] = (held * inverse_rms(held) * gain_ref[...]).astype(BF16)

        normed = n_ref[...]
        incoming = go_ref[...]
        for at in range(0, tile, part):
            rows = slice(at, at + part)
            value, slope = gelu_parts(dot_t(normed, wi_ref[rows, :]) + bi_ref[0, :, rows])
            value_low = value.astype(BF16)
            grad_pre = dot_t(incoming, wo_ref[rows, :]) * slope
            bias_grad = jnp.sum(grad_pre, axis=0, keepdims=True)
            for i in range(part // 128):
                gbi_ref[0, at // 128 + i : at // 128 + i + 1, :] = bias_grad[:, i * 128 : (i + 1) * 128]
            grad_pre_low = grad_pre.astype(BF16)
            act_ref[:, rows] = value_low
            gp_ref[:, rows] = grad_pre_low
            gw_ref[0, 0, rows, :] = transposed_times(grad_pre_low, normed).astype(BF16)
            gw_ref[1, 0, rows, :] = transposed_times(value_low, incoming).astype(BF16)

    tall, line = whole((tokens, width)), whole((1, width))
    across = pl.BlockSpec((tokens, tile), lambda i: (0, i))
    return pl.pallas_call(
        body,
        grid=(steps,),
        in_specs=[
            tall, line, tall,
            pl.BlockSpec((tile, width), lambda i: (i, 0)),
            pl.BlockSpec((tile, width), lambda i: (i + steps, 0)),
            pl.BlockSpec((1, 1, tile), lambda i: (i, 0, 0)),
        ],
        out_specs=[
            across, across,
            pl.BlockSpec((1, tile // 128, 128), lambda i: (i, 0, 0)),
            pl.BlockSpec((2, 1, tile, width), lambda i: (0, i, 0, 0)),
        ],
        out_shape=[
            jax.ShapeDtypeStruct((tokens, units), BF16),
            jax.ShapeDtypeStruct((tokens, units), BF16),
            jax.ShapeDtypeStruct((steps, tile // 128, 128), F32),
            jax.ShapeDtypeStruct((2, steps, tile, width), BF16),
        ],
        scratch_shapes=[pltpu.VMEM((tokens, width), BF16)],
        cost_estimate=pl.CostEstimate(flops=8 * tokens * width * units, transcendentals=0, bytes_accessed=40_000_000),
        compiler_params=pltpu.CompilerParams(vmem_limit_bytes=50_000_000),
        name="feed_forward_grads",
    )(second_sum, gain.reshape(1, width), grad_out_low, weights, weights, bias_input.reshape(steps, 1, tile))


def feed_forward_sums(second_sum, gain, grad_out_low, weights, activated, grad_pre_low, bias_output):
    tokens, width = second_sum.shape
    tile = FF_TILE
    steps = activated.shape[1] // tile

    def body(sum_ref, gain_ref, go_ref, wi_ref, wo_ref, act_ref, gp_ref, bo_ref, out_ref, gs_ref, gg_ref, gbo_ref, acc_ref, gn_ref):
        step = pl.program_id(0)
        out_part = product(act_ref[...], wo_ref[...])
        norm_part = product(gp_ref[...], wi_ref[...])

        @pl.when(step == 0)
        def _():
            acc_ref[...] = out_part
            gn_ref[...] = norm_part

        @pl.when(step > 0)
        def _():
            acc_ref[...] += out_part
            gn_ref[...] += norm_part

        @pl.when(step == steps - 1)
        def _():
            held = sum_ref[...]
            scale = inverse_rms(held)
            out_ref[...] = (held + acc_ref[...] + bo_ref[...]).astype(BF16)
            grad_norm = gn_ref[...]
            grad_out = go_ref[...].astype(F32)
            for ref, line in (
                (gbo_ref, jnp.sum(grad_out, axis=0, keepdims=True)),
                (gg_ref, jnp.sum(grad_norm * held * scale, axis=0, keepdims=True)),
            ):
                for i in range(width // 128):
                    ref[i : i + 1, :] = line[:, i * 128 : (i + 1) * 128]
            gs_ref[...] = grad_out + norm_back(held, scale, gain_ref[...], grad_norm)

    tall, line = whole((tokens, width)), whole((1, width))
    rows_of_128 = whole((width // 128, 128))
    across = pl.BlockSpec((tokens, tile), lambda i: (0, i))
    return pl.pallas_call(
        body,
        grid=(steps,),
        in_specs=[
            tall, line, tall,
            pl.BlockSpec((tile, width), lambda i: (i, 0)),
            pl.BlockSpec((tile, width), lambda i: (i + steps, 0)),
            across, across, line,
        ],
        out_specs=[tall, tall, rows_of_128, rows_of_128],
        out_shape=[
            jax.ShapeDtypeStruct((tokens, width), BF16),
            jax.ShapeDtypeStruct((tokens, width), F32),
            jax.ShapeDtypeStruct((width // 128, 128), F32),
            jax.ShapeDtypeStruct((width // 128, 128), F32),
        ],
        scratch_shapes=[pltpu.VMEM((tokens, width), F32), pltpu.VMEM((tokens, width), F32)],
        cost_estimate=pl.CostEstimate(flops=4 * tokens * width * steps * tile, transcendentals=0, bytes_accessed=25_000_000),
        compiler_params=pltpu.CompilerParams(vmem_limit_bytes=50_000_000),
        name="feed_forward_sums",
    )(
        second_sum, gain.reshape(1, width), grad_out_low, weights, weights, activated, grad_pre_low,
        bias_output.reshape(1, width),
    )


def self_projection(place, hidden_all, gain, matrices, tokens):
    total, width = hidden_all.shape
    rows = 256
    own = tokens // rows

    def body(place_ref, hid_ref, gain_ref, m0_ref, m1_ref, m2_ref, q_ref, k_ref, v_ref, every_ref, one_ref):
        held = hid_ref[...].astype(F32)
        normed = (held * inverse_rms(held) * gain_ref[...]).astype(BF16)
        every_ref[...] = normed
        k_ref[...] = product(normed, m1_ref[0]).astype(BF16)
        v_ref[...] = product(normed, m2_ref[0]).astype(BF16)

        @pl.when(pl.program_id(0) // own == place_ref[0])
        def _():
            one_ref[...] = normed
            q_ref[...] = product(normed, m0_ref[0]).astype(BF16)

    block = pl.BlockSpec((rows, width), lambda i, _: (i, 0))
    mine = pl.BlockSpec((rows, width), lambda i, place_ref: (jnp.clip(i - place_ref[0] * own, 0, own - 1), 0))
    matrix = lambda m: pl.BlockSpec((1, width, width), lambda i, _: (m, 0, 0))
    return pl.pallas_call(
        body,
        grid_spec=pltpu.PrefetchScalarGridSpec(
            num_scalar_prefetch=1,
            grid=(total // rows,),
            in_specs=[block, pl.BlockSpec((1, width), lambda i, _: (0, 0)), matrix(0), matrix(1), matrix(2)],
            out_specs=[mine, block, block, block, mine],
        ),
        out_shape=[
            jax.ShapeDtypeStruct((tokens, width), BF16),
            jax.ShapeDtypeStruct((total, width), BF16),
            jax.ShapeDtypeStruct((total, width), BF16),
            jax.ShapeDtypeStruct((total, width), BF16),
            jax.ShapeDtypeStruct((tokens, width), BF16),
        ],
        cost_estimate=pl.CostEstimate(flops=5 * total * width * width, transcendentals=0, bytes_accessed=25_000_000),
        name="self_projection",
    )(place, hidden_all, gain.reshape(1, width), matrices, matrices, matrices)


def span_projection(near, matrices):
    blocks, rows, width = near.shape

    def body(near_ref, mk_ref, mv_ref, k_ref, v_ref):
        k_ref[0] = product(near_ref[0], mk_ref[0]).astype(BF16)
        v_ref[0] = product(near_ref[0], mv_ref[0]).astype(BF16)

    block = pl.BlockSpec((1, rows, width), lambda i: (i, 0, 0))
    return pl.pallas_call(
        body,
        grid=(blocks,),
        in_specs=[block] + [pl.BlockSpec((1, width, width), lambda i, m=m: (m, 0, 0)) for m in (5, 6)],
        out_specs=[block, block],
        out_shape=[jax.ShapeDtypeStruct(near.shape, BF16)] * 2,
        cost_estimate=pl.CostEstimate(flops=4 * blocks * rows * width * width, transcendentals=0, bytes_accessed=15_000_000),
        name="span_projection",
    )(near, matrices, matrices)


def both_heads(values, head_size):
    return jnp.concatenate([own_lanes(values, h, head_size) for h in range(128 // head_size)], axis=0)


def picked(wide, rows, head_size):
    total = own_lanes(wide[:rows], 0, head_size)
    for h in range(1, 128 // head_size):
        total = total + own_lanes(wide[h * rows : (h + 1) * rows], h, head_size)
    return total


def softmax_down(scores):
    raised = jnp.exp(scores - jnp.max(scores, axis=0, keepdims=True))
    return raised / jnp.sum(raised, axis=0, keepdims=True)


def lane_groups(width):
    return [slice(i, i + 128) for i in range(0, width, 128)]


def side_by_side(parts):
    return jnp.concatenate(parts, axis=1)


def span_attention(query, keys, values, head_size):
    blocks, rows, width = query.shape
    span_keys = keys.shape[1]

    def body(q_ref, k_ref, v_ref, o_ref):
        groups = lane_groups(width)
        scaled = q_ref[0] * jnp.asarray(0.125, BF16)
        scores = side_by_side([dot_t(k_ref[0, :, g], both_heads(scaled[:, g], head_size)) for g in groups])
        weights = softmax_down(scores).astype(BF16)
        turned = flipped(v_ref[0])
        wide = [product(turned[g], weights[:, g]).T for g in groups]
        o_ref[0] = side_by_side([picked(w, rows, head_size) for w in wide]).astype(BF16)

    q_spec = pl.BlockSpec((1, rows, width), lambda i: (i, 0, 0))
    k_spec = pl.BlockSpec((1, span_keys, width), lambda i: (i, 0, 0))
    return pl.pallas_call(
        body,
        grid=(blocks,),
        in_specs=[q_spec, k_spec, k_spec],
        out_specs=q_spec,
        out_shape=jax.ShapeDtypeStruct(query.shape, BF16),
        cost_estimate=pl.CostEstimate(flops=16 * blocks * rows * span_keys * width, transcendentals=0, bytes_accessed=12_000_000),
        name="span_attention",
    )(query, keys, values)


def span_attention_back(query, keys, values, grad, near, matrices, head_size):
    blocks, rows, width = query.shape
    span_keys = keys.shape[1]

    def body(q_ref, k_ref, v_ref, do_ref, near_ref, mk_ref, mv_ref, dq_ref, dn_ref, gk_ref, gv_ref, gk_acc, gv_acc):
        step = pl.program_id(0)
        groups = lane_groups(width)
        scaled = q_ref[0] * jnp.asarray(0.125, BF16)
        incoming = do_ref[0]
        stacked = [both_heads(scaled[:, g], head_size) for g in groups]
        theirs = [both_heads(incoming[:, g], head_size) for g in groups]
        k, v = k_ref[0], v_ref[0]
        p = softmax_down(side_by_side([dot_t(k[:, g], s) for g, s in zip(groups, stacked)]))
        dp = side_by_side([dot_t(v[:, g], t) for g, t in zip(groups, theirs)])
        ds = p * (dp - jnp.sum(p * dp, axis=0, keepdims=True))
        ds_low, p_low = ds.astype(BF16), p.astype(BF16)
        dv = side_by_side([product(p_low[:, g], t) for g, t in zip(groups, theirs)]).astype(BF16)
        dk = side_by_side([product(ds_low[:, g], s) for g, s in zip(groups, stacked)]).astype(BF16)
        turned = flipped(k)
        wide = [(product(turned[g], ds_low[:, g]) * 0.125).T for g in groups]
        dq_ref[0] = side_by_side([picked(w, rows, head_size) for w in wide]).astype(BF16)
        dn_ref[0] = dot_t(dk, mk_ref[0]) + dot_t(dv, mv_ref[0])
        near_t = flipped(near_ref[0])

        @pl.when(step == 0)
        def _():
            gk_acc[...] = product(near_t, dk)
            gv_acc[...] = product(near_t, dv)

        @pl.when(step > 0)
        def _():
            gk_acc[...] += product(near_t, dk)
            gv_acc[...] += product(near_t, dv)

        @pl.when(step == blocks - 1)
        def _():
            gk_ref[...] = gk_acc[...].astype(BF16)
            gv_ref[...] = gv_acc[...].astype(BF16)

    q_spec = pl.BlockSpec((1, rows, width), lambda i: (i, 0, 0))
    k_spec = pl.BlockSpec((1, span_keys, width), lambda i: (i, 0, 0))
    square = whole((width, width))
    return pl.pallas_call(
        body,
        grid=(blocks,),
        in_specs=[q_spec, k_spec, k_spec, q_spec, k_spec]
        + [pl.BlockSpec((1, width, width), lambda i, m=m: (m, 0, 0)) for m in (5, 6)],
        out_specs=[q_spec, k_spec, square, square],
        out_shape=[
            jax.ShapeDtypeStruct(query.shape, BF16),
            jax.ShapeDtypeStruct(keys.shape, F32),
            jax.ShapeDtypeStruct((width, width), BF16),
            jax.ShapeDtypeStruct((width, width), BF16),
        ],
        scratch_shapes=[pltpu.VMEM((width, width), F32), pltpu.VMEM((width, width), F32)],
        cost_estimate=pl.CostEstimate(flops=20 * blocks * span_keys * width * width, transcendentals=0, bytes_accessed=40_000_000),
        compiler_params=pltpu.CompilerParams(vmem_limit_bytes=50_000_000),
        name="span_attention_back",
    )(query, keys, values, grad, near, matrices, matrices)


def per_device(hidden, neighbours, piece_starts, out_grad, attn_weights, ffw_weights, vectors, rel_table):
    count, rows, width = hidden.shape
    group = lax.axis_size("fsdp")
    length = rows * group
    heads = rel_table.shape[1]
    head_size = width // heads
    buckets = rel_table.shape[0]
    spans = neighbours.shape[1]
    span_keys = neighbours.shape[2]
    carried = SPAN - 1
    kept = rows - carried
    tokens = count * rows
    reach = -(-relative_bucket_limits[-1] // rows) + 1
    place = lax.axis_index("fsdp").astype(jnp.int32)
    share = attn_weights.shape[0]

    gather = lambda array, axes: lax.all_gather(array, axes, axis=0, tiled=True)
    layout = layout_of((lax.axis_size("dp"), group))
    vector_rows = -(-vectors.shape[0] // 2048) * 16
    vector_block = jnp.pad(vectors, (0, vector_rows * 128 - vectors.shape[0])).reshape(vector_rows, 128)
    hidden_all = gather(hidden[None], "fsdp")
    (attn_full, vector_full), tiles = gather_with_tiles(
        layout, [attn_weights, vector_block], bias_lines(rel_table, rows, reach), rows
    )
    ffw_full = gather(ffw_weights, AXES)
    matrices = attn_full.reshape(8, width, width)
    vector_full = vector_full.reshape(-1, vector_rows * 128)[:, : vectors.shape[0]].reshape(-1).astype(F32)
    bias_input = vector_full[:FF]
    gains = vector_full[FF : FF + 3 * width].reshape(3, width)
    bias_output = vector_full[FF + 3 * width :]

    key_pos = jnp.arange(length, dtype=jnp.int32)
    query_pos = place * rows + jnp.arange(rows, dtype=jnp.int32)
    key_piece = piece_labels(key_pos, piece_starts)
    query_piece = piece_labels(query_pos, piece_starts)
    allowed = (key_pos[:, None] <= query_pos[None, :])[None] | (
        (key_piece[:, :, None] == query_piece[:, None, :]) & (query_piece[:, None, :] > 0)
    )
    mask = jnp.where(allowed, 0.0, masked_score).reshape(count, group, rows, rows)
    place_arg = place.reshape(1)

    residual = hidden.reshape(tokens, width).astype(F32)
    queries, keys, values, normed_every, normed_one = self_projection(
        place_arg, hidden_all.reshape(group * tokens, width), gains[0], matrices, tokens
    )
    queries = queries.reshape(count, rows, width)
    keys = keys.reshape(group, count, rows, width)
    values = values.reshape(group, count, rows, width)
    near = neighbours.reshape(count * spans, span_keys, width)
    cross_keys, cross_values = span_projection(near, matrices)
    context, context_t, lse = self_attention(
        place_arg, queries, keys, values, tiles, mask, head_size, reach
    )
    context = context.reshape(tokens, width)
    first_sum = residual + product(context, matrices[3])
    scale_two = inverse_rms(first_sum)
    normed_two = (first_sum * scale_two * gains[1]).astype(BF16)
    cross_queries = product(normed_two, matrices[4]).astype(BF16).reshape(count, rows, width)

    def ahead(array):
        incoming = from_behind(array[:, :carried], "fsdp", -1)
        return jnp.concatenate([array[:, carried:], incoming], axis=1).reshape(count * spans, SPAN, width)

    def behind(array):
        array = array.reshape(count, rows, width)
        arriving = from_behind(array[:, kept:], "fsdp", 1)
        return jnp.concatenate([arriving, array[:, :kept]], axis=1).reshape(tokens, width)

    block_queries = ahead(cross_queries)
    placed = behind(span_attention(block_queries, cross_keys, cross_values, head_size))
    second_sum = first_sum + product(placed, matrices[7])
    out_low = out_grad.reshape(tokens, width)
    activated, grad_pre_low, grad_bias_input, ffw_step = feed_forward_grads(
        second_sum, gains[2], out_low, ffw_full, bias_input
    )
    output, grad_second, grad_gain_three, grad_bias_output = feed_forward_sums(
        second_sum, gains[2], out_low, ffw_full, activated, grad_pre_low, bias_output
    )
    blocks_of = lambda array: array.reshape((-1, width) if row_tiles(share) else (-1, share, width))
    ffw_sum = lax.psum_scatter(ffw_step.reshape(2 * FF, width), AXES, scatter_dimension=0, tiled=True)
    grad_second_low = grad_second.astype(BF16)
    grad_placed = times_transposed(grad_second_low, matrices[7]).astype(BF16).reshape(count, rows, width)
    grad_block_queries, near_grad, grad_cross_key_mat, grad_cross_value_mat = span_attention_back(
        block_queries, cross_keys, cross_values, ahead(grad_placed), near, matrices, head_size
    )
    grad_cross_queries = behind(grad_block_queries)
    grad_norm_two = times_transposed(grad_cross_queries, matrices[4])
    grad_gain_two = jnp.sum(grad_norm_two * first_sum * scale_two, axis=0)
    grad_first = grad_second + norm_back(first_sum, scale_two, gains[1], grad_norm_two)
    grad_first_low = grad_first.astype(BF16)
    grad_context = times_transposed(grad_first_low, matrices[3]).astype(BF16).reshape(count, rows, width)
    grad_queries, grad_keys, grad_values, diagonal = self_attention_back(
        place_arg, queries, keys, values, tiles, mask, context_t, lse, grad_context, head_size, reach
    )
    grad_queries = grad_queries.reshape(tokens, width)
    partial_one = (
        times_transposed(grad_keys.reshape(group * tokens, width), matrices[1])
        + times_transposed(grad_values.reshape(group * tokens, width), matrices[2])
    ).astype(BF16)
    joined = sum_of_group(partial_one.reshape(group, tokens, width), place)
    matrix_step = projection_grads(
        normed_every,
        grad_keys.reshape(group * tokens, width),
        grad_values.reshape(group * tokens, width),
        [
            (normed_one, grad_queries),
            (context, grad_first_low),
            (normed_two, grad_cross_queries),
            (placed, grad_second_low),
        ],
        (grad_cross_key_mat, grad_cross_value_mat),
        share,
    )
    lane = jnp.arange(2 * rows, dtype=jnp.int32)
    line = jnp.arange(8, dtype=jnp.int32)
    block = jnp.arange(group, dtype=jnp.int32)
    between = (block[:, None, None] - place) * rows - (lane[None, None, :] - (rows - 8) - line[None, :, None])
    hot = (bucket_of(between)[..., None] == jnp.arange(buckets, dtype=jnp.int32)).astype(F32)
    table_step = jnp.einsum("hjsl,jslb->bh", diagonal, hot, precision=lax.Precision.HIGHEST)

    lines_of = lambda array: array.reshape(-1, 128)
    table_rows = -(-buckets * heads // 128)
    table_line = jnp.pad(table_step.reshape(-1), (0, table_rows * 128 - buckets * heads)).reshape(table_rows, 128)
    attn_sum, line_sum, hidden_grad = last_steps(
        layout, (lax.axis_size("dp"), group), blocks_of(matrix_step), share,
        [lines_of(grad_bias_input), None, lines_of(grad_gain_two), grad_gain_three, grad_bias_output, table_line],
        grad_queries, matrices, joined, hidden.reshape(tokens, width), gains[0], grad_first,
    )
    line_sum = line_sum.reshape(-1)
    own = vectors.shape[0]
    vector_sum = lax.dynamic_slice(line_sum, (lax.axis_index(AXES) * own,), (own,))
    table_sum = line_sum[FF + 4 * width : FF + 4 * width + buckets * heads].reshape(buckets, heads)
    return (
        output.reshape(count, rows, width),
        hidden_grad.reshape(count, rows, width),
        near_grad.reshape(count, spans, span_keys, width),
        attn_sum,
        ffw_sum.astype(F32),
        vector_sum,
        table_sum,
    )


def solution(mesh):
    placed = (
        P("dp", "fsdp", None),
        P("dp", "fsdp", None, None),
        P("dp", None),
        P("dp", "fsdp", None),
        P(("dp", "fsdp"), None),
        P(("dp", "fsdp"), None),
        P(("dp", "fsdp")),
        P(),
    )
    return jax.shard_map(
        per_device,
        mesh=mesh,
        in_specs=placed,
        out_specs=(
            P("dp", "fsdp", None),
            P("dp", "fsdp", None),
            P("dp", "fsdp", None, None),
            P(("dp", "fsdp"), None),
            P(("dp", "fsdp"), None),
            P(("dp", "fsdp")),
            P(),
        ),
        check_vma=False,
    )
```
